32 devices in a mesh: groups: 2 (over x), dp: 8 (over z, y), mp: 2 (over core).
Axes of the slice: x: 2, y: 2, z: 4, core: 2. Of those that a mesh axis runs over, the one named last changes fastest.
Arguments:
- residual: bfloat16 [48, 128, 8192], P(('groups', 'dp'), None, 'mp'), parts along dimension 0
- lengths: int32 [48], P(('groups', 'dp')), parts along dimension 0, may hold values from 32 to 128
- labels: int32 [48], P(('groups', 'dp')), parts along dimension 0, may hold values from 0 to 1, as said below
- earlier_means: float32 [16, 79, 2, 8192], P(('groups', 'dp'), None, None, 'mp'), parts along dimension 0
- chosen: int32 [2], P('groups'), parts along dimension 0, may hold values from 0 to 79
- norm_gain: float32 [8192], P('mp'), may hold values from 0.1 to 1.9
- key_weight: bfloat16 [2, 4096, 1024], P('mp', 'dp'), may hold values from -0.0625 to 0.0625
- value_weight: bfloat16 [2, 4096, 1024], P('mp', 'dp'), may hold values from -0.0625 to 0.0625
- out_proj: bfloat16 [2, 8192, 8192], P('groups', 'mp', 'dp'), parts along dimension 0
Outputs:
- directions: float32 [160, 8192], P('groups', 'mp'), parts along dimension 0
- key_cache: bfloat16 [48, 128, 1024], P(('groups', 'dp'), None, 'mp'), parts along dimension 0
- value_cache: bfloat16 [48, 128, 1024], P(('groups', 'dp'), None, 'mp'), parts along dimension 0
- ortho_proj: bfloat16 [2, 8192, 8192], P('groups', 'mp', 'dp'), parts along dimension 0
The draws below stay inside these ranges and needn't reach their ends.
There are 2 independent parts, one for each index of `groups`. The reference program is written for one: setup_inputs(seed, part) draws one part's arguments, and reference() takes and returns one part's arrays. A program takes and returns all parts, laid end to end along the dimension named above; an argument that names none is the same for every part. Nothing has to cross between parts.
Inputs may be any that keep to these rules, and one draw needn't show every extreme that they name: Every slab of 3 consecutive prompts holds both labels.
All inputs are finite; a program needn't handle non-finite values.
Results may differ from the reference program's by a relative error of at most 0.0051.
Values may be sent and summed in bfloat16 or wider, within the bound.
A program may use at most 384 MiB of HBM per device.

```python
import math
import jax
import jax.numpy as jnp
from jax import lax

D = 8192
KV = 1024
LAYERS = 80
LEN = 128
ORTHO = 1
PROMPTS_DEV = 3
PROMPTS = 24
N_DP = 8
N_MP = 2


def feature_scales(key, salt):
    ratio = 6.0
    place = jnp.arange(D, dtype=jnp.float32) / D
    rough = jnp.exp(jax.random.uniform(jax.random.fold_in(key, salt), (D,), jnp.float32, 0.0, math.log(4.0)))
    return jnp.exp(math.log(ratio) * place) * rough


def shared_parts(key):
    slabs = PROMPTS // PROMPTS_DEV
    col_scale = feature_scales(key, 2)
    direction = jax.random.normal(jax.random.fold_in(key, 1), (D,), jnp.float32) * col_scale * 0.25
    slab_counts = jax.random.randint(jax.random.fold_in(key, 3), (slabs, 1), 1, PROMPTS_DEV)
    scores = jax.random.randint(jax.random.fold_in(key, 4), (slabs, PROMPTS_DEV), 0, 1 << 20) * PROMPTS_DEV
    scores = scores + jnp.arange(PROMPTS_DEV, dtype=jnp.int32)[None, :]
    ranks = jnp.argsort(jnp.argsort(scores, axis=1), axis=1)
    label_bits = (ranks < slab_counts).astype(jnp.int32).reshape(PROMPTS)
    return (direction, label_bits)


def draw_labels(key, part):
    return shared_parts(key)[1]


def draw_lengths(key, part):
    base = jax.random.randint(jax.random.fold_in(key, 15), (PROMPTS,), LEN // 4, LEN + 1)
    longest = jax.random.randint(jax.random.fold_in(key, 16), (), 0, PROMPTS)
    shortest = (longest + 1 + jax.random.randint(jax.random.fold_in(key, 17), (), 0, PROMPTS - 1)) % PROMPTS
    index = jnp.arange(PROMPTS, dtype=jnp.int32)
    base = jnp.where(index == longest, LEN, base)
    base = jnp.where(index == shortest, LEN // 4, base)
    return base.astype(jnp.int32)


def draw_residual(key, part):
    direction, label_bits = shared_parts(key)
    signs = (2 * label_bits - 1).astype(jnp.float32)
    strength = jax.random.uniform(jax.random.fold_in(key, 5), (PROMPTS,), jnp.float32, 0.2, 0.6) * signs
    col_noise = feature_scales(key, 7)
    row_scale = jnp.exp(jax.random.uniform(jax.random.fold_in(key, 8), (PROMPTS, LEN, 1), jnp.float32, 0.0, math.log(10.0)))
    noise = jax.random.normal(jax.random.fold_in(key, 6), (PROMPTS, LEN, D), jnp.float32)
    values = (noise * col_noise * 0.3 + strength[:, None, None] * direction[None, None, :]) * row_scale * 0.5
    return values.astype(jnp.bfloat16)


def draw_earlier_means(key, part):
    direction, label_bits = shared_parts(key)
    slabs = PROMPTS // PROMPTS_DEV
    strength = jnp.exp(jax.random.uniform(jax.random.fold_in(key, 10), (LAYERS - 1,), jnp.float32, math.log(0.3), 0.0))
    signs = jnp.array([-1.0, 1.0], jnp.float32)
    col_noise = feature_scales(key, 9)
    noise = 0.5 * jax.random.normal(jax.random.fold_in(key, 11), (slabs, LAYERS - 1, 2, D), jnp.float32)
    noise = noise * col_noise[None, None, None, :]
    return noise + signs[None, None, :, None] * strength[None, :, None, None] * direction[None, None, None, :]


def draw_out_proj(key, part):
    direction, label_bits = shared_parts(key)
    spread = jax.random.normal(jax.random.fold_in(key, 13), (ORTHO, 1, D), jnp.float32)
    noise = jax.random.normal(jax.random.fold_in(key, 14), (ORTHO, D, D), jnp.float32)
    return (noise + 0.2 * direction[None, :, None] * spread).astype(jnp.bfloat16)


def levels(stream_key, shape, pieces, least, top_value):
    def one(position, blocks):
        draws = jax.random.uniform(jax.random.fold_in(jax.random.fold_in(stream_key, 6), position), (blocks,), jnp.float32, least / len(pieces), top_value / len(pieces))
        return jnp.repeat(jnp.exp(draws), shape[position] // blocks).reshape((-1,) + (1,) * (len(shape) - position - 1))

    level = one(*pieces[0])
    for cut in pieces[1:]:
        level = level * one(*cut)
    return level


def scatter_about(stream_key, shape, width, bound, pieces=(), kind=jnp.bfloat16):
    values = jax.random.normal(stream_key, shape, jnp.float32) * width
    if len(pieces) > 0:
        values = levels(stream_key, shape, pieces, -0.22, 0.18) * values
    return jnp.clip(values, min=-bound, max=bound).astype(kind)


def setup_inputs(seed: int = 0, part: int = 0) -> dict:
    streams_of = jax.random.split(jax.random.key(seed), 10)
    part_keys = jax.random.split(jax.random.fold_in(streams_of[9], part), 10)
    return {
        "residual": draw_residual(jax.random.fold_in(jax.random.fold_in(streams_of[9], part), 71), part),
        "lengths": draw_lengths(jax.random.fold_in(jax.random.fold_in(streams_of[9], part), 71), part),
        "labels": draw_labels(jax.random.fold_in(jax.random.fold_in(streams_of[9], part), 71), part),
        "earlier_means": draw_earlier_means(jax.random.fold_in(jax.random.fold_in(streams_of[9], part), 71), part),
        "chosen": jax.random.randint(part_keys[4], (1,), 0, LAYERS).astype(jnp.int32),
        "norm_gain": jnp.clip(1.0 + 0.18 * jax.random.normal(streams_of[5], (D,), jnp.float32), 0.1, 1.9),
        "key_weight": scatter_about(streams_of[6], (N_MP, D // N_MP, KV), D ** -0.5, 0.0625, ((0, 2), (1, 8))),
        "value_weight": scatter_about(streams_of[7], (N_MP, D // N_MP, KV), D ** -0.5, 0.0625, ((0, 2), (1, 8))),
        "out_proj": draw_out_proj(jax.random.fold_in(jax.random.fold_in(streams_of[9], part), 71), part),
    }


def reference(residual, lengths, labels, earlier_means, chosen, norm_gain, key_weight, value_weight, out_proj):
    highest = lax.Precision.HIGHEST
    positions = jnp.arange(LEN, dtype=jnp.int32)
    valid_mask = (positions[None, :] < lengths[:, None]).astype(jnp.float32)
    masked_sums = jnp.einsum('pt,ptd->pd', valid_mask, residual.astype(jnp.float32), precision=highest)
    prompt_mean = masked_sums / lengths.astype(jnp.float32)[:, None]
    onehot = (labels[:, None] == jnp.arange(2, dtype=jnp.int32)[None, :]).astype(jnp.float32)
    onehot = onehot.reshape(N_DP, PROMPTS_DEV, 2)
    counts = lax.optimization_barrier(jnp.sum(onehot, axis=1))
    slab_sums = jnp.einsum('jpc,jpd->jcd', onehot, prompt_mean.reshape(N_DP, PROMPTS_DEV, D), precision=highest)
    current = slab_sums / counts[:, :, None]
    layer_means = jnp.concatenate([earlier_means, current[:, None]], axis=1)
    weighted = jnp.einsum('jc,jlcd->lcd', counts, layer_means, precision=highest)
    merged = weighted / lax.optimization_barrier(jnp.sum(counts, axis=0))[None, :, None]
    difference = merged[:, 1] - merged[:, 0]
    inverse_rms = lax.rsqrt(lax.optimization_barrier(jnp.mean(difference * difference, axis=1)) + 1e-06)
    directions = difference * inverse_rms[:, None]
    refusal_dir = lax.dynamic_index_in_dim(directions, chosen[0], 0, keepdims=False) / math.sqrt(D)
    token_rows = residual.reshape(PROMPTS * LEN, D).astype(jnp.float32)
    projection = jnp.dot(token_rows, refusal_dir, precision=highest)
    ablated = token_rows - projection[:, None] * refusal_dir[None, :]
    mean_square = lax.optimization_barrier(jnp.mean(ablated * ablated, axis=1))
    normed = (ablated * lax.rsqrt(mean_square + 1e-05)[:, None] * norm_gain[None, :]).astype(jnp.bfloat16)
    key_cache = jnp.dot(normed, key_weight.reshape(D, KV), preferred_element_type=jnp.float32)
    value_cache = jnp.dot(normed, value_weight.reshape(D, KV), preferred_element_type=jnp.float32)
    key_cache = key_cache.astype(jnp.bfloat16).reshape(PROMPTS, LEN, KV)
    value_cache = value_cache.astype(jnp.bfloat16).reshape(PROMPTS, LEN, KV)
    matrices = out_proj.astype(jnp.float32)
    column_proj = jnp.einsum('r,ori->oi', refusal_dir, matrices, precision=highest)
    ortho_proj = (matrices - refusal_dir[None, :, None] * column_proj[:, None, :]).astype(jnp.bfloat16)
    return (directions, key_cache, value_cache, ortho_proj)
```

```python
import functools
import math

import jax
import jax.numpy as jnp
from jax import lax
from jax.experimental import pallas as pl
from jax.experimental.pallas import tpu as pltpu
from jax.sharding import PartitionSpec as P

MESH = pl.DeviceIdType.MESH
F32, BF16 = jnp.float32, jnp.bfloat16
LANES = 128


def fused_kernel(
    cfg,
    lengths_ref, labels_ref, chosen_ref, res_ref, earlier_ref, gain_ref, key_ref, value_ref, proj_ref,
    dirs_ref, kv_ref, refusal_ref, column_ref,
    x_ref, swap_ref, wall_ref, normed_ref, matrix_ref, means_ref, diff_ref,
    half_recv, up_send, up_recv, down_send, down_recv, final_ref,
    count_send, count_recv, pick_send, pick_recv, unit_ref, flat_ref, current_ref,
    dots_send, dots_recv, square_send, square_recv, stat_ref, proj_tok, scale_tok, stat_send, stat_recv,
    col_send, col_recv, layer_send, layer_recv,
    away_send, away_recv, kept_ref, side_send, side_recv,
    x_sem, wall_sem, means_sem, matrix_sem,
    hop_send, hop_recv, cross_send, cross_recv,
    count_sems, pick_sems, swap_sems, half_sems, up_sems, down_sems, final_sems, share_sems,
    pair_sems, stat_sems, away_sems, side_sems,
):
    lines, pieces, prompts, length, layers = cfg
    width = 2 * lines
    tokens, half_width = res_ref.shape
    block = half_width // width
    rows = key_ref.shape[0]
    sub = block // LANES
    tiles = half_width // LANES
    pairs = pieces // 2
    model_width = 2 * half_width
    chunk = diff_ref.shape[0] // width
    group, me, core = lax.axis_index("groups"), lax.axis_index("dp"), lax.axis_index("mp")
    place, side = me // 2, lax.rem(me, 2)
    beside = me + 1 - 2 * side
    first = lax.rem(group, 2)
    across = group + 1 - 2 * first
    sibling = {"mp": 1 - core}

    def remote(src, dst, send, recv, device):
        return pltpu.make_async_remote_copy(
            src_ref=src, dst_ref=dst, send_sem=send, recv_sem=recv, device_id=device,
            device_id_type=MESH,
        )

    own_walls = []
    for m, ref in enumerate((key_ref, value_ref)):
        for i in range(pairs):
            for h in range(2):
                own_walls.append(
                    pltpu.make_async_copy(
                        ref.at[:, pl.ds((h * pairs + i) * LANES, LANES)],
                        wall_ref.at[m, i, h, pl.ds(pl.multiple_of(place * rows, rows), rows), :],
                        wall_sem.at[m, i * 2 + h],
                    )
                )
    for copy in own_walls:
        copy.start()
    own_x = [
        pltpu.make_async_copy(
            res_ref.at[:, pl.ds(j * block, block)], x_ref.at[j], x_sem.at[j]
        )
        for j in range(width)
    ]
    for copy in own_x:
        copy.start()
    own_means = pltpu.make_async_copy(earlier_ref, means_ref, means_sem.at[0])
    own_means.start()
    own_matrix = pltpu.make_async_copy(proj_ref, matrix_ref, matrix_sem.at[0])
    own_matrix.start()

    barrier = pltpu.get_barrier_semaphore()

    @pl.loop(1, width)
    def _(far):
        pl.semaphore_signal(
            barrier, inc=1, device_id={"dp": lax.rem(me + far, width)}, device_id_type=MESH
        )

    pl.semaphore_signal(barrier, inc=1, device_id={"groups": across}, device_id_type=MESH)
    pl.semaphore_signal(barrier, inc=1, device_id=sibling, device_id_type=MESH)

    ones = jnp.int32(0)
    for p in range(prompts):
        ones = ones + labels_ref[p]
    line = lax.broadcasted_iota(jnp.int32, (8, LANES), 0)
    harmful = jnp.full((8, LANES), ones.astype(F32))
    harmless = jnp.full((8, LANES), (prompts - ones).astype(F32))
    count_send[...] = jnp.where(line == 0, harmless, harmful)

    pl.semaphore_wait(barrier, width + 1)

    def spread(send_ref, recv_ref, sems, far):
        return remote(
            send_ref, recv_ref.at[me], sems.at[0, far], sems.at[1, far],
            {"dp": lax.rem(me + far, width)},
        )

    @pl.loop(1, width)
    def _(far):
        spread(count_send, count_recv, count_sems, far).start()

    count_recv[me] = count_send[...]

    for copy in own_walls:
        copy.wait()

    def slot_of(step, way):
        return lax.rem(place - way * step + width * lines, lines)

    def wall_at(slot, pc):
        return wall_ref.at[
            first, pc // 2, lax.rem(pc, 2), pl.ds(pl.multiple_of(slot * rows, rows), rows), :
        ]

    def hop(step, pc, way):
        k = 0 if way > 0 else 1
        ref = wall_at(slot_of(step - 1, way), pc)
        return remote(
            ref, ref, hop_send.at[k, step, pc], hop_recv.at[k, step, pc],
            {"dp": lax.rem(me + 2 * way + width, width)},
        )

    def arrival(step, pc, way):
        k = 0 if way > 0 else 1
        ref = wall_at(slot_of(step, way), pc)
        return remote(
            ref, ref, hop_send.at[k, step, pc], hop_recv.at[k, step, pc],
            {"dp": lax.rem(me - 2 * way + width, width)},
        )

    def cross(step, pc, way):
        k = 0 if way > 0 else 1
        ref = wall_at(slot_of(step, way), pc)
        return remote(
            ref, ref, cross_send.at[k, step, pc], cross_recv.at[k, step, pc], {"groups": across}
        )

    def crossed(step, pc, way):
        k = 0 if way > 0 else 1
        ref = wall_ref.at[
            1 - first, pc // 2, lax.rem(pc, 2),
            pl.ds(pl.multiple_of(slot_of(step, way) * rows, rows), rows), :,
        ]
        return remote(
            ref, ref, cross_send.at[k, step, pc], cross_recv.at[k, step, pc], {"groups": across}
        )

    def sends(step, way):
        return (place >= step - 1) & (place < lines - 1) if way > 0 else (
            (place > 0) & (place <= lines - step)
        )

    def holds(step, way):
        return place >= step if way > 0 else place < lines - step

    def each(count, body):
        @pl.loop(0, count)
        def _(n):
            body(n)

    def start_own(pc):
        for way in (1, -1):

            @pl.when(sends(1, way))
            def _():
                hop(1, pc, way).start()

    each(pieces, start_own)

    def service(step, pc):
        for way in (1, -1):

            @pl.when(holds(step, way))
            def _():
                arrival(step, pc, way).wait_recv()

                @pl.when(sends(step + 1, way) & (step < lines - 1))
                def _():
                    hop(step + 1, pc, way).start()

                cross(step, pc, way).start()

    for copy in own_x:
        copy.wait()

    def swap(zz):
        return remote(
            x_ref.at[2 * zz + 1 - side], swap_ref.at[zz], swap_sems.at[0, zz], swap_sems.at[1, zz],
            {"dp": beside},
        )

    early = lines // 2
    each(early, lambda zz: swap(zz).start())

    row_id = lax.broadcasted_iota(jnp.int32, (16, tokens), 0)
    token_id = lax.broadcasted_iota(jnp.int32, (16, tokens), 1)
    mask = jnp.zeros((16, tokens), F32)
    for p in range(prompts):
        inside = (token_id >= p * length) & (token_id < p * length + lengths_ref[p])
        mask = jnp.where(inside & (row_id == p), 1.0, mask)
    mask = mask.astype(BF16)

    def class_sums(j):
        sums = jnp.dot(mask, x_ref[j], preferred_element_type=F32)
        current = [jnp.zeros((1, block), F32), jnp.zeros((1, block), F32)]
        for p in range(prompts):
            mean = sums[p : p + 1, :] / jnp.full((1, block), lengths_ref[p].astype(F32))
            label = labels_ref[p].astype(F32)
            current[1] = current[1] + mean * label
            current[0] = current[0] + mean * (1.0 - label)
        current[0] = current[0] / jnp.full((1, block), (prompts - ones).astype(F32))
        current[1] = current[1] / jnp.full((1, block), ones.astype(F32))
        for c in range(2):
            for q in range(sub):
                current_ref[c, pl.ds(j * sub + q, 1), :] = current[c][:, q * LANES : (q + 1) * LANES]

    each(width, class_sums)

    @pl.loop(1, width)
    def _(far):
        spread(count_send, count_recv, count_sems, far).wait_recv()

    totals = count_recv[0]
    for j in range(1, width):
        totals = totals + count_recv[j]
    share = count_send[...] / totals
    share0, share1 = share[0:1, :], share[1:2, :]

    own_means.wait()
    current_diff = share1 * current_ref[1] - share0 * current_ref[0]
    at = jnp.minimum(chosen_ref[0], layers - 2) * (2 * tiles)
    picked = share1 * means_ref[pl.ds(at + 1, tiles, stride=2), :] - share0 * means_ref[
        pl.ds(at, tiles, stride=2), :
    ]
    pick_send[...] = jnp.where(chosen_ref[0] == layers - 1, current_diff, picked)

    @pl.loop(1, width)
    def _(far):
        spread(pick_send, pick_recv, pick_sems, far).start()

    pick_recv[me] = pick_send[...]

    @pl.loop(0, layers - 1)
    def _(l):
        e = l * (2 * tiles)
        d = share1 * means_ref[pl.ds(e + 1, tiles, stride=2), :] - share0 * means_ref[
            pl.ds(e, tiles, stride=2), :
        ]
        diff_ref[pl.ds((l // 8) * (8 * tiles) + lax.rem(l, 8), tiles, stride=8), :] = d

    diff_ref[pl.ds(((layers - 1) // 8) * (8 * tiles) + (layers - 1) % 8, tiles, stride=8), :] = (
        current_diff
    )

    def part(ref, j):
        return ref.at[pl.ds(pl.multiple_of(j * chunk, 16), chunk), :]

    def read(ref, j):
        return ref[pl.ds(pl.multiple_of(j * chunk, 16), chunk), :]

    def half(zz):
        return remote(
            part(diff_ref, 2 * zz + 1 - side), half_recv.at[zz], half_sems.at[0, zz],
            half_sems.at[1, zz], {"dp": beside},
        )

    each(lines, lambda zz: half(zz).start())
    each(lines - early, lambda zz: swap(zz + early).start())

    @pl.loop(1, width)
    def _(far):
        spread(pick_send, pick_recv, pick_sems, far).wait_recv()

    picked = pick_recv[0]
    for j in range(1, width):
        picked = picked + pick_recv[j]
    local_square = jnp.sum(jnp.sum(picked * picked, axis=1, keepdims=True), axis=0, keepdims=True)
    unit = picked * lax.rsqrt(local_square / half_width + 1e-06)
    flat_ref[...] = picked
    high = unit.astype(BF16).astype(F32)
    middle = (unit - high).astype(BF16).astype(F32)
    low = unit - high - middle
    line16 = lax.broadcasted_iota(jnp.int32, (16, LANES), 0)
    for k in range(tiles):
        spot = jnp.where(
            line16 == 0, high[k : k + 1, :],
            jnp.where(line16 == 1, middle[k : k + 1, :], jnp.where(line16 == 2, low[k : k + 1, :], 0.0)),
        )
        unit_ref[k // sub, :, (k % sub) * LANES : (k % sub + 1) * LANES] = spot.astype(BF16)

    stat_ref[...] = jnp.zeros_like(stat_ref)

    def token_dots(j):
        stat_ref[...] += lax.dot_general(
            x_ref[j], unit_ref[j], (((1,), (1,)), ((), ())), preferred_element_type=F32
        )

    each(width, token_dots)
    dots = jnp.sum(stat_ref[...], axis=1, keepdims=True)
    dots_send[pl.ds(0, tokens), :] = jnp.broadcast_to(dots, (tokens, LANES))
    dots_send[pl.ds(tokens, 8), :] = jnp.broadcast_to(local_square, (8, LANES))
    dots_copy = remote(dots_send, dots_recv, pair_sems.at[0, 0], pair_sems.at[1, 0], sibling)
    dots_copy.start()

    each(pieces // 2, lambda pc: service(1, pc))

    own_matrix.wait()
    col_send[...] = jnp.zeros_like(col_send)

    def column_dots(j):
        col_send[...] += jnp.dot(
            unit_ref[j], matrix_ref[pl.ds(pl.multiple_of(j * block, block), block), :],
            preferred_element_type=F32,
        )

    each(width, column_dots)
    col_copy = remote(col_send, col_recv, pair_sems.at[0, 1], pair_sems.at[1, 1], sibling)
    col_copy.start()

    each(pieces - pieces // 2, lambda pc: service(1, pc + pieces // 2))

    dots_copy.wait_recv()
    root = math.sqrt(model_width)
    other_square = dots_recv[pl.ds(tokens, 1), 0:1]
    mean_dir = (local_square + other_square) / model_width + 1e-06
    ratio_mine = jnp.sqrt((local_square / half_width + 1e-06) / mean_dir) / root
    ratio_other = jnp.sqrt((other_square / half_width + 1e-06) / mean_dir) / root
    flat = flat_ref[...] * (lax.rsqrt(mean_dir) / root)
    refusal_ref[...] = flat
    proj_tok[...] = dots_send[pl.ds(0, tokens), :] * ratio_mine + dots_recv[pl.ds(0, tokens), :] * (
        ratio_other
    )

    def square_rows(n):
        here = pl.ds(pl.multiple_of(n * 16, 16), 16)
        amount = proj_tok[here, :]
        total = jnp.zeros((16, LANES), F32)
        for j in range(width):
            for q in range(sub):
                k = j * sub + q
                left = x_ref[j, here, q * LANES : (q + 1) * LANES].astype(F32)
                left = left - amount * refusal_ref[k : k + 1, :]
                total = total + left * left
        square_send[here, :] = total

    each(tokens // 16, square_rows)
    square_copy = remote(square_send, square_recv, pair_sems.at[0, 2], pair_sems.at[1, 2], sibling)
    square_copy.start()

    col_copy.wait_recv()
    column_ref[...] = col_send[0:8, :] * ratio_mine + col_recv[0:8, :] * ratio_other

    each(lines, lambda zz: half(zz).wait_recv())

    square_copy.wait_recv()
    mean_square = jnp.sum(square_send[...] + square_recv[...], axis=1, keepdims=True) / model_width
    scale_tok[...] = jnp.broadcast_to(lax.rsqrt(mean_square + 1e-05), (tokens, LANES))

    eye = lax.broadcasted_iota(jnp.int32, (LANES, LANES), 0) == lax.broadcasted_iota(
        jnp.int32, (LANES, LANES), 1
    )
    bands = tokens // LANES
    for b in range(bands):
        here = pl.ds(b * LANES, LANES)
        for s, ref in enumerate((proj_tok, scale_tok)):
            stat_send[pl.ds(s * bands + b, 1), :] = jnp.sum(
                jnp.where(eye, ref[here, :], 0.0), axis=0, keepdims=True
            )
    stat_copy = remote(stat_send, stat_recv, stat_sems.at[0], stat_sems.at[1], {"dp": beside})
    stat_copy.start()

    def up(zz):
        return remote(
            up_send.at[zz], up_recv.at[zz], up_sems.at[0, zz], up_sems.at[1, zz],
            {"dp": lax.rem(me + 2, width)},
        )

    def down(zz):
        return remote(
            down_send.at[zz], down_recv.at[zz], down_sems.at[0, zz], down_sems.at[1, zz],
            {"dp": lax.rem(me - 2 + width, width)},
        )

    def chain_up(n):
        zz = lines - 1 - n

        @pl.when(zz > place)
        def _():
            up_send[zz] = read(diff_ref, 2 * zz + side) + half_recv[zz]

            @pl.when(place > 0)
            def _():
                up(zz).wait_recv()
                up_send[zz] += up_recv[zz]

            up(zz).start()

    def chain_down(zz):
        @pl.when(zz < place)
        def _():
            down_send[zz] = read(diff_ref, 2 * zz + side) + half_recv[zz]

            @pl.when(place < lines - 1)
            def _():
                down(zz).wait_recv()
                down_send[zz] += down_recv[zz]

            down(zz).start()

    @pl.when(place == 0)
    def _():
        each(lines, chain_up)

    @pl.when(place == lines - 1)
    def _():
        each(lines, chain_down)

    if lines > 2:
        each(pieces // 2, lambda pc: service(2, pc))

    def normed_rows(base, n, load, proj_at, scale_at):
        here = pl.ds(pl.multiple_of(n * 16, 16), 16)
        amount, scale = proj_at[here, :], scale_at[here, :]
        out = pl.ds(pl.multiple_of(base + n * 16, 16), 16)
        for zz in range(lines):
            j = 2 * zz + side
            vectors = refusal_ref[pl.ds(j * sub, sub), :]
            gains = gain_ref[pl.ds(j * sub, sub), :]
            for q in range(sub):
                value = load(zz, here, pl.ds(q * LANES, LANES)).astype(F32)
                value = (value - amount * vectors[q : q + 1, :]) * scale * gains[q : q + 1, :]
                normed_ref[out, pl.ds(zz * block + q * LANES, LANES)] = value.astype(BF16)

    each(
        tokens // 16,
        lambda n: normed_rows(0, n, lambda zz, a, b: x_ref[2 * zz + side, a, b], proj_tok, scale_tok),
    )

    @pl.when((place > 0) & (place < lines - 1))
    def _():
        each(lines, chain_up)
        each(lines, chain_down)

    if lines > 2:
        each(pieces - pieces // 2, lambda pc: service(2, pc + pieces // 2))

        @pl.loop(3, lines - 1)
        def _(step):
            each(pieces, lambda pc: service(step, pc))

    def gathered(far):
        ref = part(final_ref, me)
        return remote(
            ref, ref, final_sems.at[0, far], final_sems.at[1, far],
            {"dp": 2 * lax.rem(place + far, lines) + side},
        )

    def gathered_from(far):
        ref = part(final_ref, 2 * lax.rem(place - far + lines, lines) + side)
        return remote(ref, ref, final_sems.at[0, far], final_sems.at[1, far], {"dp": beside})

    def shared(zz):
        ref = part(final_ref, 2 * zz + side)
        return remote(ref, ref, share_sems.at[0, zz], share_sems.at[1, zz], {"dp": beside})

    def shared_from(zz):
        ref = part(final_ref, 2 * zz + 1 - side)
        return remote(ref, ref, share_sems.at[0, zz], share_sems.at[1, zz], {"dp": beside})

    down_send[place] = read(diff_ref, me) + half_recv[place]

    @pl.when(place > 0)
    def _():
        up(place).wait_recv()
        down_send[place] += up_recv[place]

    @pl.when(place < lines - 1)
    def _():
        down(place).wait_recv()
        down_send[place] += down_recv[place]

    final_ref[pl.ds(pl.multiple_of(me * chunk, 16), chunk), :] = down_send[place].astype(BF16)

    @pl.loop(1, lines)
    def _(far):
        gathered(far).start()

    shared(place).start()

    stat_copy.wait_recv()
    for b in range(bands):
        here = pl.ds(b * LANES, LANES)
        for s, ref in enumerate((proj_tok, scale_tok)):
            value = jnp.where(eye, stat_recv[pl.ds(s * bands + b, 1), :], 0.0)
            ref[here, :] = jnp.broadcast_to(jnp.sum(value, axis=1, keepdims=True), (LANES, LANES))
    each(lines, lambda zz: swap(zz).wait_recv())
    each(
        tokens // 16,
        lambda n: normed_rows(tokens, n, lambda zz, a, b: swap_ref[zz, a, b], proj_tok, scale_tok),
    )

    def away(u):
        return remote(
            away_send.at[u], away_recv.at[u], away_sems.at[0, u], away_sems.at[1, u], sibling
        )

    def beyond(u):
        return remote(
            side_send.at[u], side_recv.at[u], side_sems.at[0, u], side_sems.at[1, u], {"dp": beside}
        )

    units = 2 * pairs

    def product(u):
        i, odd = u // 2, lax.rem(u, 2)
        which = lax.rem(first + odd, 2)

        @pl.when(odd == 0)
        def _():
            if lines > 1:
                each(2, lambda h: service(lines - 1, 2 * i + h))

        @pl.when(odd == 1)
        def _():
            for way in (1, -1):

                @pl.loop(1, lines)
                def _(step):
                    @pl.when(holds(step, way))
                    def _():
                        each(2, lambda h: crossed(step, 2 * i + h, way).wait_recv())

        away_send[u] = jnp.dot(
            normed_ref[...], wall_ref[which, i, 1 - core], preferred_element_type=F32
        )
        away(u).start()
        kept_ref[u] = jnp.dot(normed_ref[...], wall_ref[which, i, core], preferred_element_type=F32)

    def reduce_pair(u):
        away(u).wait_recv()
        side_send[u] = (
            kept_ref[u, pl.ds(tokens, tokens), :] + away_recv[u, pl.ds(tokens, tokens), :]
        ).astype(BF16)
        beyond(u).start()

    def reduce_side(u):
        i, odd = u // 2, lax.rem(u, 2)
        which = lax.rem(first + odd, 2)
        beyond(u).wait_recv()
        total = kept_ref[u, pl.ds(0, tokens), :] + away_recv[u, pl.ds(0, tokens), :]
        total = total + side_recv[u].astype(F32)
        kv_ref[which, :, pl.ds(pl.multiple_of(i * LANES, LANES), LANES)] = total.astype(BF16)

    @pl.loop(0, units)
    def _(u):
        product(u)

        @pl.when(u >= 1)
        def _():
            reduce_pair(u - 1)

        @pl.when(u >= 2)
        def _():
            reduce_side(u - 2)

        @pl.when(u == 2)
        def _():
            @pl.loop(1, lines)
            def _(far):
                gathered_from(far).wait_recv()
                shared(lax.rem(place - far + lines, lines)).start()

        @pl.when(u == units - 2)
        def _():
            each(lines, lambda zz: shared_from(zz).wait_recv())

            @pl.loop(0, layers // 8)
            def _(t):
                total = jnp.zeros((8, LANES), F32)
                for k in range(0, tiles, 2):
                    rows16 = pl.ds(pl.multiple_of(t * (8 * tiles) + k * 8, 16), 16)
                    value = final_ref[rows16, :].astype(F32)
                    total = total + value[0:8] * value[0:8] + value[8:16] * value[8:16]
                layer_send[pl.ds(pl.multiple_of(t * 8, 8), 8), :] = total

            remote(
                layer_send, layer_recv, pair_sems.at[0, 3], pair_sems.at[1, 3], sibling
            ).start()

    reduce_pair(units - 1)
    layer_copy = remote(layer_send, layer_recv, pair_sems.at[0, 3], pair_sems.at[1, 3], sibling)
    layer_copy.wait_recv()

    @pl.loop(0, layers // 8)
    def _(t):
        here = pl.ds(pl.multiple_of(t * 8, 8), 8)
        mean = jnp.sum(layer_send[here, :] + layer_recv[here, :], axis=1, keepdims=True) / model_width
        norm = jnp.broadcast_to(lax.rsqrt(mean + 1e-06), (8, LANES))
        norm = jnp.concatenate([norm, norm], axis=0)
        for k in range(0, tiles, 2):
            rows16 = pl.ds(pl.multiple_of(t * (8 * tiles) + k * 8, 16), 16)
            dirs_ref[rows16, :] = final_ref[rows16, :].astype(F32) * norm

    reduce_side(units - 2)
    reduce_side(units - 1)

    @pl.loop(1, width)
    def _(far):
        spread(count_send, count_recv, count_sems, far).wait_send()
        spread(pick_send, pick_recv, pick_sems, far).wait_send()

    @pl.loop(1, lines)
    def _(far):
        gathered(far).wait_send()

    def drain(zz):
        swap(zz).wait_send()
        half(zz).wait_send()
        shared(zz).wait_send()

        @pl.when(zz > place)
        def _():
            up(zz).wait_send()

        @pl.when(zz < place)
        def _():
            down(zz).wait_send()

    each(lines, drain)
    dots_copy.wait_send()
    col_copy.wait_send()
    square_copy.wait_send()
    layer_copy.wait_send()
    stat_copy.wait_send()

    def drain_unit(u):
        away(u).wait_send()
        beyond(u).wait_send()

    each(units, drain_unit)

    @pl.loop(1, lines)
    def _(step):
        def drain_piece(pc):
            for way in (1, -1):

                @pl.when(sends(step, way))
                def _():
                    hop(step, pc, way).wait_send()

                @pl.when(holds(step, way))
                def _():
                    cross(step, pc, way).wait_send()

        each(pieces, drain_piece)


def fused(lines, prompts, length, lengths, labels, chosen, rows, earlier, gain, key, value, matrix):
    tokens, half_width = rows.shape
    width = 2 * lines
    block = half_width // width
    tiles = half_width // LANES
    layers = earlier.shape[0] // (2 * tiles) + 1
    columns = key.shape[1]
    pieces = columns // LANES
    pairs = pieces // 2
    units = 2 * pairs
    flat_rows = layers * tiles
    chunk = flat_rows // width
    smem = pl.BlockSpec(memory_space=pltpu.SMEM)
    vmem = pl.BlockSpec(memory_space=pltpu.VMEM)
    hbm = pl.BlockSpec(memory_space=pl.ANY)
    dma = pltpu.SemaphoreType.DMA
    return pl.pallas_call(
        functools.partial(fused_kernel, (lines, pieces, prompts, length, layers)),
        out_shape=(
            jax.ShapeDtypeStruct((flat_rows, LANES), F32),
            jax.ShapeDtypeStruct((2, tokens, columns // 2), BF16),
            jax.ShapeDtypeStruct((tiles, LANES), F32),
            jax.ShapeDtypeStruct((8, matrix.shape[1]), F32),
        ),
        in_specs=[smem, smem, smem, hbm, hbm, vmem, hbm, hbm, hbm],
        out_specs=[vmem] * 4,
        scratch_shapes=[
            pltpu.VMEM((width, tokens, block), BF16),
            pltpu.VMEM((lines, tokens, block), BF16),
            pltpu.VMEM((2, pairs, 2, lines * key.shape[0], LANES), BF16),
            pltpu.VMEM((2 * tokens, half_width // 2), BF16),
            pltpu.VMEM(matrix.shape, BF16),
            pltpu.VMEM(earlier.shape, F32),
            pltpu.VMEM((flat_rows, LANES), F32),
        ]
        + [pltpu.VMEM((lines, chunk, LANES), F32)] * 5
        + [
            pltpu.VMEM((flat_rows, LANES), BF16),
            pltpu.VMEM((8, LANES), F32),
            pltpu.VMEM((width, 8, LANES), F32),
            pltpu.VMEM((tiles, LANES), F32),
            pltpu.VMEM((width, tiles, LANES), F32),
            pltpu.VMEM((width, 16, block), BF16),
            pltpu.VMEM((tiles, LANES), F32),
            pltpu.VMEM((2, tiles, LANES), F32),
            pltpu.VMEM((tokens + 8, LANES), F32),
            pltpu.VMEM((tokens + 8, LANES), F32),
            pltpu.VMEM((tokens, LANES), F32),
            pltpu.VMEM((tokens, LANES), F32),
            pltpu.VMEM((tokens, 16), F32),
            pltpu.VMEM((tokens, LANES), F32),
            pltpu.VMEM((tokens, LANES), F32),
            pltpu.VMEM((8, LANES), F32),
            pltpu.VMEM((8, LANES), F32),
            pltpu.VMEM((16, matrix.shape[1]), F32),
            pltpu.VMEM((16, matrix.shape[1]), F32),
            pltpu.VMEM((layers, LANES), F32),
            pltpu.VMEM((layers, LANES), F32),
            pltpu.VMEM((units, 2 * tokens, LANES), F32),
            pltpu.VMEM((units, 2 * tokens, LANES), F32),
            pltpu.VMEM((units, 2 * tokens, LANES), F32),
            pltpu.VMEM((units, tokens, LANES), BF16),
            pltpu.VMEM((units, tokens, LANES), BF16),
            dma((width,)),
            dma((2, pieces)),
            dma((1,)),
            dma((1,)),
        ]
        + [dma((2, lines, pieces))] * 4
        + [
            dma((2, width)),
            dma((2, width)),
            dma((2, lines)),
            dma((2, lines)),
            dma((2, lines)),
            dma((2, lines)),
            dma((2, lines)),
            dma((2, lines)),
            dma((2, 4)),
            dma((2,)),
            dma((2, units)),
            dma((2, units)),
        ],
        compiler_params=pltpu.CompilerParams(
            collective_id=0, has_side_effects=True, vmem_limit_bytes=60 << 20
        ),
        name="fused",
    )(lengths, labels, chosen, rows, earlier, gain, key, value, matrix)


def shards(
    residual, lengths, labels, earlier_means, chosen, norm_gain, key_weight, value_weight, out_proj
):
    prompts, length, half_width = residual.shape
    lines = lax.axis_size("dp") // 2
    tiles = half_width // LANES
    earlier = earlier_means[0]
    layers = earlier.shape[0] + 1
    earlier = earlier.reshape(layers - 1, 2, tiles, LANES).transpose(0, 2, 1, 3).reshape(-1, LANES)
    matrix = out_proj[0]
    flat, caches, refusal, column = fused(
        lines, prompts, length, lengths, labels, chosen, residual.reshape(-1, half_width), earlier,
        norm_gain.reshape(tiles, LANES), key_weight[0], value_weight[0], matrix,
    )
    directions = (
        flat.reshape(layers // 8, tiles, 8, LANES).transpose(0, 2, 1, 3).reshape(layers, half_width)
    )
    refusal_dir = refusal.reshape(half_width)
    column_proj = jnp.sum(column[:3], axis=0)
    ortho_proj = (matrix.astype(F32) - refusal_dir[:, None] * column_proj[None, :]).astype(BF16)[None]
    caches = caches.reshape(2, prompts, length, -1)
    return (directions, caches[0], caches[1], ortho_proj)


def solution(mesh):
    return jax.shard_map(
        shards,
        mesh=mesh,
        in_specs=(
            P(("groups", "dp"), None, "mp"),
            P(("groups", "dp")),
            P(("groups", "dp")),
            P(("groups", "dp"), None, None, "mp"),
            P("groups"),
            P("mp"),
            P("mp", "dp", None),
            P("mp", "dp", None),
            P("groups", "mp", "dp"),
        ),
        out_specs=(
            P("groups", "mp"),
            P(("groups", "dp"), None, "mp"),
            P(("groups", "dp"), None, "mp"),
            P("groups", "mp", "dp"),
        ),
        check_vma=False,
    )
```

```python
import functools
import math

import jax
import jax.numpy as jnp
from jax import lax
from jax.experimental import pallas as pl
from jax.experimental.pallas import tpu as pltpu
from jax.sharding import PartitionSpec as P

MESH = pl.DeviceIdType.MESH
F32, BF16 = jnp.float32, jnp.bfloat16
LANES = 128


def fused_kernel(
    cfg,
    lengths_ref, labels_ref, chosen_ref, res_ref, earlier_ref, gain_ref, key_ref, value_ref, proj_ref,
    dirs_ref, kv_ref, refusal_ref, column_ref,
    x_ref, swap_ref, wall_ref, normed_ref, matrix_ref, means_ref, diff_ref,
    half_recv, up_send, up_recv, down_send, down_recv, final_ref,
    count_send, count_recv, pick_send, pick_recv, unit_ref, flat_ref, current_ref,
    dots_send, dots_recv, square_send, square_recv, stat_ref, proj_tok, scale_tok, stat_send, stat_recv,
    col_send, col_recv, layer_send, layer_recv,
    away_send, away_recv, kept_ref, side_send, side_recv,
    x_sem, wall_sem, means_sem, matrix_sem,
    hop_send, hop_recv, cross_send, cross_recv,
    count_sems, pick_sems, swap_sems, half_sems, up_sems, down_sems, final_sems, share_sems,
    pair_sems, stat_sems, away_sems, side_sems,
):
    lines, pieces, prompts, length, layers = cfg
    width = 2 * lines
    tokens, half_width = res_ref.shape
    block = half_width // width
    rows = key_ref.shape[0]
    sub = block // LANES
    tiles = half_width // LANES
    pairs = pieces // 2
    model_width = 2 * half_width
    chunk = diff_ref.shape[0] // width
    group, me, core = lax.axis_index("groups"), lax.axis_index("dp"), lax.axis_index("mp")
    place, side = me // 2, lax.rem(me, 2)
    beside = me + 1 - 2 * side
    first = lax.rem(group, 2)
    across = group + 1 - 2 * first
    sibling = {"mp": 1 - core}

    def remote(src, dst, send, recv, device):
        return pltpu.make_async_remote_copy(
            src_ref=src, dst_ref=dst, send_sem=send, recv_sem=recv, device_id=device,
            device_id_type=MESH,
        )

    barrier = pltpu.get_barrier_semaphore()

    @pl.loop(1, width)
    def _(far):
        pl.semaphore_signal(
            barrier, inc=1, device_id={"dp": lax.rem(me + far, width)}, device_id_type=MESH
        )

    pl.semaphore_signal(barrier, inc=1, device_id={"groups": across}, device_id_type=MESH)
    pl.semaphore_signal(barrier, inc=1, device_id=sibling, device_id_type=MESH)

    def each(count, body):
        @pl.loop(0, count)
        def _(n):
            body(n)

    def own_x(j):
        return pltpu.make_async_copy(
            res_ref.at[:, pl.ds(pl.multiple_of(j * block, block), block)], x_ref.at[j], x_sem.at[j]
        )

    each(width, lambda j: own_x(j).start())
    own_means = pltpu.make_async_copy(earlier_ref, means_ref, means_sem.at[0])
    own_means.start()

    ones = jnp.int32(0)
    for p in range(prompts):
        ones = ones + labels_ref[p]
    line = lax.broadcasted_iota(jnp.int32, (8, LANES), 0)
    harmful = jnp.full((8, LANES), ones.astype(F32))
    harmless = jnp.full((8, LANES), (prompts - ones).astype(F32))
    count_send[...] = jnp.where(line == 0, harmless, harmful)

    pl.semaphore_wait(barrier, width + 1)

    def slot_of(step, way):
        return lax.rem(place - way * step + width * lines, lines)

    def wall_at(slot, pc):
        return wall_ref.at[
            first, pc // 2, lax.rem(pc, 2), pl.ds(pl.multiple_of(slot * rows, rows), rows), :
        ]

    def hop(step, pc, way, source=None):
        k = 0 if way > 0 else 1
        ref = wall_at(slot_of(step - 1, way), pc)
        return remote(
            ref if source is None else source, ref, hop_send.at[k, step, pc], hop_recv.at[k, step, pc],
            {"dp": lax.rem(me + 2 * way + width, width)},
        )

    def arrival(step, pc, way):
        k = 0 if way > 0 else 1
        ref = wall_at(slot_of(step, way), pc)
        return remote(
            ref, ref, hop_send.at[k, step, pc], hop_recv.at[k, step, pc],
            {"dp": lax.rem(me - 2 * way + width, width)},
        )

    def cross(step, pc, way):
        k = 0 if way > 0 else 1
        ref = wall_at(slot_of(step, way), pc)
        return remote(
            ref, ref, cross_send.at[k, step, pc], cross_recv.at[k, step, pc], {"groups": across}
        )

    def crossed(step, pc, way):
        k = 0 if way > 0 else 1
        ref = wall_ref.at[
            1 - first, pc // 2, lax.rem(pc, 2),
            pl.ds(pl.multiple_of(slot_of(step, way) * rows, rows), rows), :,
        ]
        return remote(
            ref, ref, cross_send.at[k, step, pc], cross_recv.at[k, step, pc], {"groups": across}
        )

    def sends(step, way):
        return (place >= step - 1) & (place < lines - 1) if way > 0 else (
            (place > 0) & (place <= lines - step)
        )

    def holds(step, way):
        return place >= step if way > 0 else place < lines - step

    def piece_of(ref, pc):
        column = (lax.rem(pc, 2) * pairs + pc // 2) * LANES
        return ref.at[:, pl.ds(pl.multiple_of(column, LANES), LANES)]

    def start_own(pc):
        for way in (1, -1):
            for m, ref in enumerate((key_ref, value_ref)):

                @pl.when(sends(1, way) & (first == m))
                def _():
                    hop(1, pc, way, piece_of(ref, pc)).start()

    window = 2
    ticks = pieces + lines - 2
    each(window, start_own)

    def service(step, pc):
        for way in (1, -1):

            @pl.when(holds(step, way))
            def _():
                arrival(step, pc, way).wait_recv()

                @pl.when(sends(step + 1, way) & (step < lines - 1))
                def _():
                    hop(step + 1, pc, way).start()

                cross(step, pc, way).start()

    def tick(t):
        @pl.when(t + window < pieces)
        def _():
            start_own(t + window)

        @pl.loop(jnp.maximum(1, t - pieces + 2), jnp.minimum(lines, t + 2))
        def _(step):
            service(step, t - step + 1)

    def swap(zz):
        j = 2 * zz + 1 - side
        return remote(
            res_ref.at[:, pl.ds(pl.multiple_of(j * block, block), block)], swap_ref.at[zz],
            swap_sems.at[0, zz], swap_sems.at[1, zz], {"dp": beside},
        )

    early = max(lines // 4, 1)
    each(early, lambda zz: swap(zz).start())

    def spread(send_ref, recv_ref, sems, far):
        return remote(
            send_ref, recv_ref.at[me], sems.at[0, far], sems.at[1, far],
            {"dp": lax.rem(me + far, width)},
        )

    @pl.loop(1, width)
    def _(far):
        spread(count_send, count_recv, count_sems, far).start()

    count_recv[me] = count_send[...]

    def own_wall(m, pc):
        ref = (key_ref, value_ref)[m]
        return pltpu.make_async_copy(
            piece_of(ref, pc),
            wall_ref.at[
                m, pc // 2, lax.rem(pc, 2), pl.ds(pl.multiple_of(place * rows, rows), rows), :
            ],
            wall_sem.at[m, pc],
        )

    each(width, lambda j: own_x(j).wait())
    own_matrix = pltpu.make_async_copy(proj_ref, matrix_ref, matrix_sem.at[0])
    own_matrix.start()
    for m in range(2):
        each(pieces, lambda pc: own_wall(m, pc).start())

    tick(0)

    row_id = lax.broadcasted_iota(jnp.int32, (16, tokens), 0)
    token_id = lax.broadcasted_iota(jnp.int32, (16, tokens), 1)
    mask = jnp.zeros((16, tokens), F32)
    for p in range(prompts):
        inside = (token_id >= p * length) & (token_id < p * length + lengths_ref[p])
        mask = jnp.where(inside & (row_id == p), 1.0, mask)
    mask = mask.astype(BF16)

    def class_sums(j):
        sums = jnp.dot(mask, x_ref[j], preferred_element_type=F32)
        current = [jnp.zeros((1, block), F32), jnp.zeros((1, block), F32)]
        for p in range(prompts):
            mean = sums[p : p + 1, :] / jnp.full((1, block), lengths_ref[p].astype(F32))
            label = labels_ref[p].astype(F32)
            current[1] = current[1] + mean * label
            current[0] = current[0] + mean * (1.0 - label)
        current[0] = current[0] / jnp.full((1, block), (prompts - ones).astype(F32))
        current[1] = current[1] / jnp.full((1, block), ones.astype(F32))
        for c in range(2):
            for q in range(sub):
                current_ref[c, pl.ds(j * sub + q, 1), :] = current[c][:, q * LANES : (q + 1) * LANES]

    each(width, class_sums)

    @pl.loop(1, width)
    def _(far):
        spread(count_send, count_recv, count_sems, far).wait_recv()

    totals = count_recv[0]
    for j in range(1, width):
        totals = totals + count_recv[j]
    share = count_send[...] / totals
    share0, share1 = share[0:1, :], share[1:2, :]

    own_means.wait()
    current_diff = share1 * current_ref[1] - share0 * current_ref[0]
    at = jnp.minimum(chosen_ref[0], layers - 2) * (2 * tiles)
    picked = share1 * means_ref[pl.ds(at + 1, tiles, stride=2), :] - share0 * means_ref[
        pl.ds(at, tiles, stride=2), :
    ]
    pick_send[...] = jnp.where(chosen_ref[0] == layers - 1, current_diff, picked)

    @pl.loop(1, width)
    def _(far):
        spread(pick_send, pick_recv, pick_sems, far).start()

    pick_recv[me] = pick_send[...]

    @pl.loop(0, layers - 1)
    def _(l):
        e = l * (2 * tiles)
        d = share1 * means_ref[pl.ds(e + 1, tiles, stride=2), :] - share0 * means_ref[
            pl.ds(e, tiles, stride=2), :
        ]
        diff_ref[pl.ds((l // 8) * (8 * tiles) + lax.rem(l, 8), tiles, stride=8), :] = d

    diff_ref[pl.ds(((layers - 1) // 8) * (8 * tiles) + (layers - 1) % 8, tiles, stride=8), :] = (
        current_diff
    )

    def part(ref, j):
        return ref.at[pl.ds(pl.multiple_of(j * chunk, 16), chunk), :]

    def read(ref, j):
        return ref[pl.ds(pl.multiple_of(j * chunk, 16), chunk), :]

    def half(zz):
        return remote(
            part(diff_ref, 2 * zz + 1 - side), half_recv.at[zz], half_sems.at[0, zz],
            half_sems.at[1, zz], {"dp": beside},
        )

    each(lines, lambda zz: half(zz).start())
    each(lines - early, lambda zz: swap(zz + early).start())

    tick(1)
    tick(2)


    @pl.loop(1, width)
    def _(far):
        spread(pick_send, pick_recv, pick_sems, far).wait_recv()

    picked = pick_recv[0]
    for j in range(1, width):
        picked = picked + pick_recv[j]
    local_square = jnp.sum(jnp.sum(picked * picked, axis=1, keepdims=True), axis=0, keepdims=True)
    unit = picked * lax.rsqrt(local_square / half_width + 1e-06)
    flat_ref[...] = picked
    high = unit.astype(BF16).astype(F32)
    middle = (unit - high).astype(BF16).astype(F32)
    low = unit - high - middle
    line16 = lax.broadcasted_iota(jnp.int32, (16, LANES), 0)
    for k in range(tiles):
        spot = jnp.where(
            line16 == 0, high[k : k + 1, :],
            jnp.where(line16 == 1, middle[k : k + 1, :], jnp.where(line16 == 2, low[k : k + 1, :], 0.0)),
        )
        unit_ref[k // sub, :, (k % sub) * LANES : (k % sub + 1) * LANES] = spot.astype(BF16)

    stat_ref[...] = jnp.zeros_like(stat_ref)

    def token_dots(j):
        stat_ref[...] += lax.dot_general(
            x_ref[j], unit_ref[j], (((1,), (1,)), ((), ())), preferred_element_type=F32
        )

    each(width, token_dots)
    dots = jnp.sum(stat_ref[...], axis=1, keepdims=True)
    dots_send[pl.ds(0, tokens), :] = jnp.broadcast_to(dots, (tokens, LANES))
    dots_send[pl.ds(tokens, 8), :] = jnp.broadcast_to(local_square, (8, LANES))
    dots_copy = remote(dots_send, dots_recv, pair_sems.at[0, 0], pair_sems.at[1, 0], sibling)
    dots_copy.start()

    own_matrix.wait()
    col_send[...] = jnp.zeros_like(col_send)

    def column_dots(j):
        col_send[...] += jnp.dot(
            unit_ref[j], matrix_ref[pl.ds(pl.multiple_of(j * block, block), block), :],
            preferred_element_type=F32,
        )

    each(width, column_dots)
    col_copy = remote(col_send, col_recv, pair_sems.at[0, 1], pair_sems.at[1, 1], sibling)
    col_copy.start()


    tick(3)

    dots_copy.wait_recv()
    root = math.sqrt(model_width)
    other_square = dots_recv[pl.ds(tokens, 1), 0:1]
    mean_dir = (local_square + other_square) / model_width + 1e-06
    ratio_mine = jnp.sqrt((local_square / half_width + 1e-06) / mean_dir) / root
    ratio_other = jnp.sqrt((other_square / half_width + 1e-06) / mean_dir) / root
    flat = flat_ref[...] * (lax.rsqrt(mean_dir) / root)
    refusal_ref[...] = flat
    proj_tok[...] = dots_send[pl.ds(0, tokens), :] * ratio_mine + dots_recv[pl.ds(0, tokens), :] * (
        ratio_other
    )

    def square_rows(n):
        here = pl.ds(pl.multiple_of(n * 16, 16), 16)
        amount = proj_tok[here, :]
        total = jnp.zeros((16, LANES), F32)
        for j in range(width):
            for q in range(sub):
                k = j * sub + q
                left = x_ref[j, here, q * LANES : (q + 1) * LANES].astype(F32)
                left = left - amount * refusal_ref[k : k + 1, :]
                total = total + left * left
        square_send[here, :] = total

    each(tokens // 16, square_rows)
    square_copy = remote(square_send, square_recv, pair_sems.at[0, 2], pair_sems.at[1, 2], sibling)
    square_copy.start()

    def up(zz):
        return remote(
            up_send.at[zz], up_recv.at[zz], up_sems.at[0, zz], up_sems.at[1, zz],
            {"dp": lax.rem(me + 2, width)},
        )

    def down(zz):
        return remote(
            down_send.at[zz], down_recv.at[zz], down_sems.at[0, zz], down_sems.at[1, zz],
            {"dp": lax.rem(me - 2 + width, width)},
        )

    def chain_up(n):
        zz = lines - 1 - n

        @pl.when(zz > place)
        def _():
            up_send[zz] = read(diff_ref, 2 * zz + side) + half_recv[zz]

            @pl.when(place > 0)
            def _():
                up(zz).wait_recv()
                up_send[zz] += up_recv[zz]

            up(zz).start()

    def chain_down(zz):
        @pl.when(zz < place)
        def _():
            down_send[zz] = read(diff_ref, 2 * zz + side) + half_recv[zz]

            @pl.when(place < lines - 1)
            def _():
                down(zz).wait_recv()
                down_send[zz] += down_recv[zz]

            down(zz).start()

    each(lines, lambda zz: half(zz).wait_recv())

    @pl.when(place == 0)
    def _():
        each(lines, chain_up)

    @pl.when(place == lines - 1)
    def _():
        each(lines, chain_down)

    @pl.loop(4, lines + 1)
    def _(t):
        tick(t)

    col_copy.wait_recv()
    column_ref[...] = col_send[0:8, :] * ratio_mine + col_recv[0:8, :] * ratio_other

    square_copy.wait_recv()
    mean_square = jnp.sum(square_send[...] + square_recv[...], axis=1, keepdims=True) / model_width
    scale_tok[...] = jnp.broadcast_to(lax.rsqrt(mean_square + 1e-05), (tokens, LANES))

    eye = lax.broadcasted_iota(jnp.int32, (LANES, LANES), 0) == lax.broadcasted_iota(
        jnp.int32, (LANES, LANES), 1
    )
    bands = tokens // LANES
    for b in range(bands):
        here = pl.ds(b * LANES, LANES)
        for s, ref in enumerate((proj_tok, scale_tok)):
            stat_send[pl.ds(s * bands + b, 1), :] = jnp.sum(
                jnp.where(eye, ref[here, :], 0.0), axis=0, keepdims=True
            )
    stat_copy = remote(stat_send, stat_recv, stat_sems.at[0], stat_sems.at[1], {"dp": beside})
    stat_copy.start()

    def normed_rows(base, n, load, proj_at, scale_at):
        here = pl.ds(pl.multiple_of(n * 16, 16), 16)
        amount, scale = proj_at[here, :], scale_at[here, :]
        out = pl.ds(pl.multiple_of(base + n * 16, 16), 16)
        for zz in range(lines):
            j = 2 * zz + side
            vectors = refusal_ref[pl.ds(j * sub, sub), :]
            gains = gain_ref[pl.ds(j * sub, sub), :]
            for q in range(sub):
                value = load(zz, here, pl.ds(q * LANES, LANES)).astype(F32)
                value = (value - amount * vectors[q : q + 1, :]) * scale * gains[q : q + 1, :]
                normed_ref[out, pl.ds(zz * block + q * LANES, LANES)] = value.astype(BF16)

    each(
        tokens // 16,
        lambda n: normed_rows(0, n, lambda zz, a, b: x_ref[2 * zz + side, a, b], proj_tok, scale_tok),
    )

    @pl.when((place > 0) & (place < lines - 1))
    def _():
        each(lines, chain_up)
        each(lines, chain_down)

    def gathered(far):
        ref = part(final_ref, me)
        return remote(
            ref, ref, final_sems.at[0, far], final_sems.at[1, far],
            {"dp": 2 * lax.rem(place + far, lines) + side},
        )

    def gathered_from(far):
        ref = part(final_ref, 2 * lax.rem(place - far + lines, lines) + side)
        return remote(ref, ref, final_sems.at[0, far], final_sems.at[1, far], {"dp": beside})

    def shared(zz):
        ref = part(final_ref, 2 * zz + side)
        return remote(ref, ref, share_sems.at[0, zz], share_sems.at[1, zz], {"dp": beside})

    def shared_from(zz):
        ref = part(final_ref, 2 * zz + 1 - side)
        return remote(ref, ref, share_sems.at[0, zz], share_sems.at[1, zz], {"dp": beside})

    tick(lines + 1)

    stat_copy.wait_recv()
    for b in range(bands):
        here = pl.ds(b * LANES, LANES)
        for s, ref in enumerate((proj_tok, scale_tok)):
            value = jnp.where(eye, stat_recv[pl.ds(s * bands + b, 1), :], 0.0)
            ref[here, :] = jnp.broadcast_to(jnp.sum(value, axis=1, keepdims=True), (LANES, LANES))
    each(lines, lambda zz: swap(zz).wait_recv())
    each(
        tokens // 16,
        lambda n: normed_rows(tokens, n, lambda zz, a, b: swap_ref[zz, a, b], proj_tok, scale_tok),
    )

    def away(u):
        return remote(
            away_send.at[u], away_recv.at[u], away_sems.at[0, u], away_sems.at[1, u], sibling
        )

    def beyond(u):
        return remote(
            side_send.at[u], side_recv.at[u], side_sems.at[0, u], side_sems.at[1, u], {"dp": beside}
        )

    units = 2 * pairs

    def product(u):
        i, odd = u // 2, lax.rem(u, 2)
        which = lax.rem(first + odd, 2)

        @pl.when(odd == 1)
        def _():
            for way in (1, -1):

                @pl.loop(1, lines)
                def _(step):
                    @pl.when(holds(step, way))
                    def _():
                        each(2, lambda h: crossed(step, 2 * i + h, way).wait_recv())

        away_send[u] = jnp.dot(
            normed_ref[...], wall_ref[which, i, 1 - core], preferred_element_type=F32
        )
        away(u).start()
        kept_ref[u] = jnp.dot(normed_ref[...], wall_ref[which, i, core], preferred_element_type=F32)

    def reduce_pair(u):
        away(u).wait_recv()
        side_send[u] = (
            kept_ref[u, pl.ds(tokens, tokens), :] + away_recv[u, pl.ds(tokens, tokens), :]
        ).astype(BF16)
        beyond(u).start()

    def reduce_side(u):
        i, odd = u // 2, lax.rem(u, 2)
        which = lax.rem(first + odd, 2)
        beyond(u).wait_recv()
        total = kept_ref[u, pl.ds(0, tokens), :] + away_recv[u, pl.ds(0, tokens), :]
        total = total + side_recv[u].astype(F32)
        kv_ref[which, :, pl.ds(pl.multiple_of(i * LANES, LANES), LANES)] = total.astype(BF16)

    for m in range(2):
        each(pieces, lambda pc: own_wall(m, pc).wait())

    @pl.loop(0, pairs)
    def _(i):
        each(2, lambda odd: product(2 * i + odd))
        each(2, lambda odd: reduce_pair(2 * i + odd))

        @pl.when(i > 0)
        def _():
            each(2, lambda odd: reduce_side(2 * i - 2 + odd))

        @pl.loop(lines + 2 + (3 * i) // 2, jnp.minimum(lines + 2 + (3 * i + 3) // 2, ticks))
        def _(t):
            tick(t)

        @pl.when(i == pairs - 3)
        def _():
            down_send[place] = read(diff_ref, me) + half_recv[place]

            @pl.when(place > 0)
            def _():
                up(place).wait_recv()
                down_send[place] += up_recv[place]

            @pl.when(place < lines - 1)
            def _():
                down(place).wait_recv()
                down_send[place] += down_recv[place]

            final_ref[pl.ds(pl.multiple_of(me * chunk, 16), chunk), :] = down_send[place].astype(BF16)

            @pl.loop(1, lines)
            def _(far):
                gathered(far).start()

            shared(place).start()


        @pl.when(i == pairs - 2)
        def _():
            @pl.loop(1, lines)
            def _(far):
                gathered_from(far).wait_recv()
                shared(lax.rem(place - far + lines, lines)).start()

    def finish_layers():
        if True:
            each(lines, lambda zz: shared_from(zz).wait_recv())

            @pl.loop(0, layers // 8)
            def _(t):
                total = jnp.zeros((8, LANES), F32)
                for k in range(0, tiles, 2):
                    rows16 = pl.ds(pl.multiple_of(t * (8 * tiles) + k * 8, 16), 16)
                    value = final_ref[rows16, :].astype(F32)
                    total = total + value[0:8] * value[0:8] + value[8:16] * value[8:16]
                layer_send[pl.ds(pl.multiple_of(t * 8, 8), 8), :] = total

            remote(
                layer_send, layer_recv, pair_sems.at[0, 3], pair_sems.at[1, 3], sibling
            ).start()

    finish_layers()
    layer_copy = remote(layer_send, layer_recv, pair_sems.at[0, 3], pair_sems.at[1, 3], sibling)
    layer_copy.wait_recv()

    @pl.loop(0, layers // 8)
    def _(t):
        here = pl.ds(pl.multiple_of(t * 8, 8), 8)
        mean = jnp.sum(layer_send[here, :] + layer_recv[here, :], axis=1, keepdims=True) / model_width
        norm = jnp.broadcast_to(lax.rsqrt(mean + 1e-06), (8, LANES))
        norm = jnp.concatenate([norm, norm], axis=0)
        for k in range(0, tiles, 2):
            rows16 = pl.ds(pl.multiple_of(t * (8 * tiles) + k * 8, 16), 16)
            dirs_ref[rows16, :] = final_ref[rows16, :].astype(F32) * norm

    reduce_side(units - 2)
    reduce_side(units - 1)

    @pl.loop(1, width)
    def _(far):
        spread(count_send, count_recv, count_sems, far).wait_send()
        spread(pick_send, pick_recv, pick_sems, far).wait_send()

    @pl.loop(1, lines)
    def _(far):
        gathered(far).wait_send()

    def drain(zz):
        swap(zz).wait_send()
        half(zz).wait_send()
        shared(zz).wait_send()

        @pl.when(zz > place)
        def _():
            up(zz).wait_send()

        @pl.when(zz < place)
        def _():
            down(zz).wait_send()

    each(lines, drain)
    dots_copy.wait_send()
    col_copy.wait_send()
    square_copy.wait_send()
    layer_copy.wait_send()
    stat_copy.wait_send()

    def drain_unit(u):
        away(u).wait_send()
        beyond(u).wait_send()

    each(units, drain_unit)

    @pl.loop(1, lines)
    def _(step):
        def drain_piece(pc):
            for way in (1, -1):

                @pl.when(sends(step, way))
                def _():
                    hop(step, pc, way).wait_send()

                @pl.when(holds(step, way))
                def _():
                    cross(step, pc, way).wait_send()

        each(pieces, drain_piece)


def fused(lines, prompts, length, lengths, labels, chosen, rows, earlier, gain, key, value, matrix):
    tokens, half_width = rows.shape
    width = 2 * lines
    block = half_width // width
    tiles = half_width // LANES
    layers = earlier.shape[0] // (2 * tiles) + 1
    columns = key.shape[1]
    pieces = columns // LANES
    pairs = pieces // 2
    units = 2 * pairs
    flat_rows = layers * tiles
    chunk = flat_rows // width
    smem = pl.BlockSpec(memory_space=pltpu.SMEM)
    vmem = pl.BlockSpec(memory_space=pltpu.VMEM)
    hbm = pl.BlockSpec(memory_space=pl.ANY)
    dma = pltpu.SemaphoreType.DMA
    return pl.pallas_call(
        functools.partial(fused_kernel, (lines, pieces, prompts, length, layers)),
        out_shape=(
            jax.ShapeDtypeStruct((flat_rows, LANES), F32),
            jax.ShapeDtypeStruct((2, tokens, columns // 2), BF16),
            jax.ShapeDtypeStruct((tiles, LANES), F32),
            jax.ShapeDtypeStruct((8, matrix.shape[1]), F32),
        ),
        in_specs=[smem, smem, smem, hbm, hbm, vmem, hbm, hbm, hbm],
        out_specs=[vmem] * 4,
        scratch_shapes=[
            pltpu.VMEM((width, tokens, block), BF16),
            pltpu.VMEM((lines, tokens, block), BF16),
            pltpu.VMEM((2, pairs, 2, lines * key.shape[0], LANES), BF16),
            pltpu.VMEM((2 * tokens, half_width // 2), BF16),
            pltpu.VMEM(matrix.shape, BF16),
            pltpu.VMEM(earlier.shape, F32),
            pltpu.VMEM((flat_rows, LANES), F32),
        ]
        + [pltpu.VMEM((lines, chunk, LANES), F32)] * 5
        + [
            pltpu.VMEM((flat_rows, LANES), BF16),
            pltpu.VMEM((8, LANES), F32),
            pltpu.VMEM((width, 8, LANES), F32),
            pltpu.VMEM((tiles, LANES), F32),
            pltpu.VMEM((width, tiles, LANES), F32),
            pltpu.VMEM((width, 16, block), BF16),
            pltpu.VMEM((tiles, LANES), F32),
            pltpu.VMEM((2, tiles, LANES), F32),
            pltpu.VMEM((tokens + 8, LANES), F32),
            pltpu.VMEM((tokens + 8, LANES), F32),
            pltpu.VMEM((tokens, LANES), F32),
            pltpu.VMEM((tokens, LANES), F32),
            pltpu.VMEM((tokens, 16), F32),
            pltpu.VMEM((tokens, LANES), F32),
            pltpu.VMEM((tokens, LANES), F32),
            pltpu.VMEM((8, LANES), F32),
            pltpu.VMEM((8, LANES), F32),
            pltpu.VMEM((16, matrix.shape[1]), F32),
            pltpu.VMEM((16, matrix.shape[1]), F32),
            pltpu.VMEM((layers, LANES), F32),
            pltpu.VMEM((layers, LANES), F32),
            pltpu.VMEM((units, 2 * tokens, LANES), F32),
            pltpu.VMEM((units, 2 * tokens, LANES), F32),
            pltpu.VMEM((units, 2 * tokens, LANES), F32),
            pltpu.VMEM((units, tokens, LANES), BF16),
            pltpu.VMEM((units, tokens, LANES), BF16),
            dma((width,)),
            dma((2, pieces)),
            dma((1,)),
            dma((1,)),
        ]
        + [dma((2, lines, pieces))] * 4
        + [
            dma((2, width)),
            dma((2, width)),
            dma((2, lines)),
            dma((2, lines)),
            dma((2, lines)),
            dma((2, lines)),
            dma((2, lines)),
            dma((2, lines)),
            dma((2, 4)),
            dma((2,)),
            dma((2, units)),
            dma((2, units)),
        ],
        compiler_params=pltpu.CompilerParams(
            collective_id=0, has_side_effects=True, vmem_limit_bytes=60 << 20
        ),
        name="fused",
    )(lengths, labels, chosen, rows, earlier, gain, key, value, matrix)


def shards(
    residual, lengths, labels, earlier_means, chosen, norm_gain, key_weight, value_weight, out_proj
):
    prompts, length, half_width = residual.shape
    lines = lax.axis_size("dp") // 2
    tiles = half_width // LANES
    earlier = earlier_means[0]
    layers = earlier.shape[0] + 1
    earlier = earlier.reshape(layers - 1, 2, tiles, LANES).transpose(0, 2, 1, 3).reshape(-1, LANES)
    matrix = out_proj[0]
    flat, caches, refusal, column = fused(
        lines, prompts, length, lengths, labels, chosen, residual.reshape(-1, half_width), earlier,
        norm_gain.reshape(tiles, LANES), key_weight[0], value_weight[0], matrix,
    )
    directions = (
        flat.reshape(layers // 8, tiles, 8, LANES).transpose(0, 2, 1, 3).reshape(layers, half_width)
    )
    refusal_dir = refusal.reshape(half_width)
    column_proj = jnp.sum(column[:3], axis=0)
    ortho_proj = (matrix.astype(F32) - refusal_dir[:, None] * column_proj[None, :]).astype(BF16)[None]
    caches = caches.reshape(2, prompts, length, -1)
    return (directions, caches[0], caches[1], ortho_proj)


def solution(mesh):
    return jax.shard_map(
        shards,
        mesh=mesh,
        in_specs=(
            P(("groups", "dp"), None, "mp"),
            P(("groups", "dp")),
            P(("groups", "dp")),
            P(("groups", "dp"), None, None, "mp"),
            P("groups"),
            P("mp"),
            P("mp", "dp", None),
            P("mp", "dp", None),
            P("groups", "mp", "dp"),
        ),
        out_specs=(
            P("groups", "mp"),
            P(("groups", "dp"), None, "mp"),
            P(("groups", "dp"), None, "mp"),
            P("groups", "mp", "dp"),
        ),
        check_vma=False,
    )
```

```python
import functools
import math

import jax
import jax.numpy as jnp
from jax import lax
from jax.experimental import pallas as pl
from jax.experimental.pallas import tpu as pltpu
from jax.sharding import PartitionSpec as P

MESH = pl.DeviceIdType.MESH
F32, BF16 = jnp.float32, jnp.bfloat16
LANES = 128


def fused_kernel(
    cfg,
    lengths_ref, labels_ref, chosen_ref, res_ref, earlier_ref, gains_ref, key_ref, value_ref, proj_ref,
    dirs_ref, kv_ref, refusal_ref, column_ref,
    gain_ref, x_ref, swap_ref, wall_ref, normed_ref, matrix_ref, means_ref, diff_ref,
    half_recv, up_send, up_recv, down_send, down_recv, final_ref,
    count_send, count_recv, pick_send, pick_recv, unit_ref, flat_ref, current_ref,
    dots_send, dots_recv, square_send, square_recv, stat_ref, proj_tok, scale_tok, stat_send, stat_recv,
    col_send, col_recv, layer_send, layer_recv,
    away_send, away_recv, kept_ref, side_send, side_recv,
    x_sem, wall_sem, means_sem, matrix_sem,
    hop_send, hop_recv, cross_send, cross_recv,
    count_sems, pick_sems, swap_sems, half_sems, up_sems, down_sems, final_sems, share_sems,
    pair_sems, stat_sems, away_sems, side_sems,
):
    lines, pieces, prompts, length, layers = cfg
    width = 2 * lines
    tokens, half_width = res_ref.shape
    block = half_width // width
    rows = key_ref.shape[0]
    sub = block // LANES
    tiles = half_width // LANES
    pairs = pieces // 2
    model_width = 2 * half_width
    chunk = diff_ref.shape[0] // width
    group, me, core = lax.axis_index("groups"), lax.axis_index("dp"), lax.axis_index("mp")
    place, side = me // 2, lax.rem(me, 2)
    beside = me + 1 - 2 * side
    first = lax.rem(group, 2)
    across = group + 1 - 2 * first
    sibling = {"mp": 1 - core}

    def remote(src, dst, send, recv, device):
        return pltpu.make_async_remote_copy(
            src_ref=src, dst_ref=dst, send_sem=send, recv_sem=recv, device_id=device,
            device_id_type=MESH,
        )

    barrier = pltpu.get_barrier_semaphore()

    @pl.loop(1, width)
    def _(far):
        pl.semaphore_signal(
            barrier, inc=1, device_id={"dp": lax.rem(me + far, width)}, device_id_type=MESH
        )

    pl.semaphore_signal(barrier, inc=1, device_id={"groups": across}, device_id_type=MESH)
    pl.semaphore_signal(barrier, inc=1, device_id=sibling, device_id_type=MESH)

    def each(count, body):
        @pl.loop(0, count)
        def _(n):
            body(n)

    def own_x(j):
        return pltpu.make_async_copy(
            res_ref.at[:, pl.ds(pl.multiple_of(j * block, block), block)], x_ref.at[j], x_sem.at[j]
        )

    each(width, lambda j: own_x(j).start())
    own_means = pltpu.make_async_copy(earlier_ref, means_ref, means_sem.at[0])
    own_means.start()
    own_gains = pltpu.make_async_copy(gains_ref, gain_ref, means_sem.at[1])
    own_gains.start()

    ones = jnp.int32(0)
    for p in range(prompts):
        ones = ones + labels_ref[p]
    line = lax.broadcasted_iota(jnp.int32, (8, LANES), 0)
    harmful = jnp.full((8, LANES), ones.astype(F32))
    harmless = jnp.full((8, LANES), (prompts - ones).astype(F32))
    count_send[...] = jnp.where(line == 0, harmless, harmful)

    pl.semaphore_wait(barrier, width + 1)

    def slot_of(step, way):
        return lax.rem(place - way * step + width * lines, lines)

    def wall_at(slot, pc):
        return wall_ref.at[
            first, pc // 2, lax.rem(pc, 2), pl.ds(pl.multiple_of(slot * rows, rows), rows), :
        ]

    def hop(step, pc, way, source=None):
        k = 0 if way > 0 else 1
        ref = wall_at(slot_of(step - 1, way), pc)
        return remote(
            ref if source is None else source, ref, hop_send.at[k, step, pc], hop_recv.at[k, step, pc],
            {"dp": lax.rem(me + 2 * way + width, width)},
        )

    def arrival(step, pc, way):
        k = 0 if way > 0 else 1
        ref = wall_at(slot_of(step, way), pc)
        return remote(
            ref, ref, hop_send.at[k, step, pc], hop_recv.at[k, step, pc],
            {"dp": lax.rem(me - 2 * way + width, width)},
        )

    def cross(step, pc, way):
        k = 0 if way > 0 else 1
        ref = wall_at(slot_of(step, way), pc)
        return remote(
            ref, ref, cross_send.at[k, step, pc], cross_recv.at[k, step, pc], {"groups": across}
        )

    def crossed(step, pc, way):
        k = 0 if way > 0 else 1
        ref = wall_ref.at[
            1 - first, pc // 2, lax.rem(pc, 2),
            pl.ds(pl.multiple_of(slot_of(step, way) * rows, rows), rows), :,
        ]
        return remote(
            ref, ref, cross_send.at[k, step, pc], cross_recv.at[k, step, pc], {"groups": across}
        )

    def sends(step, way):
        return (place >= step - 1) & (place < lines - 1) if way > 0 else (
            (place > 0) & (place <= lines - step)
        )

    def holds(step, way):
        return place >= step if way > 0 else place < lines - step

    def piece_of(ref, pc):
        column = (lax.rem(pc, 2) * pairs + pc // 2) * LANES
        return ref.at[:, pl.ds(pl.multiple_of(column, LANES), LANES)]

    def start_own(pc):
        for way in (1, -1):
            for m, ref in enumerate((key_ref, value_ref)):

                @pl.when(sends(1, way) & (first == m))
                def _():
                    hop(1, pc, way, piece_of(ref, pc)).start()

    window = 2
    ticks = pieces + lines - 2
    each(window, start_own)

    def service(step, pc):
        for way in (1, -1):

            @pl.when(holds(step, way))
            def _():
                arrival(step, pc, way).wait_recv()

                @pl.when(sends(step + 1, way) & (step < lines - 1))
                def _():
                    hop(step + 1, pc, way).start()

                cross(step, pc, way).start()

    def tick(t):
        @pl.when(t + window < pieces)
        def _():
            start_own(t + window)

        @pl.loop(jnp.maximum(1, t - pieces + 2), jnp.minimum(lines, t + 2))
        def _(step):
            service(step, t - step + 1)

    def swap(zz):
        j = 2 * zz + 1 - side
        return remote(
            res_ref.at[:, pl.ds(pl.multiple_of(j * block, block), block)], swap_ref.at[zz],
            swap_sems.at[0, zz], swap_sems.at[1, zz], {"dp": beside},
        )

    early = max(lines // 4, 1)
    each(early, lambda zz: swap(zz).start())

    def spread(send_ref, recv_ref, sems, far):
        return remote(
            send_ref, recv_ref.at[me], sems.at[0, far], sems.at[1, far],
            {"dp": lax.rem(me + far, width)},
        )

    @pl.loop(1, width)
    def _(far):
        spread(count_send, count_recv, count_sems, far).start()

    count_recv[me] = count_send[...]

    def own_wall(m, pc):
        ref = (key_ref, value_ref)[m]
        return pltpu.make_async_copy(
            piece_of(ref, pc),
            wall_ref.at[
                m, pc // 2, lax.rem(pc, 2), pl.ds(pl.multiple_of(place * rows, rows), rows), :
            ],
            wall_sem.at[m, pc],
        )

    each(width, lambda j: own_x(j).wait())
    own_matrix = pltpu.make_async_copy(proj_ref, matrix_ref, matrix_sem.at[0])
    own_matrix.start()
    for m in range(2):
        each(pieces, lambda pc: own_wall(m, pc).start())

    tick(0)

    row_id = lax.broadcasted_iota(jnp.int32, (16, tokens), 0)
    token_id = lax.broadcasted_iota(jnp.int32, (16, tokens), 1)
    mask = jnp.zeros((16, tokens), F32)
    for p in range(prompts):
        inside = (token_id >= p * length) & (token_id < p * length + lengths_ref[p])
        mask = jnp.where(inside & (row_id == p), 1.0, mask)
    mask = mask.astype(BF16)

    def class_sums(j):
        sums = jnp.dot(mask, x_ref[j], preferred_element_type=F32)
        current = [jnp.zeros((1, block), F32), jnp.zeros((1, block), F32)]
        for p in range(prompts):
            mean = sums[p : p + 1, :] / jnp.full((1, block), lengths_ref[p].astype(F32))
            label = labels_ref[p].astype(F32)
            current[1] = current[1] + mean * label
            current[0] = current[0] + mean * (1.0 - label)
        current[0] = current[0] / jnp.full((1, block), (prompts - ones).astype(F32))
        current[1] = current[1] / jnp.full((1, block), ones.astype(F32))
        for c in range(2):
            for q in range(sub):
                current_ref[c, pl.ds(j * sub + q, 1), :] = current[c][:, q * LANES : (q + 1) * LANES]

    each(width, class_sums)

    @pl.loop(1, width)
    def _(far):
        spread(count_send, count_recv, count_sems, far).wait_recv()

    totals = count_recv[0]
    for j in range(1, width):
        totals = totals + count_recv[j]
    share = count_send[...] / totals
    share0, share1 = share[0:1, :], share[1:2, :]

    own_means.wait()
    own_gains.wait()
    current_diff = share1 * current_ref[1] - share0 * current_ref[0]
    at = jnp.minimum(chosen_ref[0], layers - 2) * (2 * tiles)
    picked = share1 * means_ref[pl.ds(at + 1, tiles, stride=2), :] - share0 * means_ref[
        pl.ds(at, tiles, stride=2), :
    ]
    pick_send[...] = jnp.where(chosen_ref[0] == layers - 1, current_diff, picked)

    @pl.loop(1, width)
    def _(far):
        spread(pick_send, pick_recv, pick_sems, far).start()

    pick_recv[me] = pick_send[...]

    @pl.loop(0, layers - 1)
    def _(l):
        e = l * (2 * tiles)
        d = share1 * means_ref[pl.ds(e + 1, tiles, stride=2), :] - share0 * means_ref[
            pl.ds(e, tiles, stride=2), :
        ]
        diff_ref[pl.ds((l // 8) * (8 * tiles) + lax.rem(l, 8), tiles, stride=8), :] = d

    diff_ref[pl.ds(((layers - 1) // 8) * (8 * tiles) + (layers - 1) % 8, tiles, stride=8), :] = (
        current_diff
    )

    def part(ref, j):
        return ref.at[pl.ds(pl.multiple_of(j * chunk, 16), chunk), :]

    def read(ref, j):
        return ref[pl.ds(pl.multiple_of(j * chunk, 16), chunk), :]

    def half(zz):
        return remote(
            part(diff_ref, 2 * zz + 1 - side), half_recv.at[zz], half_sems.at[0, zz],
            half_sems.at[1, zz], {"dp": beside},
        )

    each(lines, lambda zz: half(zz).start())
    each(lines - early, lambda zz: swap(zz + early).start())

    tick(1)
    tick(2)


    @pl.loop(1, width)
    def _(far):
        spread(pick_send, pick_recv, pick_sems, far).wait_recv()

    picked = pick_recv[0]
    for j in range(1, width):
        picked = picked + pick_recv[j]
    local_square = jnp.sum(jnp.sum(picked * picked, axis=1, keepdims=True), axis=0, keepdims=True)
    unit = picked * lax.rsqrt(local_square / half_width + 1e-06)
    flat_ref[...] = picked
    high = unit.astype(BF16).astype(F32)
    middle = (unit - high).astype(BF16).astype(F32)
    low = unit - high - middle
    line16 = lax.broadcasted_iota(jnp.int32, (16, LANES), 0)
    for k in range(tiles):
        spot = jnp.where(
            line16 == 0, high[k : k + 1, :],
            jnp.where(line16 == 1, middle[k : k + 1, :], jnp.where(line16 == 2, low[k : k + 1, :], 0.0)),
        )
        unit_ref[k // sub, :, (k % sub) * LANES : (k % sub + 1) * LANES] = spot.astype(BF16)

    stat_ref[...] = jnp.zeros_like(stat_ref)

    def token_dots(j):
        stat_ref[...] += lax.dot_general(
            x_ref[j], unit_ref[j], (((1,), (1,)), ((), ())), preferred_element_type=F32
        )

    each(width, token_dots)
    dots = jnp.sum(stat_ref[...], axis=1, keepdims=True)
    dots_send[pl.ds(0, tokens), :] = jnp.broadcast_to(dots, (tokens, LANES))
    dots_send[pl.ds(tokens, 8), :] = jnp.broadcast_to(local_square, (8, LANES))
    dots_copy = remote(dots_send, dots_recv, pair_sems.at[0, 0], pair_sems.at[1, 0], sibling)
    dots_copy.start()

    own_matrix.wait()
    col_send[...] = jnp.zeros_like(col_send)

    def column_dots(j):
        col_send[...] += jnp.dot(
            unit_ref[j], matrix_ref[pl.ds(pl.multiple_of(j * block, block), block), :],
            preferred_element_type=F32,
        )

    each(width, column_dots)
    col_copy = remote(col_send, col_recv, pair_sems.at[0, 1], pair_sems.at[1, 1], sibling)
    col_copy.start()


    tick(3)

    dots_copy.wait_recv()
    root = math.sqrt(model_width)
    other_square = dots_recv[pl.ds(tokens, 1), 0:1]
    mean_dir = (local_square + other_square) / model_width + 1e-06
    ratio_mine = jnp.sqrt((local_square / half_width + 1e-06) / mean_dir) / root
    ratio_other = jnp.sqrt((other_square / half_width + 1e-06) / mean_dir) / root
    flat = flat_ref[...] * (lax.rsqrt(mean_dir) / root)
    refusal_ref[...] = flat
    proj_tok[...] = dots_send[pl.ds(0, tokens), :] * ratio_mine + dots_recv[pl.ds(0, tokens), :] * (
        ratio_other
    )

    def square_rows(n):
        here = pl.ds(pl.multiple_of(n * 16, 16), 16)
        amount = proj_tok[here, :]
        total = jnp.zeros((16, LANES), F32)
        for j in range(width):
            for q in range(sub):
                k = j * sub + q
                left = x_ref[j, here, q * LANES : (q + 1) * LANES].astype(F32)
                left = left - amount * refusal_ref[k : k + 1, :]
                total = total + left * left
        square_send[here, :] = total

    each(tokens // 16, square_rows)
    square_copy = remote(square_send, square_recv, pair_sems.at[0, 2], pair_sems.at[1, 2], sibling)
    square_copy.start()

    def up(zz):
        return remote(
            up_send.at[zz], up_recv.at[zz], up_sems.at[0, zz], up_sems.at[1, zz],
            {"dp": lax.rem(me + 2, width)},
        )

    def down(zz):
        return remote(
            down_send.at[zz], down_recv.at[zz], down_sems.at[0, zz], down_sems.at[1, zz],
            {"dp": lax.rem(me - 2 + width, width)},
        )

    def chain_up(n):
        zz = lines - 1 - n

        @pl.when(zz > place)
        def _():
            up_send[zz] = read(diff_ref, 2 * zz + side) + half_recv[zz]

            @pl.when(place > 0)
            def _():
                up(zz).wait_recv()
                up_send[zz] += up_recv[zz]

            up(zz).start()

    def chain_down(zz):
        @pl.when(zz < place)
        def _():
            down_send[zz] = read(diff_ref, 2 * zz + side) + half_recv[zz]

            @pl.when(place < lines - 1)
            def _():
                down(zz).wait_recv()
                down_send[zz] += down_recv[zz]

            down(zz).start()

    each(lines, lambda zz: half(zz).wait_recv())

    @pl.when(place == 0)
    def _():
        each(lines, chain_up)

    @pl.when(place == lines - 1)
    def _():
        each(lines, chain_down)

    @pl.loop(4, lines + 1)
    def _(t):
        tick(t)

    col_copy.wait_recv()
    column = col_send[...] * ratio_mine + col_recv[...] * ratio_other
    column_ref[...] = jnp.broadcast_to(jnp.sum(column, axis=0, keepdims=True), column_ref.shape)

    square_copy.wait_recv()
    mean_square = jnp.sum(square_send[...] + square_recv[...], axis=1, keepdims=True) / model_width
    scale_tok[...] = jnp.broadcast_to(lax.rsqrt(mean_square + 1e-05), (tokens, LANES))

    eye = lax.broadcasted_iota(jnp.int32, (LANES, LANES), 0) == lax.broadcasted_iota(
        jnp.int32, (LANES, LANES), 1
    )
    bands = tokens // LANES
    for b in range(bands):
        here = pl.ds(b * LANES, LANES)
        for s, ref in enumerate((proj_tok, scale_tok)):
            stat_send[pl.ds(s * bands + b, 1), :] = jnp.sum(
                jnp.where(eye, ref[here, :], 0.0), axis=0, keepdims=True
            )
    stat_copy = remote(stat_send, stat_recv, stat_sems.at[0], stat_sems.at[1], {"dp": beside})
    stat_copy.start()

    def normed_rows(base, n, load, proj_at, scale_at):
        here = pl.ds(pl.multiple_of(n * 16, 16), 16)
        amount, scale = proj_at[here, :], scale_at[here, :]
        out = pl.ds(pl.multiple_of(base + n * 16, 16), 16)
        for zz in range(lines):
            j = 2 * zz + side
            vectors = refusal_ref[pl.ds(j * sub, sub), :]
            gains = gain_ref[pl.ds(j * sub, sub), :]
            for q in range(sub):
                value = load(zz, here, pl.ds(q * LANES, LANES)).astype(F32)
                value = (value - amount * vectors[q : q + 1, :]) * scale * gains[q : q + 1, :]
                normed_ref[out, pl.ds(zz * block + q * LANES, LANES)] = value.astype(BF16)

    each(
        tokens // 16,
        lambda n: normed_rows(0, n, lambda zz, a, b: x_ref[2 * zz + side, a, b], proj_tok, scale_tok),
    )

    @pl.when((place > 0) & (place < lines - 1))
    def _():
        each(lines, chain_up)
        each(lines, chain_down)

    def gathered(far):
        ref = part(final_ref, me)
        return remote(
            ref, ref, final_sems.at[0, far], final_sems.at[1, far],
            {"dp": 2 * lax.rem(place + far, lines) + side},
        )

    def gathered_from(far):
        ref = part(final_ref, 2 * lax.rem(place - far + lines, lines) + side)
        return remote(ref, ref, final_sems.at[0, far], final_sems.at[1, far], {"dp": beside})

    def shared(zz):
        ref = part(final_ref, 2 * zz + side)
        return remote(ref, ref, share_sems.at[0, zz], share_sems.at[1, zz], {"dp": beside})

    def shared_from(zz):
        ref = part(final_ref, 2 * zz + 1 - side)
        return remote(ref, ref, share_sems.at[0, zz], share_sems.at[1, zz], {"dp": beside})

    tick(lines + 1)

    stat_copy.wait_recv()
    for b in range(bands):
        here = pl.ds(b * LANES, LANES)
        for s, ref in enumerate((proj_tok, scale_tok)):
            value = jnp.where(eye, stat_recv[pl.ds(s * bands + b, 1), :], 0.0)
            ref[here, :] = jnp.broadcast_to(jnp.sum(value, axis=1, keepdims=True), (LANES, LANES))
    each(lines, lambda zz: swap(zz).wait_recv())
    each(
        tokens // 16,
        lambda n: normed_rows(tokens, n, lambda zz, a, b: swap_ref[zz, a, b], proj_tok, scale_tok),
    )

    def away(u):
        return remote(
            away_send.at[u], away_recv.at[u], away_sems.at[0, u], away_sems.at[1, u], sibling
        )

    def beyond(u):
        return remote(
            side_send.at[u], side_recv.at[u], side_sems.at[0, u], side_sems.at[1, u], {"dp": beside}
        )

    units = 2 * pairs

    def product(u):
        i, odd = u // 2, lax.rem(u, 2)
        which = lax.rem(first + odd, 2)

        @pl.when(odd == 1)
        def _():
            for way in (1, -1):

                @pl.loop(1, lines)
                def _(step):
                    @pl.when(holds(step, way))
                    def _():
                        each(2, lambda h: crossed(step, 2 * i + h, way).wait_recv())

        away_send[u] = jnp.dot(
            normed_ref[...], wall_ref[which, i, 1 - core], preferred_element_type=F32
        )
        away(u).start()
        kept_ref[u] = jnp.dot(normed_ref[...], wall_ref[which, i, core], preferred_element_type=F32)

    def reduce_pair(u):
        away(u).wait_recv()
        side_send[u] = (
            kept_ref[u, pl.ds(tokens, tokens), :] + away_recv[u, pl.ds(tokens, tokens), :]
        ).astype(BF16)
        beyond(u).start()

    def reduce_side(u):
        i, odd = u // 2, lax.rem(u, 2)
        which = lax.rem(first + odd, 2)
        beyond(u).wait_recv()
        total = kept_ref[u, pl.ds(0, tokens), :] + away_recv[u, pl.ds(0, tokens), :]
        total = total + side_recv[u].astype(F32)
        kv_ref[which, :, pl.ds(pl.multiple_of(i * LANES, LANES), LANES)] = total.astype(BF16)

    for m in range(2):
        each(pieces, lambda pc: own_wall(m, pc).wait())

    @pl.loop(0, pairs)
    def _(i):
        product(2 * i)

        @pl.when(i == pairs - 1)
        def _():
            @pl.loop(1, lines)
            def _(far):
                gathered_from(far).wait_recv()
                shared(lax.rem(place - far + lines, lines)).start()

        product(2 * i + 1)
        each(2, lambda odd: reduce_pair(2 * i + odd))

        @pl.when(i > 0)
        def _():
            each(2, lambda odd: reduce_side(2 * i - 2 + odd))

        @pl.loop(lines + 2 + (3 * i) // 2, jnp.minimum(lines + 2 + (3 * i + 3) // 2, ticks))
        def _(t):
            tick(t)

        @pl.when(i == pairs - 3)
        def _():
            down_send[place] = read(diff_ref, me) + half_recv[place]

            @pl.when(place > 0)
            def _():
                up(place).wait_recv()
                down_send[place] += up_recv[place]

            @pl.when(place < lines - 1)
            def _():
                down(place).wait_recv()
                down_send[place] += down_recv[place]

            final_ref[pl.ds(pl.multiple_of(me * chunk, 16), chunk), :] = down_send[place].astype(BF16)

            @pl.loop(1, lines)
            def _(far):
                gathered(far).start()

            shared(place).start()


    def finish_layers():
        if True:
            each(lines, lambda zz: shared_from(zz).wait_recv())

            @pl.loop(0, layers // 8)
            def _(t):
                total = jnp.zeros((8, LANES), F32)
                for k in range(0, tiles, 2):
                    rows16 = pl.ds(pl.multiple_of(t * (8 * tiles) + k * 8, 16), 16)
                    value = final_ref[rows16, :].astype(F32)
                    total = total + value[0:8] * value[0:8] + value[8:16] * value[8:16]
                layer_send[pl.ds(pl.multiple_of(t * 8, 8), 8), :] = total

            remote(
                layer_send, layer_recv, pair_sems.at[0, 3], pair_sems.at[1, 3], sibling
            ).start()

    finish_layers()
    layer_copy = remote(layer_send, layer_recv, pair_sems.at[0, 3], pair_sems.at[1, 3], sibling)
    layer_copy.wait_recv()

    @pl.loop(0, layers // 8)
    def _(t):
        here = pl.ds(pl.multiple_of(t * 8, 8), 8)
        mean = jnp.sum(layer_send[here, :] + layer_recv[here, :], axis=1, keepdims=True) / model_width
        norm = jnp.broadcast_to(lax.rsqrt(mean + 1e-06), (8, LANES))
        norm = jnp.concatenate([norm, norm], axis=0)
        for k in range(0, tiles, 2):
            rows16 = pl.ds(pl.multiple_of(t * (8 * tiles) + k * 8, 16), 16)
            dirs_ref[rows16, :] = final_ref[rows16, :].astype(F32) * norm

    reduce_side(units - 2)
    reduce_side(units - 1)

    @pl.loop(1, width)
    def _(far):
        spread(count_send, count_recv, count_sems, far).wait_send()
        spread(pick_send, pick_recv, pick_sems, far).wait_send()

    @pl.loop(1, lines)
    def _(far):
        gathered(far).wait_send()

    def drain(zz):
        swap(zz).wait_send()
        half(zz).wait_send()
        shared(zz).wait_send()

        @pl.when(zz > place)
        def _():
            up(zz).wait_send()

        @pl.when(zz < place)
        def _():
            down(zz).wait_send()

    each(lines, drain)
    dots_copy.wait_send()
    col_copy.wait_send()
    square_copy.wait_send()
    layer_copy.wait_send()
    stat_copy.wait_send()

    def drain_unit(u):
        away(u).wait_send()
        beyond(u).wait_send()

    each(units, drain_unit)

    @pl.loop(1, lines)
    def _(step):
        def drain_piece(pc):
            for way in (1, -1):

                @pl.when(sends(step, way))
                def _():
                    hop(step, pc, way).wait_send()

                @pl.when(holds(step, way))
                def _():
                    cross(step, pc, way).wait_send()

        each(pieces, drain_piece)


def fused(lines, prompts, length, lengths, labels, chosen, rows, earlier, gain, key, value, matrix):
    tokens, half_width = rows.shape
    width = 2 * lines
    block = half_width // width
    tiles = half_width // LANES
    layers = earlier.shape[0] // (2 * tiles) + 1
    columns = key.shape[1]
    pieces = columns // LANES
    pairs = pieces // 2
    units = 2 * pairs
    flat_rows = layers * tiles
    chunk = flat_rows // width
    smem = pl.BlockSpec(memory_space=pltpu.SMEM)
    vmem = pl.BlockSpec(memory_space=pltpu.VMEM)
    hbm = pl.BlockSpec(memory_space=pltpu.HBM)
    dma = pltpu.SemaphoreType.DMA
    return pl.pallas_call(
        functools.partial(fused_kernel, (lines, pieces, prompts, length, layers)),
        out_shape=(
            jax.ShapeDtypeStruct((flat_rows, LANES), F32),
            jax.ShapeDtypeStruct((2, tokens, columns // 2), BF16),
            jax.ShapeDtypeStruct((tiles, LANES), F32),
            jax.ShapeDtypeStruct((8, matrix.shape[1]), F32),
        ),
        in_specs=[smem, smem, smem, hbm, hbm, hbm, hbm, hbm, hbm],
        out_specs=[vmem] * 4,
        scratch_shapes=[
            pltpu.VMEM((tiles, LANES), F32),
            pltpu.VMEM((width, tokens, block), BF16),
            pltpu.VMEM((lines, tokens, block), BF16),
            pltpu.VMEM((2, pairs, 2, lines * key.shape[0], LANES), BF16),
            pltpu.VMEM((2 * tokens, half_width // 2), BF16),
            pltpu.VMEM(matrix.shape, BF16),
            pltpu.VMEM(earlier.shape, F32),
            pltpu.VMEM((flat_rows, LANES), F32),
        ]
        + [pltpu.VMEM((lines, chunk, LANES), F32)] * 5
        + [
            pltpu.VMEM((flat_rows, LANES), BF16),
            pltpu.VMEM((8, LANES), F32),
            pltpu.VMEM((width, 8, LANES), F32),
            pltpu.VMEM((tiles, LANES), F32),
            pltpu.VMEM((width, tiles, LANES), F32),
            pltpu.VMEM((width, 16, block), BF16),
            pltpu.VMEM((tiles, LANES), F32),
            pltpu.VMEM((2, tiles, LANES), F32),
            pltpu.VMEM((tokens + 8, LANES), F32),
            pltpu.VMEM((tokens + 8, LANES), F32),
            pltpu.VMEM((tokens, LANES), F32),
            pltpu.VMEM((tokens, LANES), F32),
            pltpu.VMEM((tokens, 16), F32),
            pltpu.VMEM((tokens, LANES), F32),
            pltpu.VMEM((tokens, LANES), F32),
            pltpu.VMEM((8, LANES), F32),
            pltpu.VMEM((8, LANES), F32),
            pltpu.VMEM((16, matrix.shape[1]), F32),
            pltpu.VMEM((16, matrix.shape[1]), F32),
            pltpu.VMEM((layers, LANES), F32),
            pltpu.VMEM((layers, LANES), F32),
            pltpu.VMEM((units, 2 * tokens, LANES), F32),
            pltpu.VMEM((units, 2 * tokens, LANES), F32),
            pltpu.VMEM((units, 2 * tokens, LANES), F32),
            pltpu.VMEM((units, tokens, LANES), BF16),
            pltpu.VMEM((units, tokens, LANES), BF16),
            dma((width,)),
            dma((2, pieces)),
            dma((2,)),
            dma((1,)),
        ]
        + [dma((2, lines, pieces))] * 4
        + [
            dma((2, width)),
            dma((2, width)),
            dma((2, lines)),
            dma((2, lines)),
            dma((2, lines)),
            dma((2, lines)),
            dma((2, lines)),
            dma((2, lines)),
            dma((2, 4)),
            dma((2,)),
            dma((2, units)),
            dma((2, units)),
        ],
        compiler_params=pltpu.CompilerParams(
            collective_id=0, has_side_effects=True, vmem_limit_bytes=48 << 20
        ),
        cost_estimate=pl.CostEstimate(flops=10**11, bytes_accessed=30 << 20, transcendentals=0),
        name="fused",
    )(lengths, labels, chosen, rows, earlier, gain, key, value, matrix)


def update_kernel(refusal_ref, column_ref, matrix_ref, flat_ref, caches_ref, *outs):
    ortho_ref, dirs_ref, key_ref, value_ref = outs
    n = pl.program_id(0)
    bands = matrix_ref.shape[0] // LANES
    eye = lax.broadcasted_iota(jnp.int32, (LANES, LANES), 0) == lax.broadcasted_iota(
        jnp.int32, (LANES, LANES), 1
    )
    for b in range(bands):
        row = refusal_ref[pl.ds(n * bands + b, 1), :]
        along = jnp.sum(jnp.where(eye, row, 0.0), axis=1, keepdims=True)
        here = pl.ds(b * LANES, LANES)
        value = matrix_ref[here, :].astype(F32) - along * column_ref[0:1, :]
        ortho_ref[here, :] = value.astype(BF16)
    tiles = dirs_ref.shape[1] // LANES
    for t in range(dirs_ref.shape[0] // 8):
        for k in range(tiles):
            dirs_ref[t * 8 : t * 8 + 8, k * LANES : (k + 1) * LANES] = flat_ref[
                pl.ds((t * tiles + k) * 8, 8), :
            ]
    key_ref[...] = caches_ref[0]
    value_ref[...] = caches_ref[1]


def update(refusal, column, matrix, flat, caches, steps):
    half_width, columns = matrix.shape
    tiles = half_width // LANES
    layers = flat.shape[0] // tiles
    tokens, kept = caches.shape[1:]
    rows = half_width // steps
    groups = next(g for g in range(1, layers // 8 + 1) if layers // 8 % g == 0 and layers // 8 // g <= steps)
    last = layers // 8 // groups - 1
    band = next(b for b in range(16, tokens + 1, 16) if tokens % b == 0 and tokens // b <= steps)
    top = tokens // band - 1
    whole = pl.BlockSpec(memory_space=pltpu.VMEM)
    return pl.pallas_call(
        update_kernel,
        grid=(steps,),
        in_specs=[
            whole,
            whole,
            pl.BlockSpec((rows, columns), lambda n: (n, 0)),
            pl.BlockSpec((groups * 8 * tiles, LANES), lambda n: (jnp.minimum(n, last), 0)),
            pl.BlockSpec((2, band, kept), lambda n: (0, jnp.minimum(n, top), 0)),
        ],
        out_specs=[
            pl.BlockSpec((rows, columns), lambda n: (n, 0)),
            pl.BlockSpec((groups * 8, half_width), lambda n: (jnp.minimum(n, last), 0)),
            pl.BlockSpec((band, kept), lambda n: (jnp.minimum(n, top), 0)),
            pl.BlockSpec((band, kept), lambda n: (jnp.minimum(n, top), 0)),
        ],
        out_shape=[
            jax.ShapeDtypeStruct(matrix.shape, BF16),
            jax.ShapeDtypeStruct((layers, half_width), F32),
            jax.ShapeDtypeStruct((tokens, kept), BF16),
            jax.ShapeDtypeStruct((tokens, kept), BF16),
        ],
        compiler_params=pltpu.CompilerParams(vmem_limit_bytes=24 << 20),
        name="update",
    )(refusal, column, matrix, flat, caches)


def shards(
    residual, lengths, labels, earlier_means, chosen, norm_gain, key_weight, value_weight, out_proj
):
    prompts, length, half_width = residual.shape
    lines = lax.axis_size("dp") // 2
    tiles = half_width // LANES
    earlier = earlier_means[0]
    layers = earlier.shape[0] + 1
    earlier = earlier.reshape(layers - 1, 2, tiles, LANES).transpose(0, 2, 1, 3).reshape(-1, LANES)
    matrix = out_proj[0]
    flat, caches, refusal, column = fused(
        lines, prompts, length, lengths, labels, chosen, residual.reshape(-1, half_width), earlier,
        norm_gain.reshape(tiles, LANES), key_weight[0], value_weight[0], matrix,
    )
    ortho_proj, directions, keys, values = update(refusal, column, matrix, flat, caches, 4)
    keys, values = (x.reshape(prompts, length, -1) for x in (keys, values))
    return (directions, keys, values, ortho_proj[None])


def solution(mesh):
    return jax.shard_map(
        shards,
        mesh=mesh,
        in_specs=(
            P(("groups", "dp"), None, "mp"),
            P(("groups", "dp")),
            P(("groups", "dp")),
            P(("groups", "dp"), None, None, "mp"),
            P("groups"),
            P("mp"),
            P("mp", "dp", None),
            P("mp", "dp", None),
            P("groups", "mp", "dp"),
        ),
        out_specs=(
            P("groups", "mp"),
            P(("groups", "dp"), None, "mp"),
            P(("groups", "dp"), None, "mp"),
            P("groups", "mp", "dp"),
        ),
        check_vma=False,
    )
```

```python
import functools
import math

import jax
import jax.numpy as jnp
from jax import lax
from jax.experimental import pallas as pl
from jax.experimental.pallas import tpu as pltpu
from jax.sharding import PartitionSpec as P

MESH = pl.DeviceIdType.MESH
F32, BF16 = jnp.float32, jnp.bfloat16
LANES = 128


def fused_kernel(
    cfg,
    lengths_ref, labels_ref, chosen_ref, res_ref, earlier_ref, gains_ref, key_ref, value_ref, proj_ref,
    dirs_ref, kv_ref, refusal_ref, column_ref,
    gain_ref, x_ref, swap_ref, wall_ref, normed_ref, matrix_ref, means_ref, diff_ref,
    half_recv, up_send, up_recv, down_send, down_recv, final_ref,
    count_send, count_recv, pick_send, pick_recv, unit_ref, flat_ref, current_ref,
    dots_send, dots_recv, square_send, square_recv, stat_ref, proj_tok, scale_tok, stat_send, stat_recv,
    col_send, col_recv, layer_send, layer_recv,
    away_send, away_recv, kept_ref, side_send, side_recv,
    x_sem, wall_sem, means_sem, matrix_sem,
    hop_send, hop_recv, cross_send, cross_recv,
    count_sems, pick_sems, swap_sems, half_sems, up_sems, down_sems, final_sems, share_sems,
    pair_sems, stat_sems, away_sems, side_sems,
):
    lines, pieces, prompts, length, layers = cfg
    width = 2 * lines
    tokens, half_width = res_ref.shape
    block = half_width // width
    rows = key_ref.shape[0]
    sub = block // LANES
    tiles = half_width // LANES
    pairs = pieces // 2
    model_width = 2 * half_width
    chunk = diff_ref.shape[0] // width
    group, me, core = lax.axis_index("groups"), lax.axis_index("dp"), lax.axis_index("mp")
    place, side = me // 2, lax.rem(me, 2)
    beside = me + 1 - 2 * side
    first = lax.rem(group, 2)
    across = group + 1 - 2 * first
    sibling = {"mp": 1 - core}

    def remote(src, dst, send, recv, device):
        return pltpu.make_async_remote_copy(
            src_ref=src, dst_ref=dst, send_sem=send, recv_sem=recv, device_id=device,
            device_id_type=MESH,
        )

    barrier = pltpu.get_barrier_semaphore()

    @pl.loop(1, width)
    def _(far):
        pl.semaphore_signal(
            barrier, inc=1, device_id={"dp": lax.rem(me + far, width)}, device_id_type=MESH
        )

    pl.semaphore_signal(barrier, inc=1, device_id={"groups": across}, device_id_type=MESH)
    pl.semaphore_signal(barrier, inc=1, device_id=sibling, device_id_type=MESH)

    def each(count, body):
        @pl.loop(0, count)
        def _(n):
            body(n)

    def own_x(j):
        return pltpu.make_async_copy(
            res_ref.at[:, pl.ds(pl.multiple_of(j * block, block), block)], x_ref.at[j], x_sem.at[j]
        )

    each(width, lambda j: own_x(j).start())
    own_means = pltpu.make_async_copy(earlier_ref, means_ref, means_sem.at[0])
    own_means.start()
    own_gains = pltpu.make_async_copy(gains_ref, gain_ref, means_sem.at[1])
    own_gains.start()

    ones = jnp.int32(0)
    for p in range(prompts):
        ones = ones + labels_ref[p]
    line = lax.broadcasted_iota(jnp.int32, (8, LANES), 0)
    harmful = jnp.full((8, LANES), ones.astype(F32))
    harmless = jnp.full((8, LANES), (prompts - ones).astype(F32))
    count_send[...] = jnp.where(line == 0, harmless, harmful)

    pl.semaphore_wait(barrier, width + 1)

    def slot_of(step, way):
        return lax.rem(place - way * step + width * lines, lines)

    def wall_at(slot, pc):
        return wall_ref.at[
            first, pc // 2, lax.rem(pc, 2), pl.ds(pl.multiple_of(slot * rows, rows), rows), :
        ]

    def hop(step, pc, way, source=None):
        k = 0 if way > 0 else 1
        ref = wall_at(slot_of(step - 1, way), pc)
        return remote(
            ref if source is None else source, ref, hop_send.at[k, step, pc], hop_recv.at[k, step, pc],
            {"dp": lax.rem(me + 2 * way + width, width)},
        )

    def arrival(step, pc, way):
        k = 0 if way > 0 else 1
        ref = wall_at(slot_of(step, way), pc)
        return remote(
            ref, ref, hop_send.at[k, step, pc], hop_recv.at[k, step, pc],
            {"dp": lax.rem(me - 2 * way + width, width)},
        )

    def cross(step, pc, way):
        k = 0 if way > 0 else 1
        ref = wall_at(slot_of(step, way), pc)
        return remote(
            ref, ref, cross_send.at[k, step, pc], cross_recv.at[k, step, pc], {"groups": across}
        )

    def crossed(step, pc, way):
        k = 0 if way > 0 else 1
        ref = wall_ref.at[
            1 - first, pc // 2, lax.rem(pc, 2),
            pl.ds(pl.multiple_of(slot_of(step, way) * rows, rows), rows), :,
        ]
        return remote(
            ref, ref, cross_send.at[k, step, pc], cross_recv.at[k, step, pc], {"groups": across}
        )

    def sends(step, way):
        return (place >= step - 1) & (place < lines - 1) if way > 0 else (
            (place > 0) & (place <= lines - step)
        )

    def holds(step, way):
        return place >= step if way > 0 else place < lines - step

    def piece_of(ref, pc):
        column = (lax.rem(pc, 2) * pairs + pc // 2) * LANES
        return ref.at[:, pl.ds(pl.multiple_of(column, LANES), LANES)]

    def start_own(pc):
        for way in (1, -1):
            for m, ref in enumerate((key_ref, value_ref)):

                @pl.when(sends(1, way) & (first == m))
                def _():
                    hop(1, pc, way, piece_of(ref, pc)).start()

    window = 1
    ticks = pieces + lines - 2
    each(window, start_own)

    def service(step, pc):
        for way in (1, -1):

            @pl.when(holds(step, way))
            def _():
                arrival(step, pc, way).wait_recv()

                @pl.when(sends(step + 1, way) & (step < lines - 1))
                def _():
                    hop(step + 1, pc, way).start()

                cross(step, pc, way).start()

    def tick(t):
        @pl.when(t + window < pieces)
        def _():
            start_own(t + window)

        @pl.loop(jnp.maximum(1, t - pieces + 2), jnp.minimum(lines, t + 2))
        def _(step):
            service(step, t - step + 1)

    def swap(zz):
        j = 2 * zz + 1 - side
        return remote(
            res_ref.at[:, pl.ds(pl.multiple_of(j * block, block), block)], swap_ref.at[zz],
            swap_sems.at[0, zz], swap_sems.at[1, zz], {"dp": beside},
        )

    early = max(lines // 4, 1)
    each(early, lambda zz: swap(zz).start())

    def spread(send_ref, recv_ref, sems, far):
        return remote(
            send_ref, recv_ref.at[me], sems.at[0, far], sems.at[1, far],
            {"dp": lax.rem(me + far, width)},
        )

    @pl.loop(1, width)
    def _(far):
        spread(count_send, count_recv, count_sems, far).start()

    count_recv[me] = count_send[...]

    def own_wall(m, pc):
        ref = (key_ref, value_ref)[m]
        return pltpu.make_async_copy(
            piece_of(ref, pc),
            wall_ref.at[
                m, pc // 2, lax.rem(pc, 2), pl.ds(pl.multiple_of(place * rows, rows), rows), :
            ],
            wall_sem.at[m, pc],
        )

    each(width, lambda j: own_x(j).wait())
    own_matrix = pltpu.make_async_copy(proj_ref, matrix_ref, matrix_sem.at[0])
    own_matrix.start()
    for m in range(2):
        each(pieces, lambda pc: own_wall(m, pc).start())

    tick(0)

    row_id = lax.broadcasted_iota(jnp.int32, (16, tokens), 0)
    token_id = lax.broadcasted_iota(jnp.int32, (16, tokens), 1)
    mask = jnp.zeros((16, tokens), F32)
    for p in range(prompts):
        inside = (token_id >= p * length) & (token_id < p * length + lengths_ref[p])
        mask = jnp.where(inside & (row_id == p), 1.0, mask)
    mask = mask.astype(BF16)

    def class_sums(j):
        sums = jnp.dot(mask, x_ref[j], preferred_element_type=F32)
        current = [jnp.zeros((1, block), F32), jnp.zeros((1, block), F32)]
        for p in range(prompts):
            mean = sums[p : p + 1, :] / jnp.full((1, block), lengths_ref[p].astype(F32))
            label = labels_ref[p].astype(F32)
            current[1] = current[1] + mean * label
            current[0] = current[0] + mean * (1.0 - label)
        current[0] = current[0] / jnp.full((1, block), (prompts - ones).astype(F32))
        current[1] = current[1] / jnp.full((1, block), ones.astype(F32))
        for c in range(2):
            for q in range(sub):
                current_ref[c, pl.ds(j * sub + q, 1), :] = current[c][:, q * LANES : (q + 1) * LANES]

    each(width, class_sums)

    @pl.loop(1, width)
    def _(far):
        spread(count_send, count_recv, count_sems, far).wait_recv()

    totals = count_recv[0]
    for j in range(1, width):
        totals = totals + count_recv[j]
    share = count_send[...] / totals
    share0, share1 = share[0:1, :], share[1:2, :]

    own_means.wait()
    own_gains.wait()
    current_diff = share1 * current_ref[1] - share0 * current_ref[0]
    at = jnp.minimum(chosen_ref[0], layers - 2) * (2 * tiles)
    picked = share1 * means_ref[pl.ds(at + 1, tiles, stride=2), :] - share0 * means_ref[
        pl.ds(at, tiles, stride=2), :
    ]
    pick_send[...] = jnp.where(chosen_ref[0] == layers - 1, current_diff, picked)

    @pl.loop(1, width)
    def _(far):
        spread(pick_send, pick_recv, pick_sems, far).start()

    pick_recv[me] = pick_send[...]

    @pl.loop(0, layers - 1)
    def _(l):
        e = l * (2 * tiles)
        d = share1 * means_ref[pl.ds(e + 1, tiles, stride=2), :] - share0 * means_ref[
            pl.ds(e, tiles, stride=2), :
        ]
        diff_ref[pl.ds((l // 8) * (8 * tiles) + lax.rem(l, 8), tiles, stride=8), :] = d

    diff_ref[pl.ds(((layers - 1) // 8) * (8 * tiles) + (layers - 1) % 8, tiles, stride=8), :] = (
        current_diff
    )

    def part(ref, j):
        return ref.at[pl.ds(pl.multiple_of(j * chunk, 16), chunk), :]

    def read(ref, j):
        return ref[pl.ds(pl.multiple_of(j * chunk, 16), chunk), :]

    def half(zz):
        return remote(
            part(diff_ref, 2 * zz + 1 - side), half_recv.at[zz], half_sems.at[0, zz],
            half_sems.at[1, zz], {"dp": beside},
        )

    each(lines, lambda zz: half(zz).start())
    each(lines - early, lambda zz: swap(zz + early).start())

    tick(1)
    tick(2)


    @pl.loop(1, width)
    def _(far):
        spread(pick_send, pick_recv, pick_sems, far).wait_recv()

    picked = pick_recv[0]
    for j in range(1, width):
        picked = picked + pick_recv[j]
    local_square = jnp.sum(jnp.sum(picked * picked, axis=1, keepdims=True), axis=0, keepdims=True)
    unit = picked * lax.rsqrt(local_square / half_width + 1e-06)
    flat_ref[...] = picked
    high = unit.astype(BF16).astype(F32)
    middle = (unit - high).astype(BF16).astype(F32)
    low = unit - high - middle
    line16 = lax.broadcasted_iota(jnp.int32, (16, LANES), 0)
    for k in range(tiles):
        spot = jnp.where(
            line16 == 0, high[k : k + 1, :],
            jnp.where(line16 == 1, middle[k : k + 1, :], jnp.where(line16 == 2, low[k : k + 1, :], 0.0)),
        )
        unit_ref[k // sub, :, (k % sub) * LANES : (k % sub + 1) * LANES] = spot.astype(BF16)

    stat_ref[...] = jnp.zeros_like(stat_ref)

    def token_dots(j):
        stat_ref[...] += lax.dot_general(
            x_ref[j], unit_ref[j], (((1,), (1,)), ((), ())), preferred_element_type=F32
        )

    each(width, token_dots)
    dots = jnp.sum(stat_ref[...], axis=1, keepdims=True)
    dots_send[pl.ds(0, tokens), :] = jnp.broadcast_to(dots, (tokens, LANES))
    dots_send[pl.ds(tokens, 8), :] = jnp.broadcast_to(local_square, (8, LANES))
    dots_copy = remote(dots_send, dots_recv, pair_sems.at[0, 0], pair_sems.at[1, 0], sibling)
    dots_copy.start()

    own_matrix.wait()
    col_send[...] = jnp.zeros_like(col_send)

    def column_dots(j):
        col_send[...] += jnp.dot(
            unit_ref[j], matrix_ref[pl.ds(pl.multiple_of(j * block, block), block), :],
            preferred_element_type=F32,
        )

    each(width, column_dots)
    col_copy = remote(col_send, col_recv, pair_sems.at[0, 1], pair_sems.at[1, 1], sibling)
    col_copy.start()


    tick(3)

    dots_copy.wait_recv()
    root = math.sqrt(model_width)
    other_square = dots_recv[pl.ds(tokens, 1), 0:1]
    mean_dir = (local_square + other_square) / model_width + 1e-06
    ratio_mine = jnp.sqrt((local_square / half_width + 1e-06) / mean_dir) / root
    ratio_other = jnp.sqrt((other_square / half_width + 1e-06) / mean_dir) / root
    flat = flat_ref[...] * (lax.rsqrt(mean_dir) / root)
    refusal_ref[...] = flat
    proj_tok[...] = dots_send[pl.ds(0, tokens), :] * ratio_mine + dots_recv[pl.ds(0, tokens), :] * (
        ratio_other
    )

    def square_rows(n):
        here = pl.ds(pl.multiple_of(n * 16, 16), 16)
        amount = proj_tok[here, :]
        total = jnp.zeros((16, LANES), F32)
        for j in range(width):
            for q in range(sub):
                k = j * sub + q
                left = x_ref[j, here, q * LANES : (q + 1) * LANES].astype(F32)
                left = left - amount * refusal_ref[k : k + 1, :]
                total = total + left * left
        square_send[here, :] = total

    each(tokens // 16, square_rows)
    square_copy = remote(square_send, square_recv, pair_sems.at[0, 2], pair_sems.at[1, 2], sibling)
    square_copy.start()

    def up(zz):
        return remote(
            up_send.at[zz], up_recv.at[zz], up_sems.at[0, zz], up_sems.at[1, zz],
            {"dp": lax.rem(me + 2, width)},
        )

    def down(zz):
        return remote(
            down_send.at[zz], down_recv.at[zz], down_sems.at[0, zz], down_sems.at[1, zz],
            {"dp": lax.rem(me - 2 + width, width)},
        )

    def chain_up(n):
        zz = lines - 1 - n

        @pl.when(zz > place)
        def _():
            up_send[zz] = read(diff_ref, 2 * zz + side) + half_recv[zz]

            @pl.when(place > 0)
            def _():
                up(zz).wait_recv()
                up_send[zz] += up_recv[zz]

            up(zz).start()

    def chain_down(zz):
        @pl.when(zz < place)
        def _():
            down_send[zz] = read(diff_ref, 2 * zz + side) + half_recv[zz]

            @pl.when(place < lines - 1)
            def _():
                down(zz).wait_recv()
                down_send[zz] += down_recv[zz]

            down(zz).start()

    each(lines, lambda zz: half(zz).wait_recv())

    @pl.when(place == 0)
    def _():
        each(lines, chain_up)

    @pl.when(place == lines - 1)
    def _():
        each(lines, chain_down)

    @pl.loop(4, lines + 1)
    def _(t):
        tick(t)

    col_copy.wait_recv()
    column = col_send[...] * ratio_mine + col_recv[...] * ratio_other
    column_ref[...] = jnp.broadcast_to(jnp.sum(column, axis=0, keepdims=True), column_ref.shape)

    square_copy.wait_recv()
    mean_square = jnp.sum(square_send[...] + square_recv[...], axis=1, keepdims=True) / model_width
    scale_tok[...] = jnp.broadcast_to(lax.rsqrt(mean_square + 1e-05), (tokens, LANES))

    eye = lax.broadcasted_iota(jnp.int32, (LANES, LANES), 0) == lax.broadcasted_iota(
        jnp.int32, (LANES, LANES), 1
    )
    bands = tokens // LANES
    for b in range(bands):
        here = pl.ds(b * LANES, LANES)
        for s, ref in enumerate((proj_tok, scale_tok)):
            stat_send[pl.ds(s * bands + b, 1), :] = jnp.sum(
                jnp.where(eye, ref[here, :], 0.0), axis=0, keepdims=True
            )
    stat_copy = remote(stat_send, stat_recv, stat_sems.at[0], stat_sems.at[1], {"dp": beside})
    stat_copy.start()

    def normed_rows(base, n, load, proj_at, scale_at):
        here = pl.ds(pl.multiple_of(n * 16, 16), 16)
        amount, scale = proj_at[here, :], scale_at[here, :]
        out = pl.ds(pl.multiple_of(base + n * 16, 16), 16)
        for zz in range(lines):
            j = 2 * zz + side
            vectors = refusal_ref[pl.ds(j * sub, sub), :]
            gains = gain_ref[pl.ds(j * sub, sub), :]
            for q in range(sub):
                value = load(zz, here, pl.ds(q * LANES, LANES)).astype(F32)
                value = (value - amount * vectors[q : q + 1, :]) * scale * gains[q : q + 1, :]
                normed_ref[out, pl.ds(zz * block + q * LANES, LANES)] = value.astype(BF16)

    each(
        tokens // 16,
        lambda n: normed_rows(0, n, lambda zz, a, b: x_ref[2 * zz + side, a, b], proj_tok, scale_tok),
    )

    @pl.when((place > 0) & (place < lines - 1))
    def _():
        each(lines, chain_up)
        each(lines, chain_down)

    def gathered(far):
        ref = part(final_ref, me)
        return remote(
            ref, ref, final_sems.at[0, far], final_sems.at[1, far],
            {"dp": 2 * lax.rem(place + far, lines) + side},
        )

    def gathered_from(far):
        ref = part(final_ref, 2 * lax.rem(place - far + lines, lines) + side)
        return remote(ref, ref, final_sems.at[0, far], final_sems.at[1, far], {"dp": beside})

    def shared(zz):
        ref = part(final_ref, 2 * zz + side)
        return remote(ref, ref, share_sems.at[0, zz], share_sems.at[1, zz], {"dp": beside})

    def shared_from(zz):
        ref = part(final_ref, 2 * zz + 1 - side)
        return remote(ref, ref, share_sems.at[0, zz], share_sems.at[1, zz], {"dp": beside})

    tick(lines + 1)

    stat_copy.wait_recv()
    for b in range(bands):
        here = pl.ds(b * LANES, LANES)
        for s, ref in enumerate((proj_tok, scale_tok)):
            value = jnp.where(eye, stat_recv[pl.ds(s * bands + b, 1), :], 0.0)
            ref[here, :] = jnp.broadcast_to(jnp.sum(value, axis=1, keepdims=True), (LANES, LANES))
    each(lines, lambda zz: swap(zz).wait_recv())
    each(
        tokens // 16,
        lambda n: normed_rows(tokens, n, lambda zz, a, b: swap_ref[zz, a, b], proj_tok, scale_tok),
    )

    def away(u):
        return remote(
            away_send.at[u], away_recv.at[u], away_sems.at[0, u], away_sems.at[1, u], sibling
        )

    def beyond(u):
        return remote(
            side_send.at[u], side_recv.at[u], side_sems.at[0, u], side_sems.at[1, u], {"dp": beside}
        )

    units = 2 * pairs

    def product(u):
        i, odd = u // 2, lax.rem(u, 2)
        which = lax.rem(first + odd, 2)

        @pl.when(odd == 1)
        def _():
            for way in (1, -1):

                @pl.loop(1, lines)
                def _(step):
                    @pl.when(holds(step, way))
                    def _():
                        each(2, lambda h: crossed(step, 2 * i + h, way).wait_recv())

        away_send[u] = jnp.dot(
            normed_ref[...], wall_ref[which, i, 1 - core], preferred_element_type=F32
        )
        away(u).start()
        kept_ref[u] = jnp.dot(normed_ref[...], wall_ref[which, i, core], preferred_element_type=F32)

    def reduce_pair(u):
        away(u).wait_recv()
        side_send[u] = (
            kept_ref[u, pl.ds(tokens, tokens), :] + away_recv[u, pl.ds(tokens, tokens), :]
        ).astype(BF16)
        beyond(u).start()

    def reduce_side(u):
        i, odd = u // 2, lax.rem(u, 2)
        which = lax.rem(first + odd, 2)
        beyond(u).wait_recv()
        total = kept_ref[u, pl.ds(0, tokens), :] + away_recv[u, pl.ds(0, tokens), :]
        total = total + side_recv[u].astype(F32)
        kv_ref[which, :, pl.ds(pl.multiple_of(i * LANES, LANES), LANES)] = total.astype(BF16)

    for m in range(2):
        each(pieces, lambda pc: own_wall(m, pc).wait())

    @pl.loop(0, pairs)
    def _(i):
        product(2 * i)

        @pl.loop(jnp.where(i < pairs - 1, lines + 2 + i, ticks), jnp.where(i < pairs - 2, lines + 3 + i, ticks))
        def _(t):
            tick(t)

        @pl.when(i == pairs - 1)
        def _():
            @pl.loop(1, lines)
            def _(far):
                gathered_from(far).wait_recv()
                shared(lax.rem(place - far + lines, lines)).start()

        reduce_pair(2 * i)
        product(2 * i + 1)
        reduce_pair(2 * i + 1)

        @pl.when(i > 0)
        def _():
            each(2, lambda odd: reduce_side(2 * i - 2 + odd))

        @pl.when(i == pairs - 3)
        def _():
            down_send[place] = read(diff_ref, me) + half_recv[place]

            @pl.when(place > 0)
            def _():
                up(place).wait_recv()
                down_send[place] += up_recv[place]

            @pl.when(place < lines - 1)
            def _():
                down(place).wait_recv()
                down_send[place] += down_recv[place]

            final_ref[pl.ds(pl.multiple_of(me * chunk, 16), chunk), :] = down_send[place].astype(BF16)

            @pl.loop(1, lines)
            def _(far):
                gathered(far).start()

            shared(place).start()


    def finish_layers():
        each(lines, lambda zz: shared_from(zz).wait_recv())

        @pl.loop(0, layers // 8)
        def _(t):
            total = jnp.zeros((8, LANES), F32)
            for k in range(0, tiles, 2):
                rows16 = pl.ds(pl.multiple_of(t * (8 * tiles) + k * 8, 16), 16)
                value = final_ref[rows16, :].astype(F32)
                total = total + value[0:8] * value[0:8] + value[8:16] * value[8:16]
            layer_send[pl.ds(pl.multiple_of(t * 8, 8), 8), :] = total

        remote(
            layer_send, layer_recv, pair_sems.at[0, 3], pair_sems.at[1, 3], sibling
        ).start()

    finish_layers()
    layer_copy = remote(layer_send, layer_recv, pair_sems.at[0, 3], pair_sems.at[1, 3], sibling)
    layer_copy.wait_recv()

    @pl.loop(0, layers // 8)
    def _(t):
        here = pl.ds(pl.multiple_of(t * 8, 8), 8)
        mean = jnp.sum(layer_send[here, :] + layer_recv[here, :], axis=1, keepdims=True) / model_width
        norm = jnp.broadcast_to(lax.rsqrt(mean + 1e-06), (8, LANES))
        norm = jnp.concatenate([norm, norm], axis=0)
        for k in range(0, tiles, 2):
            rows16 = pl.ds(pl.multiple_of(t * (8 * tiles) + k * 8, 16), 16)
            dirs_ref[rows16, :] = final_ref[rows16, :].astype(F32) * norm

    reduce_side(units - 2)
    reduce_side(units - 1)

    @pl.loop(1, width)
    def _(far):
        spread(count_send, count_recv, count_sems, far).wait_send()
        spread(pick_send, pick_recv, pick_sems, far).wait_send()

    @pl.loop(1, lines)
    def _(far):
        gathered(far).wait_send()

    def drain(zz):
        swap(zz).wait_send()
        half(zz).wait_send()
        shared(zz).wait_send()

        @pl.when(zz > place)
        def _():
            up(zz).wait_send()

        @pl.when(zz < place)
        def _():
            down(zz).wait_send()

    each(lines, drain)
    dots_copy.wait_send()
    col_copy.wait_send()
    square_copy.wait_send()
    layer_copy.wait_send()
    stat_copy.wait_send()

    def drain_unit(u):
        away(u).wait_send()
        beyond(u).wait_send()

    each(units, drain_unit)

    @pl.loop(1, lines)
    def _(step):
        def drain_piece(pc):
            for way in (1, -1):

                @pl.when(sends(step, way))
                def _():
                    hop(step, pc, way).wait_send()

                @pl.when(holds(step, way))
                def _():
                    cross(step, pc, way).wait_send()

        each(pieces, drain_piece)


def fused(lines, prompts, length, lengths, labels, chosen, rows, earlier, gain, key, value, matrix):
    tokens, half_width = rows.shape
    width = 2 * lines
    block = half_width // width
    tiles = half_width // LANES
    layers = earlier.shape[0] // (2 * tiles) + 1
    columns = key.shape[1]
    pieces = columns // LANES
    pairs = pieces // 2
    units = 2 * pairs
    flat_rows = layers * tiles
    chunk = flat_rows // width
    smem = pl.BlockSpec(memory_space=pltpu.SMEM)
    vmem = pl.BlockSpec(memory_space=pltpu.VMEM)
    hbm = pl.BlockSpec(memory_space=pltpu.HBM)
    dma = pltpu.SemaphoreType.DMA
    return pl.pallas_call(
        functools.partial(fused_kernel, (lines, pieces, prompts, length, layers)),
        out_shape=(
            jax.ShapeDtypeStruct((flat_rows, LANES), F32),
            jax.ShapeDtypeStruct((2, tokens, columns // 2), BF16),
            jax.ShapeDtypeStruct((tiles, LANES), F32),
            jax.ShapeDtypeStruct((8, matrix.shape[1]), F32),
        ),
        in_specs=[smem, smem, smem, hbm, hbm, hbm, hbm, hbm, hbm],
        out_specs=[vmem] * 4,
        scratch_shapes=[
            pltpu.VMEM((tiles, LANES), F32),
            pltpu.VMEM((width, tokens, block), BF16),
            pltpu.VMEM((lines, tokens, block), BF16),
            pltpu.VMEM((2, pairs, 2, lines * key.shape[0], LANES), BF16),
            pltpu.VMEM((2 * tokens, half_width // 2), BF16),
            pltpu.VMEM(matrix.shape, BF16),
            pltpu.VMEM(earlier.shape, F32),
            pltpu.VMEM((flat_rows, LANES), F32),
        ]
        + [pltpu.VMEM((lines, chunk, LANES), F32)] * 5
        + [
            pltpu.VMEM((flat_rows, LANES), BF16),
            pltpu.VMEM((8, LANES), F32),
            pltpu.VMEM((width, 8, LANES), F32),
            pltpu.VMEM((tiles, LANES), F32),
            pltpu.VMEM((width, tiles, LANES), F32),
            pltpu.VMEM((width, 16, block), BF16),
            pltpu.VMEM((tiles, LANES), F32),
            pltpu.VMEM((2, tiles, LANES), F32),
            pltpu.VMEM((tokens + 8, LANES), F32),
            pltpu.VMEM((tokens + 8, LANES), F32),
            pltpu.VMEM((tokens, LANES), F32),
            pltpu.VMEM((tokens, LANES), F32),
            pltpu.VMEM((tokens, 16), F32),
            pltpu.VMEM((tokens, LANES), F32),
            pltpu.VMEM((tokens, LANES), F32),
            pltpu.VMEM((8, LANES), F32),
            pltpu.VMEM((8, LANES), F32),
            pltpu.VMEM((16, matrix.shape[1]), F32),
            pltpu.VMEM((16, matrix.shape[1]), F32),
            pltpu.VMEM((layers, LANES), F32),
            pltpu.VMEM((layers, LANES), F32),
            pltpu.VMEM((units, 2 * tokens, LANES), F32),
            pltpu.VMEM((units, 2 * tokens, LANES), F32),
            pltpu.VMEM((units, 2 * tokens, LANES), F32),
            pltpu.VMEM((units, tokens, LANES), BF16),
            pltpu.VMEM((units, tokens, LANES), BF16),
            dma((width,)),
            dma((2, pieces)),
            dma((2,)),
            dma((1,)),
        ]
        + [dma((2, lines, pieces))] * 4
        + [
            dma((2, width)),
            dma((2, width)),
            dma((2, lines)),
            dma((2, lines)),
            dma((2, lines)),
            dma((2, lines)),
            dma((2, lines)),
            dma((2, lines)),
            dma((2, 4)),
            dma((2,)),
            dma((2, units)),
            dma((2, units)),
        ],
        compiler_params=pltpu.CompilerParams(
            collective_id=0, has_side_effects=True, vmem_limit_bytes=60 << 20
        ),
        cost_estimate=pl.CostEstimate(flops=10**11, bytes_accessed=30 << 20, transcendentals=0),
        name="fused",
    )(lengths, labels, chosen, rows, earlier, gain, key, value, matrix)


def update_kernel(refusal_ref, column_ref, matrix_ref, flat_ref, caches_ref, *outs):
    ortho_ref, dirs_ref, key_ref, value_ref = outs
    n = pl.program_id(0)
    bands = matrix_ref.shape[0] // LANES
    eye = lax.broadcasted_iota(jnp.int32, (LANES, LANES), 0) == lax.broadcasted_iota(
        jnp.int32, (LANES, LANES), 1
    )
    for b in range(bands):
        row = refusal_ref[pl.ds(n * bands + b, 1), :]
        along = jnp.sum(jnp.where(eye, row, 0.0), axis=1, keepdims=True)
        here = pl.ds(b * LANES, LANES)
        value = matrix_ref[here, :].astype(F32) - along * column_ref[0:1, :]
        ortho_ref[here, :] = value.astype(BF16)
    tiles = dirs_ref.shape[1] // LANES
    for t in range(dirs_ref.shape[0] // 8):
        for k in range(tiles):
            dirs_ref[t * 8 : t * 8 + 8, k * LANES : (k + 1) * LANES] = flat_ref[
                pl.ds((t * tiles + k) * 8, 8), :
            ]
    key_ref[...] = caches_ref[0]
    value_ref[...] = caches_ref[1]


def update(refusal, column, matrix, flat, caches, steps):
    half_width, columns = matrix.shape
    tiles = half_width // LANES
    layers = flat.shape[0] // tiles
    tokens, kept = caches.shape[1:]
    rows = half_width // steps
    groups = next(g for g in range(1, layers // 8 + 1) if layers // 8 % g == 0 and layers // 8 // g <= steps)
    last = layers // 8 // groups - 1
    band = next(b for b in range(16, tokens + 1, 16) if tokens % b == 0 and tokens // b <= steps)
    top = tokens // band - 1
    whole = pl.BlockSpec(memory_space=pltpu.VMEM)
    return pl.pallas_call(
        update_kernel,
        grid=(steps,),
        in_specs=[
            whole,
            whole,
            pl.BlockSpec((rows, columns), lambda n: (n, 0)),
            pl.BlockSpec((groups * 8 * tiles, LANES), lambda n: (jnp.minimum(n, last), 0)),
            pl.BlockSpec((2, band, kept), lambda n: (0, jnp.minimum(n, top), 0)),
        ],
        out_specs=[
            pl.BlockSpec((rows, columns), lambda n: (n, 0)),
            pl.BlockSpec((groups * 8, half_width), lambda n: (jnp.minimum(n, last), 0)),
            pl.BlockSpec((band, kept), lambda n: (jnp.minimum(n, top), 0)),
            pl.BlockSpec((band, kept), lambda n: (jnp.minimum(n, top), 0)),
        ],
        out_shape=[
            jax.ShapeDtypeStruct(matrix.shape, BF16),
            jax.ShapeDtypeStruct((layers, half_width), F32),
            jax.ShapeDtypeStruct((tokens, kept), BF16),
            jax.ShapeDtypeStruct((tokens, kept), BF16),
        ],
        compiler_params=pltpu.CompilerParams(vmem_limit_bytes=60 << 20),
        name="update",
    )(refusal, column, matrix, flat, caches)


def shards(
    residual, lengths, labels, earlier_means, chosen, norm_gain, key_weight, value_weight, out_proj
):
    prompts, length, half_width = residual.shape
    lines = lax.axis_size("dp") // 2
    tiles = half_width // LANES
    earlier = earlier_means[0]
    layers = earlier.shape[0] + 1
    earlier = earlier.reshape(layers - 1, 2, tiles, LANES).transpose(0, 2, 1, 3).reshape(-1, LANES)
    matrix = out_proj[0]
    flat, caches, refusal, column = fused(
        lines, prompts, length, lengths, labels, chosen, residual.reshape(-1, half_width), earlier,
        norm_gain.reshape(tiles, LANES), key_weight[0], value_weight[0], matrix,
    )
    ortho_proj, directions, keys, values = update(refusal, column, matrix, flat, caches, 2)
    keys, values = (x.reshape(prompts, length, -1) for x in (keys, values))
    return (directions, keys, values, ortho_proj[None])


def solution(mesh):
    return jax.shard_map(
        shards,
        mesh=mesh,
        in_specs=(
            P(("groups", "dp"), None, "mp"),
            P(("groups", "dp")),
            P(("groups", "dp")),
            P(("groups", "dp"), None, None, "mp"),
            P("groups"),
            P("mp"),
            P("mp", "dp", None),
            P("mp", "dp", None),
            P("groups", "mp", "dp"),
        ),
        out_specs=(
            P("groups", "mp"),
            P(("groups", "dp"), None, "mp"),
            P(("groups", "dp"), None, "mp"),
            P("groups", "mp", "dp"),
        ),
        check_vma=False,
    )
```

```python
import functools
import math

import jax
import jax.numpy as jnp
from jax import lax
from jax.experimental import pallas as pl
from jax.experimental.pallas import tpu as pltpu
from jax.sharding import PartitionSpec as P

MESH = pl.DeviceIdType.MESH
F32, BF16 = jnp.float32, jnp.bfloat16
LANES = 128


def fused_kernel(
    cfg,
    lengths_ref, labels_ref, chosen_ref, res_ref, earlier_ref, gains_ref, key_ref, value_ref, proj_ref,
    dirs_ref, kv_ref, refusal_ref, column_ref,
    gain_ref, x_ref, swap_ref, wall_ref, normed_ref, matrix_ref, means_ref, diff_ref,
    half_recv, up_send, up_recv, down_send, down_recv, final_ref,
    count_send, count_recv, pick_send, pick_recv, unit_ref, flat_ref, current_ref,
    dots_send, dots_recv, square_send, square_recv, stat_ref, proj_tok, scale_tok, stat_send, stat_recv,
    col_send, col_recv, layer_send, layer_recv,
    away_send, away_recv, kept_ref, side_send, side_recv,
    x_sem, wall_sem, means_sem, matrix_sem,
    hop_send, hop_recv, cross_send, cross_recv,
    count_sems, pick_sems, swap_sems, half_sems, up_sems, down_sems, final_sems, share_sems,
    pair_sems, stat_sems, away_sems, side_sems,
):
    lines, pieces, prompts, length, layers = cfg
    width = 2 * lines
    tokens, half_width = res_ref.shape
    block = half_width // width
    rows = key_ref.shape[0]
    sub = block // LANES
    tiles = half_width // LANES
    pairs = pieces // 2
    model_width = 2 * half_width
    chunk = diff_ref.shape[0] // width
    group, me, core = lax.axis_index("groups"), lax.axis_index("dp"), lax.axis_index("mp")
    place, side = me // 2, lax.rem(me, 2)
    beside = me + 1 - 2 * side
    first = lax.rem(group, 2)
    across = group + 1 - 2 * first
    sibling = {"mp": 1 - core}

    def remote(src, dst, send, recv, device):
        return pltpu.make_async_remote_copy(
            src_ref=src, dst_ref=dst, send_sem=send, recv_sem=recv, device_id=device,
            device_id_type=MESH,
        )

    barrier = pltpu.get_barrier_semaphore()

    @pl.loop(1, width)
    def _(far):
        pl.semaphore_signal(
            barrier, inc=1, device_id={"dp": lax.rem(me + far, width)}, device_id_type=MESH
        )

    pl.semaphore_signal(barrier, inc=1, device_id={"groups": across}, device_id_type=MESH)
    pl.semaphore_signal(barrier, inc=1, device_id=sibling, device_id_type=MESH)

    def each(count, body):
        @pl.loop(0, count)
        def _(n):
            body(n)

    def own_x(j):
        return pltpu.make_async_copy(
            res_ref.at[:, pl.ds(pl.multiple_of(j * block, block), block)], x_ref.at[j], x_sem.at[j]
        )

    each(width, lambda j: own_x(j).start())
    own_means = pltpu.make_async_copy(earlier_ref, means_ref, means_sem.at[0])
    own_means.start()
    own_gains = pltpu.make_async_copy(gains_ref, gain_ref, means_sem.at[1])
    own_gains.start()

    ones = jnp.int32(0)
    for p in range(prompts):
        ones = ones + labels_ref[p]
    line = lax.broadcasted_iota(jnp.int32, (8, LANES), 0)
    harmful = jnp.full((8, LANES), ones.astype(F32))
    harmless = jnp.full((8, LANES), (prompts - ones).astype(F32))
    count_send[...] = jnp.where(line == 0, harmless, harmful)

    pl.semaphore_wait(barrier, width + 1)

    def slot_of(step, way):
        return lax.rem(place - way * step + width * lines, lines)

    def wall_at(slot, pc):
        return wall_ref.at[
            first, pc // 2, lax.rem(pc, 2), pl.ds(pl.multiple_of(slot * rows, rows), rows), :
        ]

    def hop(step, pc, way, source=None):
        k = 0 if way > 0 else 1
        ref = wall_at(slot_of(step - 1, way), pc)
        return remote(
            ref if source is None else source, ref, hop_send.at[k, step, pc], hop_recv.at[k, step, pc],
            {"dp": lax.rem(me + 2 * way + width, width)},
        )

    def arrival(step, pc, way):
        k = 0 if way > 0 else 1
        ref = wall_at(slot_of(step, way), pc)
        return remote(
            ref, ref, hop_send.at[k, step, pc], hop_recv.at[k, step, pc],
            {"dp": lax.rem(me - 2 * way + width, width)},
        )

    def cross(step, pc, way):
        k = 0 if way > 0 else 1
        ref = wall_at(slot_of(step, way), pc)
        return remote(
            ref, ref, cross_send.at[k, step, pc], cross_recv.at[k, step, pc], {"groups": across}
        )

    def crossed(step, pc, way):
        k = 0 if way > 0 else 1
        ref = wall_ref.at[
            1 - first, pc // 2, lax.rem(pc, 2),
            pl.ds(pl.multiple_of(slot_of(step, way) * rows, rows), rows), :,
        ]
        return remote(
            ref, ref, cross_send.at[k, step, pc], cross_recv.at[k, step, pc], {"groups": across}
        )

    def sends(step, way):
        return (place >= step - 1) & (place < lines - 1) if way > 0 else (
            (place > 0) & (place <= lines - step)
        )

    def holds(step, way):
        return place >= step if way > 0 else place < lines - step

    def piece_of(ref, pc):
        column = (lax.rem(pc, 2) * pairs + pc // 2) * LANES
        return ref.at[:, pl.ds(pl.multiple_of(column, LANES), LANES)]

    def start_own(pc):
        for way in (1, -1):
            for m, ref in enumerate((key_ref, value_ref)):

                @pl.when(sends(1, way) & (first == m))
                def _():
                    hop(1, pc, way, piece_of(ref, pc)).start()

    window = 1
    ticks = pieces + lines - 2
    each(window, start_own)

    def service(step, pc):
        for way in (1, -1):

            @pl.when(holds(step, way))
            def _():
                arrival(step, pc, way).wait_recv()

                @pl.when(sends(step + 1, way) & (step < lines - 1))
                def _():
                    hop(step + 1, pc, way).start()

                cross(step, pc, way).start()

    def tick(t):
        @pl.when(t + window < pieces)
        def _():
            start_own(t + window)

        @pl.loop(jnp.maximum(1, t - pieces + 2), jnp.minimum(lines, t + 2))
        def _(step):
            service(step, t - step + 1)

    def swap(zz):
        j = 2 * zz + 1 - side
        return remote(
            res_ref.at[:, pl.ds(pl.multiple_of(j * block, block), block)], swap_ref.at[zz],
            swap_sems.at[0, zz], swap_sems.at[1, zz], {"dp": beside},
        )

    early = max(lines // 4, 1)
    each(early, lambda zz: swap(zz).start())

    def spread(send_ref, recv_ref, sems, far):
        return remote(
            send_ref, recv_ref.at[me], sems.at[0, far], sems.at[1, far],
            {"dp": lax.rem(me + far, width)},
        )

    @pl.loop(1, width)
    def _(far):
        spread(count_send, count_recv, count_sems, far).start()

    count_recv[me] = count_send[...]

    def own_wall(m, pc):
        ref = (key_ref, value_ref)[m]
        return pltpu.make_async_copy(
            piece_of(ref, pc),
            wall_ref.at[
                m, pc // 2, lax.rem(pc, 2), pl.ds(pl.multiple_of(place * rows, rows), rows), :
            ],
            wall_sem.at[m, pc],
        )

    each(width, lambda j: own_x(j).wait())
    own_matrix = pltpu.make_async_copy(proj_ref, matrix_ref, matrix_sem.at[0])
    own_matrix.start()
    for m in range(2):
        each(pieces, lambda pc: own_wall(m, pc).start())

    tick(0)

    row_id = lax.broadcasted_iota(jnp.int32, (16, tokens), 0)
    token_id = lax.broadcasted_iota(jnp.int32, (16, tokens), 1)
    mask = jnp.zeros((16, tokens), F32)
    for p in range(prompts):
        inside = (token_id >= p * length) & (token_id < p * length + lengths_ref[p])
        mask = jnp.where(inside & (row_id == p), 1.0, mask)
    mask = mask.astype(BF16)

    def class_sums(j):
        sums = jnp.dot(mask, x_ref[j], preferred_element_type=F32)
        current = [jnp.zeros((1, block), F32), jnp.zeros((1, block), F32)]
        for p in range(prompts):
            mean = sums[p : p + 1, :] / jnp.full((1, block), lengths_ref[p].astype(F32))
            label = labels_ref[p].astype(F32)
            current[1] = current[1] + mean * label
            current[0] = current[0] + mean * (1.0 - label)
        current[0] = current[0] / jnp.full((1, block), (prompts - ones).astype(F32))
        current[1] = current[1] / jnp.full((1, block), ones.astype(F32))
        for c in range(2):
            for q in range(sub):
                current_ref[c, pl.ds(j * sub + q, 1), :] = current[c][:, q * LANES : (q + 1) * LANES]

    each(width, class_sums)

    @pl.loop(1, width)
    def _(far):
        spread(count_send, count_recv, count_sems, far).wait_recv()

    totals = count_recv[0]
    for j in range(1, width):
        totals = totals + count_recv[j]
    share = count_send[...] / totals
    share0, share1 = share[0:1, :], share[1:2, :]

    own_means.wait()
    own_gains.wait()
    current_diff = share1 * current_ref[1] - share0 * current_ref[0]
    at = jnp.minimum(chosen_ref[0], layers - 2) * (2 * tiles)
    picked = share1 * means_ref[pl.ds(at + 1, tiles, stride=2), :] - share0 * means_ref[
        pl.ds(at, tiles, stride=2), :
    ]
    pick_send[...] = jnp.where(chosen_ref[0] == layers - 1, current_diff, picked)

    @pl.loop(1, width)
    def _(far):
        spread(pick_send, pick_recv, pick_sems, far).start()

    pick_recv[me] = pick_send[...]

    @pl.loop(0, layers - 1)
    def _(l):
        e = l * (2 * tiles)
        d = share1 * means_ref[pl.ds(e + 1, tiles, stride=2), :] - share0 * means_ref[
            pl.ds(e, tiles, stride=2), :
        ]
        diff_ref[pl.ds((l // 8) * (8 * tiles) + lax.rem(l, 8), tiles, stride=8), :] = d

    diff_ref[pl.ds(((layers - 1) // 8) * (8 * tiles) + (layers - 1) % 8, tiles, stride=8), :] = (
        current_diff
    )

    def part(ref, j):
        return ref.at[pl.ds(pl.multiple_of(j * chunk, 16), chunk), :]

    def read(ref, j):
        return ref[pl.ds(pl.multiple_of(j * chunk, 16), chunk), :]

    def half(zz):
        return remote(
            part(diff_ref, 2 * zz + 1 - side), half_recv.at[zz], half_sems.at[0, zz],
            half_sems.at[1, zz], {"dp": beside},
        )

    each(lines, lambda zz: half(zz).start())
    each(lines - early, lambda zz: swap(zz + early).start())

    tick(1)
    tick(2)


    @pl.loop(1, width)
    def _(far):
        spread(pick_send, pick_recv, pick_sems, far).wait_recv()

    picked = pick_recv[0]
    for j in range(1, width):
        picked = picked + pick_recv[j]
    local_square = jnp.sum(jnp.sum(picked * picked, axis=1, keepdims=True), axis=0, keepdims=True)
    unit = picked * lax.rsqrt(local_square / half_width + 1e-06)
    flat_ref[...] = picked
    high = unit.astype(BF16).astype(F32)
    middle = (unit - high).astype(BF16).astype(F32)
    low = unit - high - middle
    line16 = lax.broadcasted_iota(jnp.int32, (16, LANES), 0)
    for k in range(tiles):
        spot = jnp.where(
            line16 == 0, high[k : k + 1, :],
            jnp.where(line16 == 1, middle[k : k + 1, :], jnp.where(line16 == 2, low[k : k + 1, :], 0.0)),
        )
        unit_ref[k // sub, :, (k % sub) * LANES : (k % sub + 1) * LANES] = spot.astype(BF16)

    stat_ref[...] = jnp.zeros_like(stat_ref)

    def token_dots(j):
        stat_ref[...] += lax.dot_general(
            x_ref[j], unit_ref[j], (((1,), (1,)), ((), ())), preferred_element_type=F32
        )

    each(width, token_dots)
    dots = jnp.sum(stat_ref[...], axis=1, keepdims=True)
    dots_send[pl.ds(0, tokens), :] = jnp.broadcast_to(dots, (tokens, LANES))
    dots_send[pl.ds(tokens, 8), :] = jnp.broadcast_to(local_square, (8, LANES))
    dots_copy = remote(dots_send, dots_recv, pair_sems.at[0, 0], pair_sems.at[1, 0], sibling)
    dots_copy.start()

    own_matrix.wait()
    col_send[...] = jnp.zeros_like(col_send)

    def column_dots(j):
        col_send[...] += jnp.dot(
            unit_ref[j], matrix_ref[pl.ds(pl.multiple_of(j * block, block), block), :],
            preferred_element_type=F32,
        )

    each(width, column_dots)
    col_copy = remote(col_send, col_recv, pair_sems.at[0, 1], pair_sems.at[1, 1], sibling)
    col_copy.start()


    tick(3)

    dots_copy.wait_recv()
    root = math.sqrt(model_width)
    other_square = dots_recv[pl.ds(tokens, 1), 0:1]
    mean_dir = (local_square + other_square) / model_width + 1e-06
    ratio_mine = jnp.sqrt((local_square / half_width + 1e-06) / mean_dir) / root
    ratio_other = jnp.sqrt((other_square / half_width + 1e-06) / mean_dir) / root
    flat = flat_ref[...] * (lax.rsqrt(mean_dir) / root)
    refusal_ref[...] = flat
    proj_tok[...] = dots_send[pl.ds(0, tokens), :] * ratio_mine + dots_recv[pl.ds(0, tokens), :] * (
        ratio_other
    )

    def square_rows(n):
        here = pl.ds(pl.multiple_of(n * 16, 16), 16)
        amount = proj_tok[here, :]
        total = jnp.zeros((16, LANES), F32)
        for j in range(width):
            for q in range(sub):
                k = j * sub + q
                left = x_ref[j, here, q * LANES : (q + 1) * LANES].astype(F32)
                left = left - amount * refusal_ref[k : k + 1, :]
                total = total + left * left
        square_send[here, :] = total

    each(tokens // 16, square_rows)
    square_copy = remote(square_send, square_recv, pair_sems.at[0, 2], pair_sems.at[1, 2], sibling)
    square_copy.start()

    def up(zz):
        return remote(
            up_send.at[zz], up_recv.at[zz], up_sems.at[0, zz], up_sems.at[1, zz],
            {"dp": lax.rem(me + 2, width)},
        )

    def down(zz):
        return remote(
            down_send.at[zz], down_recv.at[zz], down_sems.at[0, zz], down_sems.at[1, zz],
            {"dp": lax.rem(me - 2 + width, width)},
        )

    def chain_up(n):
        zz = lines - 1 - n

        @pl.when(zz > place)
        def _():
            up_send[zz] = read(diff_ref, 2 * zz + side) + half_recv[zz]

            @pl.when(place > 0)
            def _():
                up(zz).wait_recv()
                up_send[zz] += up_recv[zz]

            up(zz).start()

    def chain_down(zz):
        @pl.when(zz < place)
        def _():
            down_send[zz] = read(diff_ref, 2 * zz + side) + half_recv[zz]

            @pl.when(place < lines - 1)
            def _():
                down(zz).wait_recv()
                down_send[zz] += down_recv[zz]

            down(zz).start()

    each(lines, lambda zz: half(zz).wait_recv())

    @pl.when(place == 0)
    def _():
        each(lines, chain_up)

    @pl.when(place == lines - 1)
    def _():
        each(lines, chain_down)

    @pl.loop(4, lines + 1)
    def _(t):
        tick(t)

    col_copy.wait_recv()
    column = col_send[...] * ratio_mine + col_recv[...] * ratio_other
    column_ref[...] = jnp.broadcast_to(jnp.sum(column, axis=0, keepdims=True), column_ref.shape)

    square_copy.wait_recv()
    mean_square = jnp.sum(square_send[...] + square_recv[...], axis=1, keepdims=True) / model_width
    scale_tok[...] = jnp.broadcast_to(lax.rsqrt(mean_square + 1e-05), (tokens, LANES))

    eye = lax.broadcasted_iota(jnp.int32, (LANES, LANES), 0) == lax.broadcasted_iota(
        jnp.int32, (LANES, LANES), 1
    )
    bands = tokens // LANES
    for b in range(bands):
        here = pl.ds(b * LANES, LANES)
        for s, ref in enumerate((proj_tok, scale_tok)):
            stat_send[pl.ds(s * bands + b, 1), :] = jnp.sum(
                jnp.where(eye, ref[here, :], 0.0), axis=0, keepdims=True
            )
    stat_copy = remote(stat_send, stat_recv, stat_sems.at[0], stat_sems.at[1], {"dp": beside})
    stat_copy.start()

    def normed_rows(base, n, load, proj_at, scale_at):
        here = pl.ds(pl.multiple_of(n * 16, 16), 16)
        amount, scale = proj_at[here, :], scale_at[here, :]
        out = pl.ds(pl.multiple_of(base + n * 16, 16), 16)
        for zz in range(lines):
            j = 2 * zz + side
            vectors = refusal_ref[pl.ds(j * sub, sub), :]
            gains = gain_ref[pl.ds(j * sub, sub), :]
            for q in range(sub):
                value = load(zz, here, pl.ds(q * LANES, LANES)).astype(F32)
                value = (value - amount * vectors[q : q + 1, :]) * scale * gains[q : q + 1, :]
                normed_ref[out, pl.ds(zz * block + q * LANES, LANES)] = value.astype(BF16)

    each(
        tokens // 16,
        lambda n: normed_rows(0, n, lambda zz, a, b: x_ref[2 * zz + side, a, b], proj_tok, scale_tok),
    )

    @pl.when((place > 0) & (place < lines - 1))
    def _():
        each(lines, chain_up)
        each(lines, chain_down)

    def gathered(far):
        ref = part(final_ref, me)
        return remote(
            ref, ref, final_sems.at[0, far], final_sems.at[1, far],
            {"dp": 2 * lax.rem(place + far, lines) + side},
        )

    def gathered_from(far):
        ref = part(final_ref, 2 * lax.rem(place - far + lines, lines) + side)
        return remote(ref, ref, final_sems.at[0, far], final_sems.at[1, far], {"dp": beside})

    def shared(zz):
        ref = part(final_ref, 2 * zz + side)
        return remote(ref, ref, share_sems.at[0, zz], share_sems.at[1, zz], {"dp": beside})

    def shared_from(zz):
        ref = part(final_ref, 2 * zz + 1 - side)
        return remote(ref, ref, share_sems.at[0, zz], share_sems.at[1, zz], {"dp": beside})

    tick(lines + 1)

    stat_copy.wait_recv()
    for b in range(bands):
        here = pl.ds(b * LANES, LANES)
        for s, ref in enumerate((proj_tok, scale_tok)):
            value = jnp.where(eye, stat_recv[pl.ds(s * bands + b, 1), :], 0.0)
            ref[here, :] = jnp.broadcast_to(jnp.sum(value, axis=1, keepdims=True), (LANES, LANES))
    each(lines, lambda zz: swap(zz).wait_recv())
    each(
        tokens // 16,
        lambda n: normed_rows(tokens, n, lambda zz, a, b: swap_ref[zz, a, b], proj_tok, scale_tok),
    )

    def away(u):
        return remote(
            away_send.at[u], away_recv.at[u], away_sems.at[0, u], away_sems.at[1, u], sibling
        )

    def beyond(u):
        return remote(
            side_send.at[u], side_recv.at[u], side_sems.at[0, u], side_sems.at[1, u], {"dp": beside}
        )

    units = 2 * pairs

    def product(u):
        i, odd = u // 2, lax.rem(u, 2)
        which = lax.rem(first + odd, 2)

        @pl.when(odd == 1)
        def _():
            for way in (1, -1):

                @pl.loop(1, lines)
                def _(step):
                    @pl.when(holds(step, way))
                    def _():
                        each(2, lambda h: crossed(step, 2 * i + h, way).wait_recv())

        both = jnp.concatenate(
            [wall_ref[which, i, 1 - core], wall_ref[which, i, core]], axis=1
        )
        total = jnp.dot(normed_ref[...], both, preferred_element_type=F32)
        away_send[u] = total[:, :LANES]
        away(u).start()
        kept_ref[u] = total[:, LANES:]

    def reduce_pair(u):
        away(u).wait_recv()
        side_send[u] = (
            kept_ref[u, pl.ds(tokens, tokens), :] + away_recv[u, pl.ds(tokens, tokens), :]
        ).astype(BF16)
        beyond(u).start()

    def reduce_side(u):
        i, odd = u // 2, lax.rem(u, 2)
        which = lax.rem(first + odd, 2)
        beyond(u).wait_recv()
        total = kept_ref[u, pl.ds(0, tokens), :] + away_recv[u, pl.ds(0, tokens), :]
        total = total + side_recv[u].astype(F32)
        kv_ref[which, :, pl.ds(pl.multiple_of(i * LANES, LANES), LANES)] = total.astype(BF16)

    for m in range(2):
        each(pieces, lambda pc: own_wall(m, pc).wait())

    @pl.loop(0, pairs)
    def _(i):
        product(2 * i)

        @pl.loop(jnp.where(i < pairs - 1, lines + 2 + i, ticks), jnp.where(i < pairs - 2, lines + 3 + i, ticks))
        def _(t):
            tick(t)

        @pl.when(i == pairs - 1)
        def _():
            @pl.loop(1, lines)
            def _(far):
                gathered_from(far).wait_recv()
                shared(lax.rem(place - far + lines, lines)).start()

        reduce_pair(2 * i)
        product(2 * i + 1)
        reduce_pair(2 * i + 1)

        @pl.when(i > 0)
        def _():
            each(2, lambda odd: reduce_side(2 * i - 2 + odd))

        @pl.when(i == pairs - 3)
        def _():
            down_send[place] = read(diff_ref, me) + half_recv[place]

            @pl.when(place > 0)
            def _():
                up(place).wait_recv()
                down_send[place] += up_recv[place]

            @pl.when(place < lines - 1)
            def _():
                down(place).wait_recv()
                down_send[place] += down_recv[place]

            final_ref[pl.ds(pl.multiple_of(me * chunk, 16), chunk), :] = down_send[place].astype(BF16)

            @pl.loop(1, lines)
            def _(far):
                gathered(far).start()

            shared(place).start()


    def finish_layers():
        each(lines, lambda zz: shared_from(zz).wait_recv())

        @pl.loop(0, layers // 8)
        def _(t):
            total = jnp.zeros((8, LANES), F32)
            for k in range(0, tiles, 2):
                rows16 = pl.ds(pl.multiple_of(t * (8 * tiles) + k * 8, 16), 16)
                value = final_ref[rows16, :].astype(F32)
                total = total + value[0:8] * value[0:8] + value[8:16] * value[8:16]
            layer_send[pl.ds(pl.multiple_of(t * 8, 8), 8), :] = total

        remote(
            layer_send, layer_recv, pair_sems.at[0, 3], pair_sems.at[1, 3], sibling
        ).start()

    finish_layers()
    layer_copy = remote(layer_send, layer_recv, pair_sems.at[0, 3], pair_sems.at[1, 3], sibling)
    layer_copy.wait_recv()

    @pl.loop(0, layers // 8)
    def _(t):
        here = pl.ds(pl.multiple_of(t * 8, 8), 8)
        mean = jnp.sum(layer_send[here, :] + layer_recv[here, :], axis=1, keepdims=True) / model_width
        norm = jnp.broadcast_to(lax.rsqrt(mean + 1e-06), (8, LANES))
        norm = jnp.concatenate([norm, norm], axis=0)
        for k in range(0, tiles, 2):
            rows16 = pl.ds(pl.multiple_of(t * (8 * tiles) + k * 8, 16), 16)
            dirs_ref[rows16, :] = final_ref[rows16, :].astype(F32) * norm

    reduce_side(units - 2)
    reduce_side(units - 1)

    @pl.loop(1, width)
    def _(far):
        spread(count_send, count_recv, count_sems, far).wait_send()
        spread(pick_send, pick_recv, pick_sems, far).wait_send()

    @pl.loop(1, lines)
    def _(far):
        gathered(far).wait_send()

    def drain(zz):
        swap(zz).wait_send()
        half(zz).wait_send()
        shared(zz).wait_send()

        @pl.when(zz > place)
        def _():
            up(zz).wait_send()

        @pl.when(zz < place)
        def _():
            down(zz).wait_send()

    each(lines, drain)
    dots_copy.wait_send()
    col_copy.wait_send()
    square_copy.wait_send()
    layer_copy.wait_send()
    stat_copy.wait_send()

    def drain_unit(u):
        away(u).wait_send()
        beyond(u).wait_send()

    each(units, drain_unit)

    @pl.loop(1, lines)
    def _(step):
        def drain_piece(pc):
            for way in (1, -1):

                @pl.when(sends(step, way))
                def _():
                    hop(step, pc, way).wait_send()

                @pl.when(holds(step, way))
                def _():
                    cross(step, pc, way).wait_send()

        each(pieces, drain_piece)


def fused(lines, prompts, length, lengths, labels, chosen, rows, earlier, gain, key, value, matrix):
    tokens, half_width = rows.shape
    width = 2 * lines
    block = half_width // width
    tiles = half_width // LANES
    layers = earlier.shape[0] // (2 * tiles) + 1
    columns = key.shape[1]
    pieces = columns // LANES
    pairs = pieces // 2
    units = 2 * pairs
    flat_rows = layers * tiles
    chunk = flat_rows // width
    smem = pl.BlockSpec(memory_space=pltpu.SMEM)
    vmem = pl.BlockSpec(memory_space=pltpu.VMEM)
    hbm = pl.BlockSpec(memory_space=pltpu.HBM)
    dma = pltpu.SemaphoreType.DMA
    return pl.pallas_call(
        functools.partial(fused_kernel, (lines, pieces, prompts, length, layers)),
        out_shape=(
            jax.ShapeDtypeStruct((flat_rows, LANES), F32),
            jax.ShapeDtypeStruct((2, tokens, columns // 2), BF16),
            jax.ShapeDtypeStruct((tiles, LANES), F32),
            jax.ShapeDtypeStruct((8, matrix.shape[1]), F32),
        ),
        in_specs=[smem, smem, smem, hbm, hbm, hbm, hbm, hbm, hbm],
        out_specs=[vmem] * 4,
        scratch_shapes=[
            pltpu.VMEM((tiles, LANES), F32),
            pltpu.VMEM((width, tokens, block), BF16),
            pltpu.VMEM((lines, tokens, block), BF16),
            pltpu.VMEM((2, pairs, 2, lines * key.shape[0], LANES), BF16),
            pltpu.VMEM((2 * tokens, half_width // 2), BF16),
            pltpu.VMEM(matrix.shape, BF16),
            pltpu.VMEM(earlier.shape, F32),
            pltpu.VMEM((flat_rows, LANES), F32),
        ]
        + [pltpu.VMEM((lines, chunk, LANES), F32)] * 5
        + [
            pltpu.VMEM((flat_rows, LANES), BF16),
            pltpu.VMEM((8, LANES), F32),
            pltpu.VMEM((width, 8, LANES), F32),
            pltpu.VMEM((tiles, LANES), F32),
            pltpu.VMEM((width, tiles, LANES), F32),
            pltpu.VMEM((width, 16, block), BF16),
            pltpu.VMEM((tiles, LANES), F32),
            pltpu.VMEM((2, tiles, LANES), F32),
            pltpu.VMEM((tokens + 8, LANES), F32),
            pltpu.VMEM((tokens + 8, LANES), F32),
            pltpu.VMEM((tokens, LANES), F32),
            pltpu.VMEM((tokens, LANES), F32),
            pltpu.VMEM((tokens, 16), F32),
            pltpu.VMEM((tokens, LANES), F32),
            pltpu.VMEM((tokens, LANES), F32),
            pltpu.VMEM((8, LANES), F32),
            pltpu.VMEM((8, LANES), F32),
            pltpu.VMEM((16, matrix.shape[1]), F32),
            pltpu.VMEM((16, matrix.shape[1]), F32),
            pltpu.VMEM((layers, LANES), F32),
            pltpu.VMEM((layers, LANES), F32),
            pltpu.VMEM((units, 2 * tokens, LANES), F32),
            pltpu.VMEM((units, 2 * tokens, LANES), F32),
            pltpu.VMEM((units, 2 * tokens, LANES), F32),
            pltpu.VMEM((units, tokens, LANES), BF16),
            pltpu.VMEM((units, tokens, LANES), BF16),
            dma((width,)),
            dma((2, pieces)),
            dma((2,)),
            dma((1,)),
        ]
        + [dma((2, lines, pieces))] * 4
        + [
            dma((2, width)),
            dma((2, width)),
            dma((2, lines)),
            dma((2, lines)),
            dma((2, lines)),
            dma((2, lines)),
            dma((2, lines)),
            dma((2, lines)),
            dma((2, 4)),
            dma((2,)),
            dma((2, units)),
            dma((2, units)),
        ],
        compiler_params=pltpu.CompilerParams(
            collective_id=0, has_side_effects=True, vmem_limit_bytes=60 << 20
        ),
        cost_estimate=pl.CostEstimate(flops=10**11, bytes_accessed=30 << 20, transcendentals=0),
        name="fused",
    )(lengths, labels, chosen, rows, earlier, gain, key, value, matrix)


def update_kernel(refusal_ref, column_ref, matrix_ref, flat_ref, caches_ref, *outs):
    ortho_ref, dirs_ref, key_ref, value_ref = outs
    n = pl.program_id(0)
    bands = matrix_ref.shape[0] // LANES
    eye = lax.broadcasted_iota(jnp.int32, (LANES, LANES), 0) == lax.broadcasted_iota(
        jnp.int32, (LANES, LANES), 1
    )
    for b in range(bands):
        row = refusal_ref[pl.ds(n * bands + b, 1), :]
        along = jnp.sum(jnp.where(eye, row, 0.0), axis=1, keepdims=True)
        here = pl.ds(b * LANES, LANES)
        value = matrix_ref[here, :].astype(F32) - along * column_ref[0:1, :]
        ortho_ref[here, :] = value.astype(BF16)
    tiles = dirs_ref.shape[1] // LANES
    for t in range(dirs_ref.shape[0] // 8):
        for k in range(tiles):
            dirs_ref[t * 8 : t * 8 + 8, k * LANES : (k + 1) * LANES] = flat_ref[
                pl.ds((t * tiles + k) * 8, 8), :
            ]
    key_ref[...] = caches_ref[0]
    value_ref[...] = caches_ref[1]


def update(refusal, column, matrix, flat, caches, steps):
    half_width, columns = matrix.shape
    tiles = half_width // LANES
    layers = flat.shape[0] // tiles
    tokens, kept = caches.shape[1:]
    rows = half_width // steps
    groups = next(g for g in range(1, layers // 8 + 1) if layers // 8 % g == 0 and layers // 8 // g <= steps)
    last = layers // 8 // groups - 1
    band = next(b for b in range(16, tokens + 1, 16) if tokens % b == 0 and tokens // b <= steps)
    top = tokens // band - 1
    whole = pl.BlockSpec(memory_space=pltpu.VMEM)
    return pl.pallas_call(
        update_kernel,
        grid=(steps,),
        in_specs=[
            whole,
            whole,
            pl.BlockSpec((rows, columns), lambda n: (n, 0)),
            pl.BlockSpec((groups * 8 * tiles, LANES), lambda n: (jnp.minimum(n, last), 0)),
            pl.BlockSpec((2, band, kept), lambda n: (0, jnp.minimum(n, top), 0)),
        ],
        out_specs=[
            pl.BlockSpec((rows, columns), lambda n: (n, 0)),
            pl.BlockSpec((groups * 8, half_width), lambda n: (jnp.minimum(n, last), 0)),
            pl.BlockSpec((band, kept), lambda n: (jnp.minimum(n, top), 0)),
            pl.BlockSpec((band, kept), lambda n: (jnp.minimum(n, top), 0)),
        ],
        out_shape=[
            jax.ShapeDtypeStruct(matrix.shape, BF16),
            jax.ShapeDtypeStruct((layers, half_width), F32),
            jax.ShapeDtypeStruct((tokens, kept), BF16),
            jax.ShapeDtypeStruct((tokens, kept), BF16),
        ],
        compiler_params=pltpu.CompilerParams(vmem_limit_bytes=60 << 20),
        name="update",
    )(refusal, column, matrix, flat, caches)


def shards(
    residual, lengths, labels, earlier_means, chosen, norm_gain, key_weight, value_weight, out_proj
):
    prompts, length, half_width = residual.shape
    lines = lax.axis_size("dp") // 2
    tiles = half_width // LANES
    earlier = earlier_means[0]
    layers = earlier.shape[0] + 1
    earlier = earlier.reshape(layers - 1, 2, tiles, LANES).transpose(0, 2, 1, 3).reshape(-1, LANES)
    matrix = out_proj[0]
    flat, caches, refusal, column = fused(
        lines, prompts, length, lengths, labels, chosen, residual.reshape(-1, half_width), earlier,
        norm_gain.reshape(tiles, LANES), key_weight[0], value_weight[0], matrix,
    )
    ortho_proj, directions, keys, values = update(refusal, column, matrix, flat, caches, 2)
    keys, values = (x.reshape(prompts, length, -1) for x in (keys, values))
    return (directions, keys, values, ortho_proj[None])


def solution(mesh):
    return jax.shard_map(
        shards,
        mesh=mesh,
        in_specs=(
            P(("groups", "dp"), None, "mp"),
            P(("groups", "dp")),
            P(("groups", "dp")),
            P(("groups", "dp"), None, None, "mp"),
            P("groups"),
            P("mp"),
            P("mp", "dp", None),
            P("mp", "dp", None),
            P("groups", "mp", "dp"),
        ),
        out_specs=(
            P("groups", "mp"),
            P(("groups", "dp"), None, "mp"),
            P(("groups", "dp"), None, "mp"),
            P("groups", "mp", "dp"),
        ),
        check_vma=False,
    )
```

```python
import functools
import math

import jax
import jax.numpy as jnp
from jax import lax
from jax.experimental import pallas as pl
from jax.experimental.pallas import tpu as pltpu
from jax.sharding import PartitionSpec as P

MESH = pl.DeviceIdType.MESH
F32, BF16 = jnp.float32, jnp.bfloat16
LANES = 128


def fused_kernel(
    cfg,
    lengths_ref, labels_ref, chosen_ref, res_ref, earlier_ref, gains_ref, key_ref, value_ref, proj_ref,
    dirs_ref, kv_ref, refusal_ref, column_ref,
    gain_ref, x_ref, swap_ref, wall_ref, normed_ref, matrix_ref, means_ref, diff_ref,
    half_recv, up_send, up_recv, down_send, down_recv, final_ref,
    count_send, count_recv, pick_send, pick_recv, unit_ref, flat_ref, current_ref,
    dots_send, dots_recv, square_send, square_recv, stat_ref, proj_tok, scale_tok, stat_send, stat_recv,
    col_send, col_recv, layer_send, layer_recv,
    away_send, away_recv, kept_ref, side_send, side_recv,
    x_sem, wall_sem, means_sem, matrix_sem,
    hop_send, hop_recv, cross_send, cross_recv,
    count_sems, pick_sems, swap_sems, half_sems, up_sems, down_sems, final_sems, share_sems,
    pair_sems, stat_sems, away_sems, side_sems,
):
    lines, pieces, prompts, length, layers = cfg
    width = 2 * lines
    tokens, half_width = res_ref.shape
    block = half_width // width
    rows = key_ref.shape[0]
    sub = block // LANES
    tiles = half_width // LANES
    pairs = pieces // 2
    model_width = 2 * half_width
    chunk = diff_ref.shape[0] // width
    group, me, core = lax.axis_index("groups"), lax.axis_index("dp"), lax.axis_index("mp")
    place, side = me // 2, lax.rem(me, 2)
    beside = me + 1 - 2 * side
    first = lax.rem(group, 2)
    across = group + 1 - 2 * first
    sibling = {"mp": 1 - core}

    def remote(src, dst, send, recv, device):
        return pltpu.make_async_remote_copy(
            src_ref=src, dst_ref=dst, send_sem=send, recv_sem=recv, device_id=device,
            device_id_type=MESH,
        )

    barrier = pltpu.get_barrier_semaphore()

    @pl.loop(1, width)
    def _(far):
        pl.semaphore_signal(
            barrier, inc=1, device_id={"dp": lax.rem(me + far, width)}, device_id_type=MESH
        )

    pl.semaphore_signal(barrier, inc=1, device_id={"groups": across}, device_id_type=MESH)
    pl.semaphore_signal(barrier, inc=1, device_id=sibling, device_id_type=MESH)

    def each(count, body):
        @pl.loop(0, count)
        def _(n):
            body(n)

    def own_x(j):
        return pltpu.make_async_copy(
            res_ref.at[:, pl.ds(pl.multiple_of(j * block, block), block)], x_ref.at[j], x_sem.at[j]
        )

    each(width, lambda j: own_x(j).start())
    own_means = pltpu.make_async_copy(earlier_ref, means_ref, means_sem.at[0])
    own_means.start()
    own_gains = pltpu.make_async_copy(gains_ref, gain_ref, means_sem.at[1])
    own_gains.start()

    ones = jnp.int32(0)
    for p in range(prompts):
        ones = ones + labels_ref[p]
    line = lax.broadcasted_iota(jnp.int32, (8, LANES), 0)
    harmful = jnp.full((8, LANES), ones.astype(F32))
    harmless = jnp.full((8, LANES), (prompts - ones).astype(F32))
    count_send[...] = jnp.where(line == 0, harmless, harmful)

    pl.semaphore_wait(barrier, width + 1)

    def slot_of(step, way):
        return lax.rem(place - way * step + width * lines, lines)

    def wall_at(slot, pc):
        return wall_ref.at[
            first, pc // 2, lax.rem(pc, 2), pl.ds(pl.multiple_of(slot * rows, rows), rows), :
        ]

    def hop(step, pc, way, source=None):
        k = 0 if way > 0 else 1
        ref = wall_at(slot_of(step - 1, way), pc)
        return remote(
            ref if source is None else source, ref, hop_send.at[k, step, pc], hop_recv.at[k, step, pc],
            {"dp": lax.rem(me + 2 * way + width, width)},
        )

    def arrival(step, pc, way):
        k = 0 if way > 0 else 1
        ref = wall_at(slot_of(step, way), pc)
        return remote(
            ref, ref, hop_send.at[k, step, pc], hop_recv.at[k, step, pc],
            {"dp": lax.rem(me - 2 * way + width, width)},
        )

    def cross(step, pc, way):
        k = 0 if way > 0 else 1
        ref = wall_at(slot_of(step, way), pc)
        return remote(
            ref, ref, cross_send.at[k, step, pc], cross_recv.at[k, step, pc], {"groups": across}
        )

    def crossed(step, pc, way):
        k = 0 if way > 0 else 1
        ref = wall_ref.at[
            1 - first, pc // 2, lax.rem(pc, 2),
            pl.ds(pl.multiple_of(slot_of(step, way) * rows, rows), rows), :,
        ]
        return remote(
            ref, ref, cross_send.at[k, step, pc], cross_recv.at[k, step, pc], {"groups": across}
        )

    def sends(step, way):
        return (place >= step - 1) & (place < lines - 1) if way > 0 else (
            (place > 0) & (place <= lines - step)
        )

    def holds(step, way):
        return place >= step if way > 0 else place < lines - step

    def piece_of(ref, pc):
        column = (lax.rem(pc, 2) * pairs + pc // 2) * LANES
        return ref.at[:, pl.ds(pl.multiple_of(column, LANES), LANES)]

    def start_own(pc):
        for way in (1, -1):
            for m, ref in enumerate((key_ref, value_ref)):

                @pl.when(sends(1, way) & (first == m))
                def _():
                    hop(1, pc, way, piece_of(ref, pc)).start()

    window = 1
    ticks = pieces + lines - 2
    each(window, start_own)

    def service(step, pc):
        for way in (1, -1):

            @pl.when(holds(step, way))
            def _():
                arrival(step, pc, way).wait_recv()

                @pl.when(sends(step + 1, way) & (step < lines - 1))
                def _():
                    hop(step + 1, pc, way).start()

                cross(step, pc, way).start()

    def tick(t):
        @pl.when(t + window < pieces)
        def _():
            start_own(t + window)

        @pl.loop(jnp.maximum(1, t - pieces + 2), jnp.minimum(lines, t + 2))
        def _(step):
            service(step, t - step + 1)

    def swap(zz):
        j = 2 * zz + 1 - side
        return remote(
            res_ref.at[:, pl.ds(pl.multiple_of(j * block, block), block)], swap_ref.at[zz],
            swap_sems.at[0, zz], swap_sems.at[1, zz], {"dp": beside},
        )

    early = max(lines // 4, 1)
    each(early, lambda zz: swap(zz).start())

    def spread(send_ref, recv_ref, sems, far):
        return remote(
            send_ref, recv_ref.at[me], sems.at[0, far], sems.at[1, far],
            {"dp": lax.rem(me + far, width)},
        )

    @pl.loop(1, width)
    def _(far):
        spread(count_send, count_recv, count_sems, far).start()

    count_recv[me] = count_send[...]

    def own_wall(m, pc):
        ref = (key_ref, value_ref)[m]
        return pltpu.make_async_copy(
            piece_of(ref, pc),
            wall_ref.at[
                m, pc // 2, lax.rem(pc, 2), pl.ds(pl.multiple_of(place * rows, rows), rows), :
            ],
            wall_sem.at[m, pc],
        )

    each(width, lambda j: own_x(j).wait())
    own_matrix = pltpu.make_async_copy(proj_ref, matrix_ref, matrix_sem.at[0])
    own_matrix.start()
    for m in range(2):
        each(pieces, lambda pc: own_wall(m, pc).start())

    tick(0)

    row_id = lax.broadcasted_iota(jnp.int32, (16, tokens), 0)
    token_id = lax.broadcasted_iota(jnp.int32, (16, tokens), 1)
    mask = jnp.zeros((16, tokens), F32)
    for p in range(prompts):
        inside = (token_id >= p * length) & (token_id < p * length + lengths_ref[p])
        mask = jnp.where(inside & (row_id == p), 1.0, mask)
    mask = mask.astype(BF16)

    def class_sums(j):
        sums = jnp.dot(mask, x_ref[j], preferred_element_type=F32)
        current = [jnp.zeros((1, block), F32), jnp.zeros((1, block), F32)]
        for p in range(prompts):
            mean = sums[p : p + 1, :] / jnp.full((1, block), lengths_ref[p].astype(F32))
            label = labels_ref[p].astype(F32)
            current[1] = current[1] + mean * label
            current[0] = current[0] + mean * (1.0 - label)
        current[0] = current[0] / jnp.full((1, block), (prompts - ones).astype(F32))
        current[1] = current[1] / jnp.full((1, block), ones.astype(F32))
        for c in range(2):
            for q in range(sub):
                current_ref[c, pl.ds(j * sub + q, 1), :] = current[c][:, q * LANES : (q + 1) * LANES]

    each(width, class_sums)

    @pl.loop(1, width)
    def _(far):
        spread(count_send, count_recv, count_sems, far).wait_recv()

    totals = count_recv[0]
    for j in range(1, width):
        totals = totals + count_recv[j]
    share = count_send[...] / totals
    share0, share1 = share[0:1, :], share[1:2, :]

    own_means.wait()
    own_gains.wait()
    current_diff = share1 * current_ref[1] - share0 * current_ref[0]
    at = jnp.minimum(chosen_ref[0], layers - 2) * (2 * tiles)
    picked = share1 * means_ref[pl.ds(at + 1, tiles, stride=2), :] - share0 * means_ref[
        pl.ds(at, tiles, stride=2), :
    ]
    pick_send[...] = jnp.where(chosen_ref[0] == layers - 1, current_diff, picked)

    @pl.loop(1, width)
    def _(far):
        spread(pick_send, pick_recv, pick_sems, far).start()

    pick_recv[me] = pick_send[...]

    @pl.loop(0, layers - 1)
    def _(l):
        e = l * (2 * tiles)
        d = share1 * means_ref[pl.ds(e + 1, tiles, stride=2), :] - share0 * means_ref[
            pl.ds(e, tiles, stride=2), :
        ]
        diff_ref[pl.ds((l // 8) * (8 * tiles) + lax.rem(l, 8), tiles, stride=8), :] = d

    diff_ref[pl.ds(((layers - 1) // 8) * (8 * tiles) + (layers - 1) % 8, tiles, stride=8), :] = (
        current_diff
    )

    def part(ref, j):
        return ref.at[pl.ds(pl.multiple_of(j * chunk, 16), chunk), :]

    def read(ref, j):
        return ref[pl.ds(pl.multiple_of(j * chunk, 16), chunk), :]

    def half(zz):
        return remote(
            part(diff_ref, 2 * zz + 1 - side), half_recv.at[zz], half_sems.at[0, zz],
            half_sems.at[1, zz], {"dp": beside},
        )

    each(lines, lambda zz: half(zz).start())
    tick(1)
    tick(2)

    each(lines - early, lambda zz: swap(zz + early).start())


    @pl.loop(1, width)
    def _(far):
        spread(pick_send, pick_recv, pick_sems, far).wait_recv()

    picked = pick_recv[0]
    for j in range(1, width):
        picked = picked + pick_recv[j]
    local_square = jnp.sum(jnp.sum(picked * picked, axis=1, keepdims=True), axis=0, keepdims=True)
    unit = picked * lax.rsqrt(local_square / half_width + 1e-06)
    flat_ref[...] = picked
    high = unit.astype(BF16).astype(F32)
    middle = (unit - high).astype(BF16).astype(F32)
    low = unit - high - middle
    line16 = lax.broadcasted_iota(jnp.int32, (16, LANES), 0)
    for k in range(tiles):
        spot = jnp.where(
            line16 == 0, high[k : k + 1, :],
            jnp.where(line16 == 1, middle[k : k + 1, :], jnp.where(line16 == 2, low[k : k + 1, :], 0.0)),
        )
        unit_ref[k // sub, :, (k % sub) * LANES : (k % sub + 1) * LANES] = spot.astype(BF16)

    stat_ref[...] = jnp.zeros_like(stat_ref)

    def token_dots(j):
        stat_ref[...] += lax.dot_general(
            x_ref[j], unit_ref[j], (((1,), (1,)), ((), ())), preferred_element_type=F32
        )

    each(width, token_dots)
    dots = jnp.sum(stat_ref[...], axis=1, keepdims=True)
    dots_send[pl.ds(0, tokens), :] = jnp.broadcast_to(dots, (tokens, LANES))
    dots_send[pl.ds(tokens, 8), :] = jnp.broadcast_to(local_square, (8, LANES))
    dots_copy = remote(dots_send, dots_recv, pair_sems.at[0, 0], pair_sems.at[1, 0], sibling)
    dots_copy.start()

    own_matrix.wait()
    col_send[...] = jnp.zeros_like(col_send)

    def column_dots(j):
        col_send[...] += jnp.dot(
            unit_ref[j], matrix_ref[pl.ds(pl.multiple_of(j * block, block), block), :],
            preferred_element_type=F32,
        )

    each(width, column_dots)
    col_copy = remote(col_send, col_recv, pair_sems.at[0, 1], pair_sems.at[1, 1], sibling)
    col_copy.start()


    tick(3)

    dots_copy.wait_recv()
    root = math.sqrt(model_width)
    other_square = dots_recv[pl.ds(tokens, 1), 0:1]
    mean_dir = (local_square + other_square) / model_width + 1e-06
    ratio_mine = jnp.sqrt((local_square / half_width + 1e-06) / mean_dir) / root
    ratio_other = jnp.sqrt((other_square / half_width + 1e-06) / mean_dir) / root
    flat = flat_ref[...] * (lax.rsqrt(mean_dir) / root)
    refusal_ref[...] = flat
    proj_tok[...] = dots_send[pl.ds(0, tokens), :] * ratio_mine + dots_recv[pl.ds(0, tokens), :] * (
        ratio_other
    )

    def square_rows(n):
        here = pl.ds(pl.multiple_of(n * 16, 16), 16)
        amount = proj_tok[here, :]
        total = jnp.zeros((16, LANES), F32)
        for j in range(width):
            for q in range(sub):
                k = j * sub + q
                left = x_ref[j, here, q * LANES : (q + 1) * LANES].astype(F32)
                left = left - amount * refusal_ref[k : k + 1, :]
                total = total + left * left
        square_send[here, :] = total

    each(tokens // 16, square_rows)
    square_copy = remote(square_send, square_recv, pair_sems.at[0, 2], pair_sems.at[1, 2], sibling)
    square_copy.start()

    def up(zz):
        return remote(
            up_send.at[zz], up_recv.at[zz], up_sems.at[0, zz], up_sems.at[1, zz],
            {"dp": lax.rem(me + 2, width)},
        )

    def down(zz):
        return remote(
            down_send.at[zz], down_recv.at[zz], down_sems.at[0, zz], down_sems.at[1, zz],
            {"dp": lax.rem(me - 2 + width, width)},
        )

    def chain_up(n):
        zz = lines - 1 - n

        @pl.when(zz > place)
        def _():
            up_send[zz] = read(diff_ref, 2 * zz + side) + half_recv[zz]

            @pl.when(place > 0)
            def _():
                up(zz).wait_recv()
                up_send[zz] += up_recv[zz]

            up(zz).start()

    def chain_down(zz):
        @pl.when(zz < place)
        def _():
            down_send[zz] = read(diff_ref, 2 * zz + side) + half_recv[zz]

            @pl.when(place < lines - 1)
            def _():
                down(zz).wait_recv()
                down_send[zz] += down_recv[zz]

            down(zz).start()

    each(lines, lambda zz: half(zz).wait_recv())

    @pl.when(place == 0)
    def _():
        each(lines, chain_up)

    @pl.when(place == lines - 1)
    def _():
        each(lines, chain_down)

    @pl.loop(4, lines + 1)
    def _(t):
        tick(t)

    col_copy.wait_recv()
    column = col_send[...] * ratio_mine + col_recv[...] * ratio_other
    column_ref[...] = jnp.broadcast_to(jnp.sum(column, axis=0, keepdims=True), column_ref.shape)

    square_copy.wait_recv()
    mean_square = jnp.sum(square_send[...] + square_recv[...], axis=1, keepdims=True) / model_width
    scale_tok[...] = jnp.broadcast_to(lax.rsqrt(mean_square + 1e-05), (tokens, LANES))

    eye = lax.broadcasted_iota(jnp.int32, (LANES, LANES), 0) == lax.broadcasted_iota(
        jnp.int32, (LANES, LANES), 1
    )
    bands = tokens // LANES
    for b in range(bands):
        here = pl.ds(b * LANES, LANES)
        for s, ref in enumerate((proj_tok, scale_tok)):
            stat_send[pl.ds(s * bands + b, 1), :] = jnp.sum(
                jnp.where(eye, ref[here, :], 0.0), axis=0, keepdims=True
            )
    stat_copy = remote(stat_send, stat_recv, stat_sems.at[0], stat_sems.at[1], {"dp": beside})
    stat_copy.start()

    def normed_rows(base, n, load, proj_at, scale_at):
        here = pl.ds(pl.multiple_of(n * 16, 16), 16)
        amount, scale = proj_at[here, :], scale_at[here, :]
        out = pl.ds(pl.multiple_of(base + n * 16, 16), 16)
        for zz in range(lines):
            j = 2 * zz + side
            vectors = refusal_ref[pl.ds(j * sub, sub), :]
            gains = gain_ref[pl.ds(j * sub, sub), :]
            for q in range(sub):
                value = load(zz, here, pl.ds(q * LANES, LANES)).astype(F32)
                value = (value - amount * vectors[q : q + 1, :]) * scale * gains[q : q + 1, :]
                normed_ref[out, pl.ds(zz * block + q * LANES, LANES)] = value.astype(BF16)

    each(
        tokens // 16,
        lambda n: normed_rows(0, n, lambda zz, a, b: x_ref[2 * zz + side, a, b], proj_tok, scale_tok),
    )

    @pl.when((place > 0) & (place < lines - 1))
    def _():
        each(lines, chain_up)
        each(lines, chain_down)

    def gathered(far):
        ref = part(final_ref, me)
        return remote(
            ref, ref, final_sems.at[0, far], final_sems.at[1, far],
            {"dp": 2 * lax.rem(place + far, lines) + side},
        )

    def gathered_from(far):
        ref = part(final_ref, 2 * lax.rem(place - far + lines, lines) + side)
        return remote(ref, ref, final_sems.at[0, far], final_sems.at[1, far], {"dp": beside})

    def shared(zz):
        ref = part(final_ref, 2 * zz + side)
        return remote(ref, ref, share_sems.at[0, zz], share_sems.at[1, zz], {"dp": beside})

    def shared_from(zz):
        ref = part(final_ref, 2 * zz + 1 - side)
        return remote(ref, ref, share_sems.at[0, zz], share_sems.at[1, zz], {"dp": beside})

    tick(lines + 1)

    stat_copy.wait_recv()
    for b in range(bands):
        here = pl.ds(b * LANES, LANES)
        for s, ref in enumerate((proj_tok, scale_tok)):
            value = jnp.where(eye, stat_recv[pl.ds(s * bands + b, 1), :], 0.0)
            ref[here, :] = jnp.broadcast_to(jnp.sum(value, axis=1, keepdims=True), (LANES, LANES))
    each(lines, lambda zz: swap(zz).wait_recv())
    each(
        tokens // 16,
        lambda n: normed_rows(tokens, n, lambda zz, a, b: swap_ref[zz, a, b], proj_tok, scale_tok),
    )

    def away(u):
        return remote(
            away_send.at[u], away_recv.at[u], away_sems.at[0, u], away_sems.at[1, u], sibling
        )

    def beyond(u):
        return remote(
            side_send.at[u], side_recv.at[u], side_sems.at[0, u], side_sems.at[1, u], {"dp": beside}
        )

    units = 2 * pairs

    def product(u):
        i, odd = u // 2, lax.rem(u, 2)
        which = lax.rem(first + odd, 2)

        @pl.when(odd == 1)
        def _():
            for way in (1, -1):

                @pl.loop(1, lines)
                def _(step):
                    @pl.when(holds(step, way))
                    def _():
                        each(2, lambda h: crossed(step, 2 * i + h, way).wait_recv())

        both = jnp.concatenate(
            [wall_ref[which, i, 1 - core], wall_ref[which, i, core]], axis=1
        )
        total = jnp.dot(normed_ref[...], both, preferred_element_type=F32)
        away_send[u] = total[:, :LANES]
        away(u).start()
        kept_ref[u] = total[:, LANES:]

    def reduce_pair(u):
        away(u).wait_recv()
        side_send[u] = (
            kept_ref[u, pl.ds(tokens, tokens), :] + away_recv[u, pl.ds(tokens, tokens), :]
        ).astype(BF16)
        beyond(u).start()

    def reduce_side(u):
        i, odd = u // 2, lax.rem(u, 2)
        which = lax.rem(first + odd, 2)
        beyond(u).wait_recv()
        total = kept_ref[u, pl.ds(0, tokens), :] + away_recv[u, pl.ds(0, tokens), :]
        total = total + side_recv[u].astype(F32)
        kv_ref[which, :, pl.ds(pl.multiple_of(i * LANES, LANES), LANES)] = total.astype(BF16)

    for m in range(2):
        each(pieces, lambda pc: own_wall(m, pc).wait())

    @pl.loop(0, pairs)
    def _(i):
        product(2 * i)

        @pl.loop(jnp.where(i < pairs - 1, lines + 2 + i, ticks), jnp.where(i < pairs - 2, lines + 3 + i, ticks))
        def _(t):
            tick(t)

        @pl.when(i == pairs - 1)
        def _():
            @pl.loop(1, lines)
            def _(far):
                gathered_from(far).wait_recv()
                shared(lax.rem(place - far + lines, lines)).start()

        reduce_pair(2 * i)
        product(2 * i + 1)
        reduce_pair(2 * i + 1)

        @pl.when(i > 0)
        def _():
            each(2, lambda odd: reduce_side(2 * i - 2 + odd))

        @pl.when(i == pairs - 3)
        def _():
            down_send[place] = read(diff_ref, me) + half_recv[place]

            @pl.when(place > 0)
            def _():
                up(place).wait_recv()
                down_send[place] += up_recv[place]

            @pl.when(place < lines - 1)
            def _():
                down(place).wait_recv()
                down_send[place] += down_recv[place]

            final_ref[pl.ds(pl.multiple_of(me * chunk, 16), chunk), :] = down_send[place].astype(BF16)

            @pl.loop(1, lines)
            def _(far):
                gathered(far).start()

            shared(place).start()


    def finish_layers():
        each(lines, lambda zz: shared_from(zz).wait_recv())

        @pl.loop(0, layers // 8)
        def _(t):
            total = jnp.zeros((8, LANES), F32)
            for k in range(0, tiles, 2):
                rows16 = pl.ds(pl.multiple_of(t * (8 * tiles) + k * 8, 16), 16)
                value = final_ref[rows16, :].astype(F32)
                total = total + value[0:8] * value[0:8] + value[8:16] * value[8:16]
            layer_send[pl.ds(pl.multiple_of(t * 8, 8), 8), :] = total

        remote(
            layer_send, layer_recv, pair_sems.at[0, 3], pair_sems.at[1, 3], sibling
        ).start()

    finish_layers()
    layer_copy = remote(layer_send, layer_recv, pair_sems.at[0, 3], pair_sems.at[1, 3], sibling)
    layer_copy.wait_recv()

    @pl.loop(0, layers // 8)
    def _(t):
        here = pl.ds(pl.multiple_of(t * 8, 8), 8)
        mean = jnp.sum(layer_send[here, :] + layer_recv[here, :], axis=1, keepdims=True) / model_width
        norm = jnp.broadcast_to(lax.rsqrt(mean + 1e-06), (8, LANES))
        norm = jnp.concatenate([norm, norm], axis=0)
        for k in range(0, tiles, 2):
            rows16 = pl.ds(pl.multiple_of(t * (8 * tiles) + k * 8, 16), 16)
            dirs_ref[rows16, :] = final_ref[rows16, :].astype(F32) * norm

    reduce_side(units - 2)
    reduce_side(units - 1)

    @pl.loop(1, width)
    def _(far):
        spread(count_send, count_recv, count_sems, far).wait_send()
        spread(pick_send, pick_recv, pick_sems, far).wait_send()

    @pl.loop(1, lines)
    def _(far):
        gathered(far).wait_send()

    def drain(zz):
        swap(zz).wait_send()
        half(zz).wait_send()
        shared(zz).wait_send()

        @pl.when(zz > place)
        def _():
            up(zz).wait_send()

        @pl.when(zz < place)
        def _():
            down(zz).wait_send()

    each(lines, drain)
    dots_copy.wait_send()
    col_copy.wait_send()
    square_copy.wait_send()
    layer_copy.wait_send()
    stat_copy.wait_send()

    def drain_unit(u):
        away(u).wait_send()
        beyond(u).wait_send()

    each(units, drain_unit)

    @pl.loop(1, lines)
    def _(step):
        def drain_piece(pc):
            for way in (1, -1):

                @pl.when(sends(step, way))
                def _():
                    hop(step, pc, way).wait_send()

                @pl.when(holds(step, way))
                def _():
                    cross(step, pc, way).wait_send()

        each(pieces, drain_piece)


def fused(lines, prompts, length, lengths, labels, chosen, rows, earlier, gain, key, value, matrix):
    tokens, half_width = rows.shape
    width = 2 * lines
    block = half_width // width
    tiles = half_width // LANES
    layers = earlier.shape[0] // (2 * tiles) + 1
    columns = key.shape[1]
    pieces = columns // LANES
    pairs = pieces // 2
    units = 2 * pairs
    flat_rows = layers * tiles
    chunk = flat_rows // width
    smem = pl.BlockSpec(memory_space=pltpu.SMEM)
    vmem = pl.BlockSpec(memory_space=pltpu.VMEM)
    hbm = pl.BlockSpec(memory_space=pltpu.HBM)
    dma = pltpu.SemaphoreType.DMA
    return pl.pallas_call(
        functools.partial(fused_kernel, (lines, pieces, prompts, length, layers)),
        out_shape=(
            jax.ShapeDtypeStruct((flat_rows, LANES), F32),
            jax.ShapeDtypeStruct((2, tokens, columns // 2), BF16),
            jax.ShapeDtypeStruct((tiles, LANES), F32),
            jax.ShapeDtypeStruct((8, matrix.shape[1]), F32),
        ),
        in_specs=[smem, smem, smem, hbm, hbm, hbm, hbm, hbm, hbm],
        out_specs=[vmem] * 4,
        scratch_shapes=[
            pltpu.VMEM((tiles, LANES), F32),
            pltpu.VMEM((width, tokens, block), BF16),
            pltpu.VMEM((lines, tokens, block), BF16),
            pltpu.VMEM((2, pairs, 2, lines * key.shape[0], LANES), BF16),
            pltpu.VMEM((2 * tokens, half_width // 2), BF16),
            pltpu.VMEM(matrix.shape, BF16),
            pltpu.VMEM(earlier.shape, F32),
            pltpu.VMEM((flat_rows, LANES), F32),
        ]
        + [pltpu.VMEM((lines, chunk, LANES), F32)] * 5
        + [
            pltpu.VMEM((flat_rows, LANES), BF16),
            pltpu.VMEM((8, LANES), F32),
            pltpu.VMEM((width, 8, LANES), F32),
            pltpu.VMEM((tiles, LANES), F32),
            pltpu.VMEM((width, tiles, LANES), F32),
            pltpu.VMEM((width, 16, block), BF16),
            pltpu.VMEM((tiles, LANES), F32),
            pltpu.VMEM((2, tiles, LANES), F32),
            pltpu.VMEM((tokens + 8, LANES), F32),
            pltpu.VMEM((tokens + 8, LANES), F32),
            pltpu.VMEM((tokens, LANES), F32),
            pltpu.VMEM((tokens, LANES), F32),
            pltpu.VMEM((tokens, 16), F32),
            pltpu.VMEM((tokens, LANES), F32),
            pltpu.VMEM((tokens, LANES), F32),
            pltpu.VMEM((8, LANES), F32),
            pltpu.VMEM((8, LANES), F32),
            pltpu.VMEM((16, matrix.shape[1]), F32),
            pltpu.VMEM((16, matrix.shape[1]), F32),
            pltpu.VMEM((layers, LANES), F32),
            pltpu.VMEM((layers, LANES), F32),
            pltpu.VMEM((units, 2 * tokens, LANES), F32),
            pltpu.VMEM((units, 2 * tokens, LANES), F32),
            pltpu.VMEM((units, 2 * tokens, LANES), F32),
            pltpu.VMEM((units, tokens, LANES), BF16),
            pltpu.VMEM((units, tokens, LANES), BF16),
            dma((width,)),
            dma((2, pieces)),
            dma((2,)),
            dma((1,)),
        ]
        + [dma((2, lines, pieces))] * 4
        + [
            dma((2, width)),
            dma((2, width)),
            dma((2, lines)),
            dma((2, lines)),
            dma((2, lines)),
            dma((2, lines)),
            dma((2, lines)),
            dma((2, lines)),
            dma((2, 4)),
            dma((2,)),
            dma((2, units)),
            dma((2, units)),
        ],
        compiler_params=pltpu.CompilerParams(
            collective_id=0, has_side_effects=True, vmem_limit_bytes=60 << 20
        ),
        cost_estimate=pl.CostEstimate(flops=10**11, bytes_accessed=30 << 20, transcendentals=0),
        name="fused",
    )(lengths, labels, chosen, rows, earlier, gain, key, value, matrix)


def update_kernel(refusal_ref, column_ref, matrix_ref, flat_ref, caches_ref, *outs):
    ortho_ref, dirs_ref, key_ref, value_ref = outs
    n = pl.program_id(0)
    bands = matrix_ref.shape[0] // LANES
    eye = lax.broadcasted_iota(jnp.int32, (LANES, LANES), 0) == lax.broadcasted_iota(
        jnp.int32, (LANES, LANES), 1
    )
    for b in range(bands):
        row = refusal_ref[pl.ds(n * bands + b, 1), :]
        along = jnp.sum(jnp.where(eye, row, 0.0), axis=1, keepdims=True)
        here = pl.ds(b * LANES, LANES)
        value = matrix_ref[here, :].astype(F32) - along * column_ref[0:1, :]
        ortho_ref[here, :] = value.astype(BF16)
    tiles = dirs_ref.shape[1] // LANES
    for t in range(dirs_ref.shape[0] // 8):
        for k in range(tiles):
            dirs_ref[t * 8 : t * 8 + 8, k * LANES : (k + 1) * LANES] = flat_ref[
                pl.ds((t * tiles + k) * 8, 8), :
            ]
    key_ref[...] = caches_ref[0]
    value_ref[...] = caches_ref[1]


def update(refusal, column, matrix, flat, caches, steps):
    half_width, columns = matrix.shape
    tiles = half_width // LANES
    layers = flat.shape[0] // tiles
    tokens, kept = caches.shape[1:]
    rows = half_width // steps
    groups = next(g for g in range(1, layers // 8 + 1) if layers // 8 % g == 0 and layers // 8 // g <= steps)
    last = layers // 8 // groups - 1
    band = next(b for b in range(16, tokens + 1, 16) if tokens % b == 0 and tokens // b <= steps)
    top = tokens // band - 1
    whole = pl.BlockSpec(memory_space=pltpu.VMEM)
    return pl.pallas_call(
        update_kernel,
        grid=(steps,),
        in_specs=[
            whole,
            whole,
            pl.BlockSpec((rows, columns), lambda n: (n, 0)),
            pl.BlockSpec((groups * 8 * tiles, LANES), lambda n: (jnp.minimum(n, last), 0)),
            pl.BlockSpec((2, band, kept), lambda n: (0, jnp.minimum(n, top), 0)),
        ],
        out_specs=[
            pl.BlockSpec((rows, columns), lambda n: (n, 0)),
            pl.BlockSpec((groups * 8, half_width), lambda n: (jnp.minimum(n, last), 0)),
            pl.BlockSpec((band, kept), lambda n: (jnp.minimum(n, top), 0)),
            pl.BlockSpec((band, kept), lambda n: (jnp.minimum(n, top), 0)),
        ],
        out_shape=[
            jax.ShapeDtypeStruct(matrix.shape, BF16),
            jax.ShapeDtypeStruct((layers, half_width), F32),
            jax.ShapeDtypeStruct((tokens, kept), BF16),
            jax.ShapeDtypeStruct((tokens, kept), BF16),
        ],
        compiler_params=pltpu.CompilerParams(vmem_limit_bytes=60 << 20),
        name="update",
    )(refusal, column, matrix, flat, caches)


def shards(
    residual, lengths, labels, earlier_means, chosen, norm_gain, key_weight, value_weight, out_proj
):
    prompts, length, half_width = residual.shape
    lines = lax.axis_size("dp") // 2
    tiles = half_width // LANES
    earlier = earlier_means[0]
    layers = earlier.shape[0] + 1
    earlier = earlier.reshape(layers - 1, 2, tiles, LANES).transpose(0, 2, 1, 3).reshape(-1, LANES)
    matrix = out_proj[0]
    flat, caches, refusal, column = fused(
        lines, prompts, length, lengths, labels, chosen, residual.reshape(-1, half_width), earlier,
        norm_gain.reshape(tiles, LANES), key_weight[0], value_weight[0], matrix,
    )
    ortho_proj, directions, keys, values = update(refusal, column, matrix, flat, caches, 2)
    keys, values = (x.reshape(prompts, length, -1) for x in (keys, values))
    return (directions, keys, values, ortho_proj[None])


def solution(mesh):
    return jax.shard_map(
        shards,
        mesh=mesh,
        in_specs=(
            P(("groups", "dp"), None, "mp"),
            P(("groups", "dp")),
            P(("groups", "dp")),
            P(("groups", "dp"), None, None, "mp"),
            P("groups"),
            P("mp"),
            P("mp", "dp", None),
            P("mp", "dp", None),
            P("groups", "mp", "dp"),
        ),
        out_specs=(
            P("groups", "mp"),
            P(("groups", "dp"), None, "mp"),
            P(("groups", "dp"), None, "mp"),
            P("groups", "mp", "dp"),
        ),
        check_vma=False,
    )
```
